128 devices in a mesh: fsdp: 64 (over z, x_hi, y, core), seq: 2 (over x_lo).
Axes of the slice: x: 4 (x_hi: 2, x_lo: 2; x = x_hi * 2 + x_lo), y: 4, z: 4, core: 2. Of those that a mesh axis runs over, the one named last changes fastest.
Arguments:
- tokens_in: bfloat16 [64, 256, 1024], P('fsdp', 'seq'), may hold values from -16 to 16
- noise_emb: bfloat16 [64, 1024], P('fsdp'), may hold values from -6 to 6
- text_emb: bfloat16 [64, 8, 768], P('fsdp'), may hold values from -16 to 16
- prompt_len: int32 [64], P('fsdp'), may hold values from 1 to 8, as said below
- mod_weight: bfloat16 [1024, 2048], P('fsdp'), may hold values from -0.09375 to 0.09375
- qkv_weight: bfloat16 [1024, 3, 1024], P('fsdp'), may hold values from -0.1875 to 0.1875
- proj_weight: bfloat16 [1024, 1024], P('fsdp'), may hold values from -1.5 to 1.5
- cq_weight: bfloat16 [1024, 1024], P('fsdp'), may hold values from -0.1875 to 0.1875
- text_weight: bfloat16 [768, 2, 1024], P('fsdp', None, 'seq'), may hold values from -0.21875 to 0.21875
- co_weight: bfloat16 [1024, 1024], P('fsdp'), may hold values from -0.375 to 0.375
- norm_gains: bfloat16 [2, 1024], P(None, 'fsdp'), may hold values from 0.099609375 to 1.8984375
- up_weight: bfloat16 [1024, 4096], P('fsdp'), may hold values from -0.1875 to 0.1875
- down_weight: bfloat16 [4096, 1024], P('fsdp'), may hold values from -0.09375 to 0.09375
- out_grad: bfloat16 [64, 256, 1024], P('fsdp', 'seq'), may hold values from -6 to 6
Outputs:
- block_out: bfloat16 [64, 256, 1024], P('fsdp', 'seq')
- tokens_grad: float32 [64, 256, 1024], P('fsdp', 'seq')
- noise_grad: float32 [64, 1024], P('fsdp')
- text_grad: float32 [64, 8, 768], P('fsdp')
- mod_wgrad: float32 [1024, 2048], P('fsdp')
- qkv_wgrad: float32 [1024, 3, 1024], P('fsdp')
- proj_wgrad: float32 [1024, 1024], P('fsdp')
- cq_wgrad: float32 [1024, 1024], P('fsdp')
- text_wgrad: float32 [768, 2, 1024], P('fsdp', None, 'seq')
- co_wgrad: float32 [1024, 1024], P('fsdp')
- gains_grad: float32 [2, 1024], P(None, 'fsdp')
- up_wgrad: float32 [1024, 4096], P('fsdp')
- down_wgrad: float32 [4096, 1024], P('fsdp')
The draws below stay inside these ranges and needn't reach their ends.
Inputs may be any that keep to these rules, and one draw needn't show every extreme that they name: Image i uses its first prompt_len[i] text positions as keys; in every draw some image uses all 8.
All inputs are finite; a program needn't handle non-finite values.
Results may differ from the reference program's by a relative error of at most 0.018.
Values may be sent and summed in bfloat16 or wider, within the bound.
No kernel may reach another device: no remote copies, remote signals or barrier semaphores. Data moves between devices by JAX's collectives and lax.ppermute only.
A program may use at most 192 MiB of HBM per device.

```python
from functools import partial
import jax
import jax.numpy as jnp
from jax import lax

D = 1024
HEAD_DIM = 64
FF = 4096
TEXT_W = 768
NOISE_W = 1024
TXT_LEN = 8
TOK_IMG = 256
IMAGES = 64


def draw_prompt_len(key, part):
    key_len = jax.random.fold_in(key, 11)
    key_full = jax.random.fold_in(key, 23)
    drawn = jax.random.randint(key_len, (IMAGES,), 1, TXT_LEN + 1)
    full_at = jax.random.randint(key_full, (), 0, IMAGES)
    return jnp.where(jnp.arange(IMAGES) == full_at, TXT_LEN, drawn).astype(jnp.int32)


def raised(values, rng, source, target, shards_of, factor):
    def block_of(dim):
        return (jnp.arange(values.shape[dim]) // (values.shape[dim] // shards_of)).reshape((-1,) + (1,) * (values.ndim - 1 - dim))

    near = jax.random.permutation(rng, shards_of)[block_of(target)]
    second = (block_of(target) + shards_of // 2) % shards_of
    return jnp.where((block_of(source) == near) | (block_of(source) == second), factor * values, values)


def level_of(key, extent, pieces, smallest, high):
    def one(position, shards_of):
        heights = jax.random.uniform(jax.random.fold_in(jax.random.fold_in(key, 6), position), (shards_of,), jnp.float32, smallest / len(pieces), high / len(pieces))
        return jnp.repeat(jnp.exp(heights), extent[position] // shards_of).reshape((-1,) + (1,) * (len(extent) - position - 1))

    gain = one(*pieces[0])
    for cut in pieces[1:]:
        gain = gain * one(*cut)
    return gain


def scatter_about(rng, extent, scale, most, shards=(), held_as=jnp.bfloat16):
    values = scale * jax.random.normal(rng, extent, jnp.float32)
    if shards:
        values = values * level_of(rng, extent, shards, -0.22, 0.18)
    return jnp.clip(values, -most, most).astype(held_as)


def bell_draw_with(own_key, extent, width, most, pieces, heavy, kind=jnp.bfloat16):
    values = width * jax.random.normal(own_key, extent, jnp.float32)
    if pieces:
        values = values * level_of(own_key, extent, pieces, -0.22, 0.18)
    return jnp.clip(raised(values, jax.random.fold_in(own_key, 3), *heavy), -most, most).astype(kind)


def setup_inputs(seed: int = 0) -> dict:
    splits = jax.random.split(jax.random.key(seed), 15)
    tokens_in = bell_draw_with(splits[0], (IMAGES, TOK_IMG, D), 1.0, 16.0, ((0, 64), (1, 2)), (0, 2, 64, 4.0))
    noise_emb = scatter_about(splits[1], (IMAGES, NOISE_W), 1.0, 6.0, ((0, 64),))
    text_emb = bell_draw_with(splits[2], (IMAGES, TXT_LEN, TEXT_W), 1.0, 16.0, ((0, 64),), (0, 2, 64, 4.0))
    prompt_len = draw_prompt_len(jax.random.fold_in(splits[14], 71), 0)
    mod_weight = scatter_about(splits[4], (NOISE_W, 2 * D), (4 * NOISE_W) ** -0.5, 0.09375, ((0, 64),))
    qkv_weight = scatter_about(splits[5], (D, 3, D), D ** -0.5, 0.1875, ((0, 64),))
    proj_weight = scatter_about(splits[6], (D, D), (4 * D // TOK_IMG) ** -0.5, 1.5, ((0, 64),))
    cq_weight = scatter_about(splits[7], (D, D), D ** -0.5, 0.1875, ((0, 64),))
    text_weight = scatter_about(splits[8], (TEXT_W, 2, D), TEXT_W ** -0.5, 0.21875, ((0, 64), (2, 2)))
    co_weight = scatter_about(splits[9], (D, D), (2 * D // TXT_LEN) ** -0.5, 0.375, ((0, 64),))
    norm_gains = jnp.clip(1.0 + 0.18 * jax.random.normal(splits[10], (2, D), jnp.float32), 0.099609375, 1.8984375).astype(jnp.bfloat16)
    up_weight = scatter_about(splits[11], (D, FF), D ** -0.5, 0.1875, ((0, 64),))
    down_weight = scatter_about(splits[12], (FF, D), FF ** -0.5, 0.09375, ((0, 64),))
    out_grad = scatter_about(splits[13], (IMAGES, TOK_IMG, D), 1.0, 6.0, ((0, 64), (1, 2)))
    return {"tokens_in": tokens_in, "noise_emb": noise_emb, "text_emb": text_emb, "prompt_len": prompt_len, "mod_weight": mod_weight, "qkv_weight": qkv_weight, "proj_weight": proj_weight, "cq_weight": cq_weight, "text_weight": text_weight, "co_weight": co_weight, "norm_gains": norm_gains, "up_weight": up_weight, "down_weight": down_weight, "out_grad": out_grad}


EPSILON = 1e-06
HIGHEST_PREC = lax.Precision.HIGHEST
NEG_LARGE = -1e+30

@jax.custom_vjp
def low(v):
    return lax.optimization_barrier(v.astype(jnp.bfloat16)).astype(jnp.float32)

@jax.custom_vjp
def low_back(v):
    return v

def low_keep(v):
    return (low(v), None)

def low_pass(kept, grad):
    return (grad,)

def back_keep(v):
    return (v, None)

def back_low(kept, grad):
    return (low(grad),)
low.defvjp(low_keep, low_pass)
low_back.defvjp(back_keep, back_low)

def both_ways(tensor):
    return low(low_back(tensor))

def rms_norm(tensor):
    return tensor * lax.rsqrt(lax.optimization_barrier(jnp.mean(tensor * tensor, axis=-1, keepdims=True)) + EPSILON)

def matmul(left, right):
    return jnp.dot(left, right, precision=HIGHEST_PREC)

def split_heads(tensor):
    return tensor.reshape(tensor.shape[:-1] + (tensor.shape[-1] // HEAD_DIM, HEAD_DIM))

def one_image(weights, packed):
    mod_weight, qkv_weight, proj_weight, cq_weight, text_weight, co_weight, norm_gains, up_weight, down_weight = weights
    tokens, noise_row, text_rows, length = packed
    factor = HEAD_DIM ** (-0.5)
    modulation = matmul(noise_row[None, :], mod_weight)[0]
    mod_scale = modulation[:D]
    mod_shift = modulation[D:]
    normed_one = low(rms_norm(tokens) * (1.0 + mod_scale) + mod_shift)
    qkv_all = both_ways(jnp.einsum('td,dcn->tcn', normed_one, qkv_weight, precision=HIGHEST_PREC))
    queries = split_heads(qkv_all[:, 0])
    keys_all = split_heads(qkv_all[:, 1])
    values_all = split_heads(qkv_all[:, 2])
    self_scores = low_back(jnp.einsum('qhd,khd->hqk', queries, keys_all, precision=HIGHEST_PREC) * factor)
    self_probs = low(jax.nn.softmax(self_scores, axis=-1))
    attended = both_ways(jnp.einsum('hqk,khd->qhd', self_probs, values_all, precision=HIGHEST_PREC).reshape(TOK_IMG, D))
    after_self = tokens + low_back(matmul(attended, proj_weight))
    normed_two = low(rms_norm(after_self) * norm_gains[0])
    cross_q = split_heads(both_ways(matmul(normed_two, cq_weight)))
    text_kv = both_ways(jnp.einsum('jt,tcn->jcn', text_rows, text_weight, precision=HIGHEST_PREC))
    text_keys = split_heads(text_kv[:, 0])
    text_vals = split_heads(text_kv[:, 1])
    cross_scores = low_back(jnp.einsum('qhd,khd->hqk', cross_q, text_keys, precision=HIGHEST_PREC) * factor)
    usable = jnp.arange(TXT_LEN, dtype=jnp.int32) < length
    cross_scores = jnp.where(usable[None, None, :], cross_scores, NEG_LARGE)
    cross_probs = low(jax.nn.softmax(cross_scores, axis=-1))
    cross_att = both_ways(jnp.einsum('hqk,khd->qhd', cross_probs, text_vals, precision=HIGHEST_PREC).reshape(TOK_IMG, D))
    after_cross = after_self + low_back(matmul(cross_att, co_weight))
    normed_three = low(rms_norm(after_cross) * norm_gains[1])
    pre_act = low_back(matmul(normed_three, up_weight))
    activated = low(jax.nn.gelu(pre_act, approximate=True))
    return after_cross + matmul(activated, down_weight)

def reference(tokens_in, noise_emb, text_emb, prompt_len, mod_weight, qkv_weight, proj_weight, cq_weight, text_weight, co_weight, norm_gains, up_weight, down_weight, out_grad):
    weight_list = tuple((item.astype(jnp.float32) for item in (mod_weight, qkv_weight, proj_weight, cq_weight, text_weight, co_weight, norm_gains, up_weight, down_weight)))

    def forward(tokens, noise_rows, text_all, *weights):
        image_fn = jax.checkpoint(partial(one_image, weights))
        return lax.map(image_fn, (tokens, noise_rows, text_all, prompt_len))
    result, pullback = jax.vjp(forward, tokens_in.astype(jnp.float32), noise_emb.astype(jnp.float32), text_emb.astype(jnp.float32), *weight_list)
    grads = pullback(out_grad.astype(jnp.float32))
    block_out = result.astype(jnp.bfloat16)
    return (block_out, grads[0], grads[1], grads[2], grads[3], grads[4], grads[5], grads[6], grads[7], grads[8], grads[9], grads[10], grads[11])
```

```python
from functools import partial

import jax
import jax.numpy as jnp
from jax import lax
from jax.sharding import Mesh
from jax.sharding import PartitionSpec as P

HEAD_DIM = 64
EPSILON = 1e-06
HIGHEST_PREC = lax.Precision.HIGHEST
NEG_LARGE = -1e30
BF = jnp.bfloat16
F32 = jnp.float32

AXES = ("z", "xh", "y", "core", "xl")
SIZES = (4, 2, 4, 2, 2)
FSDP = ("z", "xh", "y", "core")
RING_X = ("xh", "xl")

D = 1024
FF = 4096
TEXT_W = 768
TXT = 8
CHIPS = 32

C_MOD, C_QKV, C_CQ, C_TEXT, C_PROJ, C_CO = 1024, 1536, 512, 512, 512, 512
TEXT_COLS = (C_MOD + C_QKV + C_CQ, C_MOD + C_QKV + C_CQ + C_TEXT)
C_UP, C_DOWN = 2048, 2048


def rms_norm(tensor):
    return tensor * lax.rsqrt(jnp.mean(tensor * tensor, axis=-1, keepdims=True) + EPSILON)


def gained_norm(tensor, gain_vec):
    return rms_norm(tensor) * gain_vec


def modulated_norm(tensor, scale, shift):
    return rms_norm(tensor) * (1.0 + scale[:, None, :]) + shift[:, None, :]


def split_heads(tensor):
    return tensor.reshape(tensor.shape[:-1] + (tensor.shape[-1] // HEAD_DIM, HEAD_DIM))


def score_block(queries, keys_all, usable):
    scores = jnp.einsum(
        "iqhd,ikhd->ihqk", queries, keys_all, preferred_element_type=F32
    ) * HEAD_DIM ** (-0.5)
    if usable is None:
        return scores
    return jnp.where(usable[:, None, None, :], scores, NEG_LARGE)


def attend_forward(queries, keys_all, values_all, usable):
    scores = score_block(queries, keys_all, usable)
    row_max = jnp.max(scores, axis=-1, keepdims=True)
    log_total = row_max + jnp.log(jnp.sum(jnp.exp(scores - row_max), axis=-1, keepdims=True))
    softmax_w = jnp.exp(scores - log_total).astype(BF)
    mixed = jnp.einsum("ihqk,ikhd->iqhd", softmax_w, values_all, preferred_element_type=F32)
    return mixed, log_total


def attend_backward(queries, keys_all, values_all, usable, log_total, mixed_grad):
    factor = HEAD_DIM ** (-0.5)
    scores = score_block(queries, keys_all, usable)
    softmax_w = jnp.exp(scores - log_total)
    softmax_low = softmax_w.astype(BF)
    prob_grad = jnp.einsum("iqhd,ikhd->ihqk", mixed_grad, values_all, preferred_element_type=F32)
    inner = jnp.sum(softmax_w * prob_grad, axis=-1, keepdims=True)
    score_grad = (softmax_w * (prob_grad - inner)).astype(BF)
    query_grad = factor * jnp.einsum(
        "ihqk,ikhd->iqhd", score_grad, keys_all, preferred_element_type=F32
    )
    key_grad = factor * jnp.einsum(
        "ihqk,iqhd->ikhd", score_grad, queries, preferred_element_type=F32
    )
    value_grad = jnp.einsum("ihqk,iqhd->ikhd", softmax_low, mixed_grad, preferred_element_type=F32)
    return query_grad, key_grad, value_grad


def matmul(left, right):
    return jnp.einsum("itd,de->ite", left, right, preferred_element_type=F32)


def matmul_back(left, right):
    return jnp.einsum("ite,de->itd", left, right, preferred_element_type=F32)


def outer_sum(left, right):
    return jnp.einsum("itd,ite->de", left, right, preferred_element_type=F32)


def swap_core(value):
    return lax.ppermute(value, "core", [(0, 1), (1, 0)])


def swap_seq(value):
    return lax.ppermute(value, "xl", [(0, 1), (1, 0)])


def swap_x(value, pairs):
    return lax.ppermute(value, RING_X, [p for a, b in pairs for p in ((a, b), (b, a))])


def in_order(index, mine, other, axis):
    first = jnp.where(index == 0, mine, other)
    second = jnp.where(index == 0, other, mine)
    return jnp.stack((first, second), axis=axis)


def join(index, mine, other, axis):
    first = jnp.where(index == 0, mine, other)
    second = jnp.where(index == 0, other, mine)
    return jnp.concatenate((first, second), axis=axis)


def pick(value, index, axis):
    return jnp.where(
        index == 0, lax.index_in_dim(value, 0, axis, False), lax.index_in_dim(value, 1, axis, False)
    )


def gather_chips(block, xh, text_cols=None):
    other = swap_x(block, ((0, 3), (1, 2)))
    if text_cols is not None:
        lo, hi = text_cols
        far = swap_x(block[:, lo:hi], ((0, 2), (1, 3)))
        other = jnp.concatenate((other[:, :lo], far, other[:, hi:]), axis=1)
    pair = in_order(xh, block, other, 0)
    full = lax.all_gather(pair, ("z", "y"), axis=0, tiled=False)
    cols = block.shape[-1]
    full = full.reshape(4, 4, 2, 32, cols)
    return full.transpose(0, 2, 1, 3, 4).reshape(CHIPS * 32, cols)


def scatter_chips(full, xh, text_cols=None):
    cols = full.shape[-1]
    blocks = full.reshape(4, 2, 4, 32, cols).transpose(0, 2, 1, 3, 4).reshape(16 * 64, cols)
    part = lax.psum_scatter(blocks, ("z", "y"), scatter_dimension=0, tiled=True)
    part = part.reshape(2, 32, cols)
    own = pick(part, xh, 0)
    far = pick(part, 1 - xh, 0)
    a = swap_x(own, ((0, 1), (2, 3)))
    b = swap_x(far, ((0, 3), (1, 2)))
    e = swap_x(far, ((0, 2), (1, 3)))
    near = a.astype(F32) + b.astype(F32)
    if text_cols is not None:
        col = lax.broadcasted_iota(jnp.int32, near.shape, 1)
        row = lax.broadcasted_iota(jnp.int32, near.shape, 0)
        is_text = (col >= text_cols[0]) & (col < text_cols[1]) & (row % 16 < 12)
        near = jnp.where(is_text, 0.0, near)
    return (own.astype(F32) + e.astype(F32)) + near


def halves_as_rows(value):
    k = value.shape[-1] // 2
    return jnp.concatenate((value[:, :k], value[:, k:]), axis=0)


def rows_as_halves(value):
    r = value.shape[0] // 2
    return jnp.concatenate((value[:r], value[r:]), axis=1)


def per_device(
    tokens_in,
    noise_emb,
    text_emb,
    prompt_len,
    mod_weight,
    qkv_weight,
    proj_weight,
    cq_weight,
    text_weight,
    co_weight,
    norm_gains,
    up_weight,
    down_weight,
    out_grad,
):
    core = lax.axis_index("core")
    xh = lax.axis_index("xh")
    xl = lax.axis_index("xl")
    rows = tokens_in.shape[1]

    misc = jnp.concatenate(
        (
            noise_emb,
            jnp.pad(text_emb[0], ((0, 0), (0, D - TEXT_W))),
            jnp.broadcast_to(prompt_len.astype(BF)[:, None], (7, D)),
        ),
        axis=0,
    )
    mine = jnp.concatenate((tokens_in[0], out_grad[0], misc), axis=0)
    both = in_order(core, mine, swap_core(mine), 0)
    tokens = both[:, :rows].astype(F32)
    grad_low = both[:, rows : 2 * rows]
    noise = both[:, 2 * rows]
    text = both[:, 2 * rows + 1 : 2 * rows + 9, :TEXT_W]
    lens = both[:, 2 * rows + 9, 0].astype(jnp.int32)

    def side(which):
        up = pick(up_weight.reshape(16, 32, 2, 64), which, 2).reshape(16, C_UP)
        qkv = pick(qkv_weight.reshape(16, 3, 2, 512), which, 2).reshape(16, C_QKV)
        mod = pick(mod_weight.reshape(16, 2, 2, 512), which, 2).reshape(16, C_MOD)
        cq = pick(cq_weight.reshape(16, 2, 512), which, 1)
        txt = pick(text_weight.reshape(12, 2, 2, 256), which, 2).reshape(12, C_TEXT)
        gains = jnp.pad(norm_gains, ((0, 2), (0, C_TEXT - 16)))
        return jnp.concatenate((mod, qkv, cq, jnp.concatenate((txt, gains), axis=0), up), axis=1)

    shared = join(core, side(core), swap_core(side(1 - core)), 0)
    first = jnp.concatenate(
        (
            shared[:, : C_MOD + C_QKV + C_CQ + C_TEXT],
            halves_as_rows(proj_weight),
            halves_as_rows(co_weight),
        ),
        axis=1,
    )
    second = jnp.concatenate(
        (shared[:, C_MOD + C_QKV + C_CQ + C_TEXT :],
         jnp.concatenate((down_weight[:32], down_weight[32:]), axis=1)),
        axis=1,
    )
    full_one = gather_chips(first, xh, TEXT_COLS)
    full_two = gather_chips(second, xh)

    at = 0
    pieces = []
    for width in (C_MOD, C_QKV, C_CQ, C_TEXT, C_PROJ, C_CO):
        pieces.append(full_one[:, at : at + width])
        at += width
    mod_w, qkv_w, cq_w, text_rows, proj_raw, co_raw = pieces
    text_rows = text_rows.reshape(64, 16, C_TEXT)
    text_w = text_rows[:, :12].reshape(TEXT_W, 2, 256)
    gains = text_rows[:, 12:14, :16].transpose(1, 0, 2).reshape(2, D).astype(F32)
    gain_two, gain_three = gains[0], gains[1]
    raw = jnp.stack((proj_raw, co_raw), axis=0).reshape(2, CHIPS, 2, 16, 512)
    raw = raw.transpose(0, 1, 3, 2, 4).reshape(2, 2, 16, 16, D)
    kept = pick(raw, core, 1)
    came = swap_core(pick(raw, 1 - core, 1))
    by_head = in_order(core, kept, came, 2).reshape(2, 512, D)
    proj_w, co_w = by_head[0], by_head[1]
    up_w = full_two[:, :C_UP]
    down_w = full_two[:, C_UP:].reshape(CHIPS, 32, 2, D).transpose(0, 2, 1, 3).reshape(2048, D)

    mod_part = jnp.dot(noise, mod_w, preferred_element_type=F32).reshape(2, 2, 512)
    mod_all = join(core, mod_part, swap_core(mod_part), 2)
    mod_scale, mod_shift = mod_all[:, 0], mod_all[:, 1]
    normed_one = modulated_norm(tokens, mod_scale, mod_shift).astype(BF)
    qkv = matmul(normed_one, qkv_w).astype(BF)
    queries = split_heads(qkv[:, :, :512])
    kv_own = qkv[:, :, 512:]
    kv_all = jnp.concatenate((kv_own, swap_seq(kv_own)), axis=1)
    keys_all = split_heads(kv_all[:, :, :512])
    values_all = split_heads(kv_all[:, :, 512:])
    mixed, self_lse = attend_forward(queries, keys_all, values_all, None)
    attended = mixed.reshape(2, rows, 512).astype(BF)
    proj_part = matmul(attended, proj_w)
    after_self = tokens + (proj_part + swap_core(proj_part))
    normed_two = gained_norm(after_self, gain_two).astype(BF)
    cross_q = split_heads(matmul(normed_two, cq_w).astype(BF))
    text_own = jnp.einsum("ijt,tcn->ijcn", text, text_w, preferred_element_type=F32).astype(BF)
    text_xl = in_order(xl, text_own, swap_seq(text_own), 0)
    text_kv = join(core, pick(text_xl, core, 0), swap_core(pick(text_xl, 1 - core, 0)), 3)
    text_keys = split_heads(text_kv[:, :, 0])
    text_vals = split_heads(text_kv[:, :, 1])
    usable = jnp.arange(TXT, dtype=jnp.int32)[None, :] < lens[:, None]
    cross_heads, cross_lse = attend_forward(cross_q, text_keys, text_vals, usable)
    cross_att = cross_heads.reshape(2, rows, 512).astype(BF)
    co_part = matmul(cross_att, co_w)
    after_cross = after_self + (co_part + swap_core(co_part))
    normed_three = gained_norm(after_cross, gain_three).astype(BF)
    pre_act = matmul(normed_three, up_w)
    activated = jax.nn.gelu(pre_act, approximate=True).astype(BF)
    down_part = matmul(activated, down_w)
    down_own = pick(down_part, core, 0) + swap_core(pick(down_part, 1 - core, 0))
    block_out = (pick(after_cross, core, 0) + down_own).astype(BF)[None]

    down_wg = outer_sum(activated, grad_low)
    act_grad = matmul_back(grad_low, down_w)
    _, gelu_back = jax.vjp(partial(jax.nn.gelu, approximate=True), pre_act)
    pre_grad = gelu_back(act_grad)[0].astype(BF)
    up_wg = outer_sum(normed_three, pre_grad)
    three_part = matmul_back(pre_grad, up_w)
    down_pack = down_wg.reshape(CHIPS, 2, 32, D).transpose(0, 2, 1, 3).reshape(D, C_DOWN)
    grads_two = scatter_chips(
        jnp.concatenate((up_wg.astype(BF), down_pack.astype(BF)), axis=1), xh
    )
    three_grad = three_part + swap_core(three_part)
    _, back_three = jax.vjp(gained_norm, after_cross, gain_three)
    cross_tok_grad, gain_three_grad = back_three(three_grad)
    cross_res_grad = grad_low.astype(F32) + cross_tok_grad
    cross_out_grad = cross_res_grad.astype(BF)
    co_wg = outer_sum(cross_att, cross_out_grad)
    cross_att_grad = matmul_back(cross_out_grad, co_w).astype(BF)
    cq_heads_grad, text_key_grad, text_val_grad = attend_backward(
        cross_q, text_keys, text_vals, usable, cross_lse, split_heads(cross_att_grad)
    )
    text_sum = jnp.stack(
        (text_key_grad.reshape(2, TXT, 512), text_val_grad.reshape(2, TXT, 512)), axis=2
    )
    text_sum = (text_sum + swap_seq(text_sum.astype(BF)).astype(F32)).astype(BF)
    text_quarters = text_sum.reshape(2, TXT, 2, 2, 256)
    text_kept = pick(text_quarters, core, 3)
    text_came = swap_core(pick(text_quarters, 1 - core, 3))
    text_kv_grad = jnp.where(core == xl, text_kept, text_came)
    text_wg = jnp.einsum("ijt,ijcn->tcn", text, text_kv_grad, preferred_element_type=F32)
    text_part = jnp.einsum("ijcn,tcn->ijt", text_kv_grad, text_w, preferred_element_type=F32)
    cross_q_grad = cq_heads_grad.reshape(2, rows, 512).astype(BF)
    cq_wg = outer_sum(normed_two, cross_q_grad)
    two_part = matmul_back(cross_q_grad, cq_w)
    two_grad = two_part + swap_core(two_part)
    _, back_two = jax.vjp(gained_norm, after_self, gain_two)
    self_tok_grad, gain_two_grad = back_two(two_grad)
    self_res_grad = cross_res_grad + self_tok_grad
    proj_out_grad = self_res_grad.astype(BF)
    proj_wg = outer_sum(attended, proj_out_grad)
    attended_grad = matmul_back(proj_out_grad, proj_w).astype(BF)
    query_grad, key_grad, value_grad = attend_backward(
        queries, keys_all, values_all, None, self_lse, split_heads(attended_grad)
    )
    kv_sum = jnp.concatenate(
        (key_grad.reshape(2, 2 * rows, 512), value_grad.reshape(2, 2 * rows, 512)), axis=2
    )
    kv_came = swap_seq(kv_sum[:, rows:].astype(BF))
    kv_grad = (kv_sum[:, :rows] + kv_came.astype(F32)).astype(BF)
    qkv_grad = jnp.concatenate((query_grad.reshape(2, rows, 512).astype(BF), kv_grad), axis=2)
    qkv_wg = outer_sum(normed_one, qkv_grad)
    one_part = matmul_back(qkv_grad, qkv_w)
    one_grad = pick(one_part, core, 0) + swap_core(pick(one_part, 1 - core, 0))

    own_tokens = tokens_in.astype(F32)
    _, mod_back = jax.vjp(
        modulated_norm, own_tokens, pick(mod_scale, core, 0)[None], pick(mod_shift, core, 0)[None]
    )
    input_part, scale_grad, shift_grad = mod_back(one_grad[None])
    tokens_grad = pick(self_res_grad, core, 0)[None] + input_part
    mod_own = jnp.concatenate((scale_grad, shift_grad), axis=0)
    mod_grad = in_order(core, mod_own, swap_core(mod_own), 0)
    mod_half = pick(mod_grad.reshape(2, 2, 2, 512), core, 2).reshape(2, C_MOD)
    mod_wg = jnp.dot(noise.astype(F32).T, mod_half, precision=HIGHEST_PREC)
    noise_part = jnp.dot(mod_half, mod_w.astype(F32).T, precision=HIGHEST_PREC)

    rows_wg = jnp.stack((proj_wg.astype(BF), co_wg.astype(BF)), axis=0).reshape(2, 16, 2, 16, D)
    rows_kept = pick(rows_wg, core, 2)
    rows_came = swap_core(pick(rows_wg, 1 - core, 2))
    rows_all = join(core, rows_kept, rows_came, 1)
    rows_all = rows_all.reshape(2, CHIPS, 16, 2, 512).transpose(0, 1, 3, 2, 4).reshape(2, D, 512)
    gains_wg = jnp.stack((gain_two_grad, gain_three_grad), axis=0).astype(BF)
    gains_wg = jnp.pad(
        gains_wg.reshape(2, 64, 16).transpose(1, 0, 2), ((0, 0), (0, 2), (0, C_TEXT - 16))
    )
    text_pack = jnp.concatenate((text_wg.astype(BF).reshape(64, 12, C_TEXT), gains_wg), axis=1)
    grads_one = scatter_chips(
        jnp.concatenate(
            (
                mod_wg.astype(BF),
                qkv_wg.astype(BF),
                cq_wg.astype(BF),
                text_pack.reshape(D, C_TEXT),
                rows_all[0],
                rows_all[1],
            ),
            axis=1,
        ),
        xh,
        TEXT_COLS,
    )

    shared_cols = C_MOD + C_QKV + C_CQ + C_TEXT
    grads = jnp.concatenate((grads_one[:, :shared_cols], grads_two[:, :C_UP]), axis=1)
    grads = grads.reshape(2, 16, shared_cols + C_UP)
    got = swap_core(pick(grads, 1 - core, 0).astype(BF)).astype(F32)
    kept_cols = pick(grads, core, 0)
    by_core = in_order(core, kept_cols, got, 0)
    at = 0
    pieces = []
    for width in (C_MOD, C_QKV, C_CQ, C_TEXT, C_UP):
        pieces.append(by_core[:, :, at : at + width])
        at += width
    mod_g, qkv_g, cq_g, text_g, up_g = pieces
    mod_wgrad = mod_g.reshape(2, 16, 2, 512).transpose(1, 2, 0, 3).reshape(16, 2 * D)
    qkv_wgrad = qkv_g.reshape(2, 16, 3, 512).transpose(1, 2, 0, 3).reshape(16, 3, D)
    cq_wgrad = cq_g.transpose(1, 0, 2).reshape(16, D)
    text_wgrad = text_g[:, :12].reshape(2, 12, 2, 256).transpose(1, 2, 0, 3).reshape(12, 2, 512)
    gains_grad = kept_cols[12:14, C_MOD + C_QKV + C_CQ : C_MOD + C_QKV + C_CQ + 16]
    up_wgrad = up_g.reshape(2, 16, 32, 64).transpose(1, 2, 0, 3).reshape(16, FF)
    proj_wgrad = rows_as_halves(grads_one[:, shared_cols : shared_cols + C_PROJ])
    co_wgrad = rows_as_halves(grads_one[:, shared_cols + C_PROJ :])
    down_g = grads_two[:, C_UP:]
    down_wgrad = jnp.concatenate((down_g[:, :D], down_g[:, D:]), axis=0)

    small = jnp.concatenate((noise_part[:, None], jnp.pad(text_part, ((0, 0), (0, 0), (0, D - TEXT_W)))), axis=1)
    small = pick(small, core, 0) + swap_core(pick(small, 1 - core, 0))
    small = small + swap_seq(small)
    return (
        block_out,
        tokens_grad,
        small[:1],
        small[None, 1:, :TEXT_W],
        mod_wgrad,
        qkv_wgrad,
        proj_wgrad,
        cq_wgrad,
        text_wgrad,
        co_wgrad,
        gains_grad,
        up_wgrad,
        down_wgrad,
    )


def solution(mesh):
    split = Mesh(mesh.devices.reshape(SIZES), AXES)
    in_specs = (
        P(FSDP, "xl", None),
        P(FSDP, None),
        P(FSDP, None, None),
        P(FSDP),
        P(FSDP, None),
        P(FSDP, None, None),
        P(FSDP, None),
        P(FSDP, None),
        P(FSDP, None, "xl"),
        P(FSDP, None),
        P(None, FSDP),
        P(FSDP, None),
        P(FSDP, None),
        P(FSDP, "xl", None),
    )
    out_specs = (
        P(FSDP, "xl", None),
        P(FSDP, "xl", None),
        P(FSDP, None),
        P(FSDP, None, None),
        P(FSDP, None),
        P(FSDP, None, None),
        P(FSDP, None),
        P(FSDP, None),
        P(FSDP, None, "xl"),
        P(FSDP, None),
        P(None, FSDP),
        P(FSDP, None),
        P(FSDP, None),
    )
    return jax.shard_map(
        per_device, mesh=split, in_specs=in_specs, out_specs=out_specs, check_vma=False
    )
```

```python
import jax
import jax.numpy as jnp
from jax import lax
from jax.experimental import pallas as pl
from jax.experimental.pallas import tpu as pltpu
from jax.sharding import Mesh
from jax.sharding import PartitionSpec as P

HEAD_DIM = 64
EPSILON = 1e-06
HIGHEST_PREC = lax.Precision.HIGHEST
NEG_LARGE = -1e30
BF = jnp.bfloat16
F32 = jnp.float32

AXES = ("z", "xh", "y", "core", "xl")
SIZES = (4, 2, 4, 2, 2)
FSDP = ("z", "xh", "y", "core")
RING_X = ("xh", "xl")

D = 1024
FF = 4096
TEXT_W = 768
TXT = 8
CHIPS = 32

C_MOD, C_QKV, C_CQ, C_TEXT, C_PROJ, C_CO = 1024, 1536, 512, 512, 512, 512
TEXT_COLS = (C_MOD + C_QKV + C_CQ, C_MOD + C_QKV + C_CQ + C_TEXT)
C_UP, C_DOWN = 2048, 2048


def rms_norm(tensor):
    return tensor * lax.rsqrt(jnp.mean(tensor * tensor, axis=-1, keepdims=True) + EPSILON)


def modulated_norm(tensor, scale, shift):
    return rms_norm(tensor) * (1.0 + scale[:, None, :]) + shift[:, None, :]


def mm(a, b):
    return jnp.dot(a, b, preferred_element_type=F32)


def mm_nt(a, b):
    return lax.dot_general(a, b, (((1,), (1,)), ((), ())), preferred_element_type=F32)


def mm_tn(a, b):
    return lax.dot_general(a, b, (((0,), (0,)), ((), ())), preferred_element_type=F32)


CHIP_ORDER = [(z, xh, y) for z in range(4) for xh in range(2) for y in range(4)]


def nat(ref):
    return jnp.concatenate([ref[z, y, xh] for z, xh, y in CHIP_ORDER], axis=0)


def store_nat(ref, value):
    for i, (z, xh, y) in enumerate(CHIP_ORDER):
        ref[z, y, xh] = value[32 * i : 32 * i + 32].astype(ref.dtype)


def norm_of(x):
    inv = lax.rsqrt(jnp.mean(x * x, axis=-1, keepdims=True) + EPSILON)
    return x * inv, inv


def norm_grad(unit, inv, dh_w):
    return (dh_w - unit * jnp.mean(dh_w * unit, axis=-1, keepdims=True)) * inv


def call(body, outs, ins, scratch=(), specs=None, out_specs=None, grid=None, prefetch=0):
    whole = pl.BlockSpec(memory_space=pltpu.VMEM)
    return pl.pallas_call(
        body,
        out_shape=outs,
        grid_spec=pltpu.PrefetchScalarGridSpec(
            num_scalar_prefetch=prefetch,
            grid=grid or (),
            in_specs=specs or [whole] * len(ins),
            out_specs=out_specs or [whole] * len(outs),
            scratch_shapes=list(scratch),
        ),
        compiler_params=pltpu.CompilerParams(vmem_limit_bytes=60 * 1024 * 1024),
    )(*ins)


def shape(dims, dtype):
    return jax.ShapeDtypeStruct(dims, dtype)


WHOLE = pl.BlockSpec(memory_space=pltpu.VMEM)
SMEM = pl.BlockSpec(memory_space=pltpu.SMEM)


def cols_spec(block, width=512):
    return pl.BlockSpec((4, 4, 2, 32, width), lambda i: (0, 0, 0, 0, block))


def fixed(dims):
    return pl.BlockSpec(dims, lambda i: (0,) * len(dims))


def mod_body(noise, w, out):
    out[...] = mm(noise[...], nat(w))


def mod_kernel(noise, full):
    return call(
        mod_body,
        [shape((2, 1024), F32)],
        (noise, full),
        specs=[fixed((2, D)), cols_spec(0, 1024)],
        out_specs=[fixed((2, 1024))],
        grid=(1,),
    )[0]


def qkv_body(tok, scale, shift, wq, wk, wv, n1_out, q_out, kv_out):
    for b in range(2):
        r = slice(128 * b, 128 * b + 128)
        unit, _ = norm_of(tok[r].astype(F32))
        n1_out[r] = (unit * (1.0 + scale[b : b + 1]) + shift[b : b + 1]).astype(BF)
    n1 = n1_out[...]
    q_out[...] = mm(n1, nat(wq)).astype(BF)
    kv_out[:, :512] = mm(n1, nat(wk)).astype(BF)
    kv_out[:, 512:] = mm(n1, nat(wv)).astype(BF)


def qkv_kernel(tok, scale, shift, full):
    return call(
        qkv_body,
        [shape((256, D), BF), shape((256, 512), BF), shape((256, D), BF)],
        (tok, scale, shift, full, full, full),
        specs=[fixed((256, D)), fixed((2, D)), fixed((2, D)), cols_spec(2), cols_spec(3), cols_spec(4)],
        out_specs=[fixed((256, D)), fixed((256, 512)), fixed((256, D))],
        grid=(1,),
    )


def head_cols(h):
    return slice(64 * h, 64 * h + 64)


def self_probs(q, k):
    scores = mm_nt(q, k) * HEAD_DIM ** (-0.5)
    e = jnp.exp(scores - jnp.max(scores, axis=-1, keepdims=True))
    return e * (1.0 / jnp.sum(e, axis=-1, keepdims=True))


def attend_body(q, kv, kv_far, proj_w, att_out, part_out):
    for b in range(2):
        r = slice(128 * b, 128 * b + 128)
        for h in range(8):
            k = jnp.concatenate((kv[r, head_cols(h)], kv_far[r, head_cols(h)]), axis=0)
            v = jnp.concatenate((kv[r, head_cols(8 + h)], kv_far[r, head_cols(8 + h)]), axis=0)
            p = self_probs(q[r, head_cols(h)], k).astype(BF)
            att_out[r, head_cols(h)] = mm(p, v).astype(BF)
    part_out[...] = mm(att_out[...], proj_w[...])


def attend_kernel(q, kv, kv_far, proj_w):
    return call(
        attend_body, [shape((256, 512), BF), shape((256, D), F32)], (q, kv, kv_far, proj_w)
    )


def spread_heads(rows8):
    tall = jnp.concatenate([rows8.astype(F32)] * 16, axis=0)
    row = lax.broadcasted_iota(jnp.int32, tall.shape, 0) // 8
    col = lax.broadcasted_iota(jnp.int32, tall.shape, 1) // 64
    return jnp.where(row == col, tall, 0.0).astype(BF)


def fold_heads(tall):
    row = lax.broadcasted_iota(jnp.int32, tall.shape, 0) // 8
    col = lax.broadcasted_iota(jnp.int32, tall.shape, 1) // 64
    kept = jnp.where(row == col, tall, 0.0)
    total = kept[0:8]
    for h in range(1, 8):
        total = total + kept[8 * h : 8 * h + 8]
    return total


def by_eights(op, x):
    lane = lax.broadcasted_iota(jnp.int32, x.shape, 1)
    for step in (1, 2, 4):
        up = pltpu.roll(x, x.shape[1] - step, 1)
        down = pltpu.roll(x, step, 1)
        x = op(x, jnp.where((lane & step) == 0, up, down))
    return x


def cross_probs(q, keys, length):
    scores = mm_nt(q, keys) * HEAD_DIM ** (-0.5)
    lane = lax.broadcasted_iota(jnp.int32, scores.shape, 1)
    scores = jnp.where((lane & 7) < length, scores, NEG_LARGE)
    e = jnp.exp(scores - by_eights(jnp.maximum, scores))
    return e * (1.0 / by_eights(jnp.add, e))


def cross_body(
    tok, part, part_far, gains, cq_w, text_kv, lens, co_w, res_out, n2_out, cq_out, att_out, part_out
):
    res_out[...] = tok[...].astype(F32) + (part[...] + part_far[...])
    unit, _ = norm_of(res_out[...])
    n2_out[...] = (unit * gains[0:1]).astype(BF)
    cq_out[...] = mm(n2_out[...], nat(cq_w)).astype(BF)
    for b in range(2):
        r = slice(128 * b, 128 * b + 128)
        keys = spread_heads(text_kv[b, :, 0:512])
        vals = spread_heads(text_kv[b, :, 512:1024])
        p = cross_probs(cq_out[r], keys, lens[b]).astype(BF)
        att_out[r] = mm(p, vals).astype(BF)
    part_out[...] = mm(att_out[...], co_w[...])


def cross_kernel(tok, part, part_far, gains, full, text_kv, lens, co_w):
    f = fixed
    return call(
        cross_body,
        [
            shape((256, D), F32),
            shape((256, D), BF),
            shape((256, 512), BF),
            shape((256, 512), BF),
            shape((256, D), F32),
        ],
        (tok, part, part_far, gains, full, text_kv, lens, co_w),
        specs=[
            f((256, D)),
            f((256, D)),
            f((256, D)),
            f((2, D)),
            cols_spec(5),
            f((2, 8, D)),
            SMEM,
            f((512, D)),
        ],
        out_specs=[f((256, D)), f((256, D)), f((256, 512)), f((256, 512)), f((256, D))],
        grid=(1,),
    )


GELU_A = 0.7978845608028654
GELU_B = 0.044715


def ff_body(
    res, part, part_far, gains, og, up, down, res_out, grad_out, three_out, down_out, n3, g_up, g_down
):
    i = pl.program_id(0)

    @pl.when(i == 0)
    def _():
        res_out[...] = res[...] + (part[...] + part_far[...])
        unit, _ = norm_of(res_out[...])
        n3[...] = (unit * gains[1:2]).astype(BF)

    up_w = nat(up)
    down_w = jnp.concatenate(
        [
            down[0, y, xh, :, D * h : D * h + D]
            for xh in range(2)
            for y in range(4)
            for h in range(2)
        ],
        axis=0,
    )
    pre = mm(n3[...], up_w)
    t = jnp.tanh(GELU_A * (pre + GELU_B * (pre * pre * pre)))
    act = (0.5 * pre * (1.0 + t)).astype(BF)
    slope = 0.5 * (1.0 + t) + 0.5 * pre * (1.0 - t * t) * (
        GELU_A * (1.0 + 3.0 * GELU_B * (pre * pre))
    )
    pre_grad = (mm_nt(og[...], down_w) * slope).astype(BF)
    down_part = mm(act, down_w)
    three_part = mm_nt(pre_grad, up_w)

    @pl.when(i == 0)
    def _():
        down_out[...] = down_part
        three_out[...] = three_part

    @pl.when(i > 0)
    def _():
        down_out[...] += down_part
        three_out[...] += three_part

    up_wg = mm_tn(n3[...], pre_grad).astype(BF)
    down_wg = mm_tn(act, og[...]).astype(BF)
    for j, (z, xh, y) in enumerate(CHIP_ORDER):
        g_up[z, y, xh] = up_wg[32 * j : 32 * j + 32]
    j = 0
    for xh in range(2):
        for y in range(4):
            for h in range(2):
                g_down[0, y, xh, :, D * h : D * h + D] = down_wg[32 * j : 32 * j + 32]
                j += 1
    grad_out[:, :, :, :, pl.ds(pl.multiple_of(i * 512, 512), 512)] = g_up[...]
    grad_out[pl.ds(i, 1), :, :, :, C_UP:] = g_down[...]


def ff_kernel(res, part, part_far, gains, og, full):
    f = fixed
    return call(
        ff_body,
        [
            shape((256, D), F32),
            shape((4, 4, 2, 32, C_UP + C_DOWN), BF),
            shape((256, D), F32),
            shape((256, D), F32),
        ],
        (res, part, part_far, gains, og, full, full),
        scratch=[
            pltpu.VMEM((256, D), BF),
            pltpu.VMEM((4, 4, 2, 32, 512), BF),
            pltpu.VMEM((1, 4, 2, 32, 2048), BF),
        ],
        specs=[
            f((256, D)),
            f((256, D)),
            f((256, D)),
            f((2, D)),
            f((256, D)),
            pl.BlockSpec((4, 4, 2, 32, 512), lambda i: (0, 0, 0, 0, i)),
            pl.BlockSpec((1, 4, 2, 32, 2048), lambda i: (i, 0, 0, 0, 1)),
        ],
        out_specs=[f((256, D)), f((4, 4, 2, 32, C_UP + C_DOWN)), f((256, D)), f((256, D))],
        grid=(4,),
    )


def cross_back_body(
    part, part_far, res, og, gains, att, cq, n2, text_kv, lens, co_w, cq_w,
    grad_out, gain_out, co_out, cqw_out, text_out, two_out, ag, dq,
):
    unit, inv = norm_of(res[...])
    three = part[...] + part_far[...]
    gain_out[...] = jnp.sum(three * unit, axis=0, keepdims=True)
    grad_out[...] = og[...].astype(F32) + norm_grad(unit, inv, three * gains[1:2])
    low = grad_out[...].astype(BF)
    co_out[...] = mm_tn(att[...], low).astype(BF)
    ag[...] = mm_nt(low, co_w[...]).astype(BF)
    for b in range(2):
        r = slice(128 * b, 128 * b + 128)
        keys = spread_heads(text_kv[b, :, 0:512])
        vals = spread_heads(text_kv[b, :, 512:1024])
        p = cross_probs(cq[r], keys, lens[b])
        dp = mm_nt(ag[r], vals)
        ds = (p * (dp - by_eights(jnp.add, p * dp))).astype(BF)
        dq[r] = (mm(ds, keys) * HEAD_DIM ** (-0.5)).astype(BF)
        text_out[b, :, 0:512] = fold_heads(mm_tn(ds, cq[r])) * HEAD_DIM ** (-0.5)
        text_out[b, :, 512:1024] = fold_heads(mm_tn(p.astype(BF), ag[r]))
    store_nat(cqw_out, mm_tn(n2[...], dq[...]))
    two_out[...] = mm_nt(dq[...], nat(cq_w))


def cross_back_kernel(part, part_far, res, og, gains, att, cq, n2, text_kv, lens, co_w, full):
    f = fixed
    return call(
        cross_back_body,
        [
            shape((256, D), F32),
            shape((1, D), F32),
            shape((512, D), BF),
            shape((4, 4, 2, 32, 512), BF),
            shape((2, 8, D), F32),
            shape((256, D), F32),
        ],
        (part, part_far, res, og, gains, att, cq, n2, text_kv, lens, co_w, full),
        scratch=[pltpu.VMEM((256, 512), BF), pltpu.VMEM((256, 512), BF)],
        specs=[
            f((256, D)),
            f((256, D)),
            f((256, D)),
            f((256, D)),
            f((2, D)),
            f((256, 512)),
            f((256, 512)),
            f((256, D)),
            f((2, 8, D)),
            SMEM,
            f((512, D)),
            cols_spec(5),
        ],
        out_specs=[
            f((256, D)),
            f((1, D)),
            f((512, D)),
            f((4, 4, 2, 32, 512)),
            f((2, 8, D)),
            f((256, D)),
        ],
        grid=(1,),
    )


def self_back_body(
    part, part_far, res, res_grad, gains, att, q, kv, kv_far, proj_w,
    grad_out, gain_out, proj_out, dq_out, dkv_out, dfar_out, ag,
):
    unit, inv = norm_of(res[...])
    two = part[...] + part_far[...]
    gain_out[...] = jnp.sum(two * unit, axis=0, keepdims=True)
    grad_out[...] = res_grad[...] + norm_grad(unit, inv, two * gains[0:1])
    low = grad_out[...].astype(BF)
    proj_out[...] = mm_tn(att[...], low).astype(BF)
    ag[...] = mm_nt(low, proj_w[...]).astype(BF)
    factor = HEAD_DIM ** (-0.5)
    for b in range(2):
        r = slice(128 * b, 128 * b + 128)
        for h in range(8):
            kc, vc = head_cols(h), head_cols(8 + h)
            k = jnp.concatenate((kv[r, kc], kv_far[r, kc]), axis=0)
            v = jnp.concatenate((kv[r, vc], kv_far[r, vc]), axis=0)
            qh = q[r, kc]
            gh = ag[r, kc]
            p = self_probs(qh, k)
            dp = mm_nt(gh, v)
            ds = (p * (dp - jnp.sum(p * dp, axis=-1, keepdims=True))).astype(BF)
            dq_out[r, kc] = (mm(ds, k) * factor).astype(BF)
            dk = mm_tn(ds, qh) * factor
            dv = mm_tn(p.astype(BF), gh)
            dkv_out[r, kc] = dk[:128]
            dkv_out[r, vc] = dv[:128]
            dfar_out[r, kc] = dk[128:].astype(BF)
            dfar_out[r, vc] = dv[128:].astype(BF)


def self_back_kernel(part, part_far, res, res_grad, gains, att, q, kv, kv_far, proj_w):
    return call(
        self_back_body,
        [
            shape((256, D), F32),
            shape((1, D), F32),
            shape((512, D), BF),
            shape((256, 512), BF),
            shape((256, D), F32),
            shape((256, D), BF),
        ],
        (part, part_far, res, res_grad, gains, att, q, kv, kv_far, proj_w),
        scratch=[pltpu.VMEM((256, 512), BF)],
    )


def qkv_back_body(dq, dkv, dfar, n1, wq, wk, wv, wg_out, part_out):
    n = n1[...]
    dqv = dq[...]
    dkvv = (dkv[...] + dfar[...].astype(F32)).astype(BF)
    grads = (dqv, dkvv[:, :512], dkvv[:, 512:])
    total = None
    for i, (g, w) in enumerate(zip(grads, (wq, wk, wv))):
        wg = mm_tn(n, g).astype(BF)
        for j, (z, xh, y) in enumerate(CHIP_ORDER):
            wg_out[z, y, xh, :, 512 * i : 512 * i + 512] = wg[32 * j : 32 * j + 32]
        t = mm_nt(g, nat(w))
        total = t if total is None else total + t
    part_out[...] = total


def qkv_back_kernel(dq, dkv, dfar, n1, full):
    f = fixed
    return call(
        qkv_back_body,
        [shape((4, 4, 2, 32, 1536), BF), shape((256, D), F32)],
        (dq, dkv, dfar, n1, full, full, full),
        specs=[
            f((256, 512)),
            f((256, D)),
            f((256, D)),
            f((256, D)),
            cols_spec(2),
            cols_spec(3),
            cols_spec(4),
        ],
        out_specs=[f((4, 4, 2, 32, 1536)), f((256, D))],
        grid=(1,),
    )


def rows_body(core, kept, came, proj_out, co_out):
    first = core[0] == 0
    i = 0
    for z in range(2):
        for xh in range(2):
            for y in range(4):
                a, b = kept[z, y, xh], came[z, y, xh]
                for bit in range(2):
                    t = jnp.where(first, a, b) if bit == 0 else jnp.where(first, b, a)
                    for out, c in ((proj_out, 0), (co_out, 512)):
                        out[16 * i : 16 * i + 16, :512] = t[:16, c : c + 512]
                        out[16 * i : 16 * i + 16, 512:] = t[16:, c : c + 512]
                    i += 1


def rows_kernel(core, kept, came):
    return call(
        rows_body,
        [shape((512, D), BF), shape((512, D), BF)],
        (core, kept, came),
        specs=[SMEM, WHOLE, WHOLE],
    )


def rows_back_body(core, proj_wg, co_wg, kept_out, sent_out):
    first = core[0] == 0
    i = 0
    for z in range(2):
        for xh in range(2):
            for y in range(4):
                t = []
                for bit in range(2):
                    r = slice(16 * i, 16 * i + 16)
                    t.append(
                        jnp.concatenate(
                            (
                                jnp.concatenate((proj_wg[r, :512], proj_wg[r, 512:]), axis=0),
                                jnp.concatenate((co_wg[r, :512], co_wg[r, 512:]), axis=0),
                            ),
                            axis=1,
                        )
                    )
                    i += 1
                kept_out[z, y, xh] = jnp.where(first, t[0], t[1])
                sent_out[z, y, xh] = jnp.where(first, t[1], t[0])


def rows_back_kernel(core, proj_wg, co_wg):
    dims = shape((2, 4, 2, 32, D), BF)
    return call(
        rows_back_body, [dims, dims], (core, proj_wg, co_wg), specs=[SMEM, WHOLE, WHOLE]
    )


def swap_core(value):
    return lax.ppermute(value, "core", [(0, 1), (1, 0)])


def swap_seq(value):
    return lax.ppermute(value, "xl", [(0, 1), (1, 0)])


def swap_x(value, pairs):
    return lax.ppermute(value, RING_X, [p for a, b in pairs for p in ((a, b), (b, a))])


def in_order(index, mine, other, axis):
    first = jnp.where(index == 0, mine, other)
    second = jnp.where(index == 0, other, mine)
    return jnp.stack((first, second), axis=axis)


def join(index, mine, other, axis):
    first = jnp.where(index == 0, mine, other)
    second = jnp.where(index == 0, other, mine)
    return jnp.concatenate((first, second), axis=axis)


def pick(value, index, axis):
    return jnp.where(
        index == 0, lax.index_in_dim(value, 0, axis, False), lax.index_in_dim(value, 1, axis, False)
    )


def gather_chips(block, xh, text_cols=None):
    other = swap_x(block, ((0, 3), (1, 2)))
    if text_cols is not None:
        lo, hi = text_cols
        far = swap_x(block[:, lo:hi], ((0, 2), (1, 3)))
        other = jnp.concatenate((other[:, :lo], far, other[:, hi:]), axis=1)
    pair = in_order(xh, block, other, 0)
    full = lax.all_gather(pair, ("z", "y"), axis=0, tiled=False)
    cols = block.shape[-1]
    return full.reshape(4, 4, 2, 32, cols)


def scatter_chips(full, xh, text_cols=None):
    cols = full.shape[-1]
    part = lax.psum_scatter(full.reshape(D, cols), ("z", "y"), scatter_dimension=0, tiled=True)
    part = part.reshape(2, 32, cols)
    own = pick(part, xh, 0)
    far = pick(part, 1 - xh, 0)
    a = swap_x(own, ((0, 1), (2, 3)))
    b = swap_x(far, ((0, 3), (1, 2)))
    e = swap_x(far, ((0, 2), (1, 3)))
    near = a.astype(F32) + b.astype(F32)
    if text_cols is not None:
        col = lax.broadcasted_iota(jnp.int32, near.shape, 1)
        row = lax.broadcasted_iota(jnp.int32, near.shape, 0)
        is_text = (col >= text_cols[0]) & (col < text_cols[1]) & (row % 16 < 12)
        near = jnp.where(is_text, 0.0, near)
    return (own.astype(F32) + e.astype(F32)) + near


def halves_as_rows(value):
    k = value.shape[-1] // 2
    return jnp.concatenate((value[:, :k], value[:, k:]), axis=0)


def rows_as_halves(value):
    r = value.shape[0] // 2
    return jnp.concatenate((value[:r], value[r:]), axis=1)


def per_device(
    tokens_in,
    noise_emb,
    text_emb,
    prompt_len,
    mod_weight,
    qkv_weight,
    proj_weight,
    cq_weight,
    text_weight,
    co_weight,
    norm_gains,
    up_weight,
    down_weight,
    out_grad,
):
    core = lax.axis_index("core")
    xh = lax.axis_index("xh")
    xl = lax.axis_index("xl")
    rows = tokens_in.shape[1]

    misc = jnp.concatenate(
        (
            noise_emb,
            jnp.pad(text_emb[0], ((0, 0), (0, D - TEXT_W))),
            jnp.broadcast_to(prompt_len.astype(BF)[:, None], (7, D)),
        ),
        axis=0,
    )
    mine = jnp.concatenate((tokens_in[0], out_grad[0], misc), axis=0)
    both = in_order(core, mine, swap_core(mine), 0)
    tok = both[:, :rows].reshape(256, D)
    og = both[:, rows : 2 * rows].reshape(256, D)
    noise = both[:, 2 * rows]
    text = both[:, 2 * rows + 1 : 2 * rows + 9, :TEXT_W]
    lens = both[:, 2 * rows + 9, 0].astype(jnp.int32)

    def side(which):
        up = pick(up_weight.reshape(16, 32, 2, 64), which, 2).reshape(16, C_UP)
        qkv = pick(qkv_weight.reshape(16, 3, 2, 512), which, 2).reshape(16, C_QKV)
        mod = pick(mod_weight.reshape(16, 2, 2, 512), which, 2).reshape(16, C_MOD)
        cq = pick(cq_weight.reshape(16, 2, 512), which, 1)
        txt = pick(text_weight.reshape(12, 2, 2, 256), which, 2).reshape(12, C_TEXT)
        gains = jnp.pad(norm_gains, ((0, 2), (0, C_TEXT - 16)))
        return jnp.concatenate((mod, qkv, cq, jnp.concatenate((txt, gains), axis=0), up), axis=1)

    shared = join(core, side(core), swap_core(side(1 - core)), 0)
    first = jnp.concatenate(
        (
            shared[:, : C_MOD + C_QKV + C_CQ + C_TEXT],
            halves_as_rows(proj_weight),
            halves_as_rows(co_weight),
        ),
        axis=1,
    )
    second = jnp.concatenate(
        (
            shared[:, C_MOD + C_QKV + C_CQ + C_TEXT :],
            jnp.concatenate((down_weight[:32], down_weight[32:]), axis=1),
        ),
        axis=1,
    )
    full_one = gather_chips(first, xh, TEXT_COLS)
    full_two = gather_chips(second, xh)

    text_rows = full_one[..., TEXT_COLS[0] : TEXT_COLS[1]].transpose(0, 2, 1, 3, 4)
    text_rows = text_rows.reshape(64, 16, C_TEXT)
    text_w = text_rows[:, :12].reshape(TEXT_W, 2, 256)
    gains = text_rows[:, 12:14, :16].transpose(1, 0, 2).reshape(2, D).astype(F32)
    halves = full_one[..., TEXT_COLS[1] :].reshape(2, 2, 4, 2, 32, D)
    kept = pick(halves, core, 0)
    core_id = core.astype(jnp.int32)[None]
    proj_w, co_w = rows_kernel(core_id, kept, swap_core(pick(halves, 1 - core, 0)))

    mod_part = mod_kernel(noise, full_one).reshape(2, 2, 512)
    mod_all = join(core, mod_part, swap_core(mod_part), 2)
    mod_scale, mod_shift = mod_all[:, 0], mod_all[:, 1]
    normed_one, queries, kv_own = qkv_kernel(tok, mod_scale, mod_shift, full_one)
    kv_far = swap_seq(kv_own)
    attended, proj_part = attend_kernel(queries, kv_own, kv_far, proj_w)
    text_own = jnp.einsum("ijt,tcn->ijcn", text, text_w, preferred_element_type=F32).astype(BF)
    text_xl = in_order(xl, text_own, swap_seq(text_own), 0)
    text_kv = join(core, pick(text_xl, core, 0), swap_core(pick(text_xl, 1 - core, 0)), 3)
    text_kv = text_kv.reshape(2, TXT, D)
    after_self, normed_two, cross_q, cross_att, co_part = cross_kernel(
        tok, proj_part, swap_core(proj_part), gains, full_one, text_kv, lens, co_w
    )
    after_cross, grads_ff, three_part, down_part = ff_kernel(
        after_self, co_part, swap_core(co_part), gains, og, full_two
    )
    grads_two = scatter_chips(grads_ff, xh)
    down_part = down_part.reshape(2, rows, D)
    down_own = pick(down_part, core, 0) + swap_core(pick(down_part, 1 - core, 0))
    block_out = (pick(after_cross.reshape(2, rows, D), core, 0) + down_own).astype(BF)[None]

    cross_res_grad, gain_three_grad, co_wg, cq_wg, text_sum, two_part = cross_back_kernel(
        three_part, swap_core(three_part), after_cross, og, gains, cross_att, cross_q,
        normed_two, text_kv, lens, co_w, full_one,
    )
    self_res_grad, gain_two_grad, proj_wg, dq, dkv, dkv_far = self_back_kernel(
        two_part, swap_core(two_part), after_self, cross_res_grad, gains, attended, queries,
        kv_own, kv_far, proj_w,
    )
    qkv_wg, one_part = qkv_back_kernel(dq, dkv, swap_seq(dkv_far), normed_one, full_one)

    text_sum = (text_sum + swap_seq(text_sum.astype(BF)).astype(F32)).astype(BF)
    text_quarters = text_sum.reshape(2, TXT, 2, 2, 256)
    text_kept = pick(text_quarters, core, 3)
    text_came = swap_core(pick(text_quarters, 1 - core, 3))
    text_kv_grad = jnp.where(core == xl, text_kept, text_came)
    text_wg = jnp.einsum("ijt,ijcn->tcn", text, text_kv_grad, preferred_element_type=F32)
    text_part = jnp.einsum("ijcn,tcn->ijt", text_kv_grad, text_w, preferred_element_type=F32)

    one_part = one_part.reshape(2, rows, D)
    one_grad = pick(one_part, core, 0) + swap_core(pick(one_part, 1 - core, 0))
    own_tokens = tokens_in.astype(F32)
    _, mod_back = jax.vjp(
        modulated_norm, own_tokens, pick(mod_scale, core, 0)[None], pick(mod_shift, core, 0)[None]
    )
    input_part, scale_grad, shift_grad = mod_back(one_grad[None])
    tokens_grad = pick(self_res_grad.reshape(2, rows, D), core, 0)[None] + input_part
    mod_own = jnp.concatenate((scale_grad, shift_grad), axis=0)
    mod_grad = in_order(core, mod_own, swap_core(mod_own), 0)
    mod_half = pick(mod_grad.reshape(2, 2, 2, 512), core, 2).reshape(2, C_MOD)
    noise_f = noise.astype(F32)
    noise_rows = noise_f.reshape(2, 4, 2, 4, 32).transpose(0, 1, 3, 2, 4)[..., None]
    mod_wg = noise_rows[0] * mod_half[0] + noise_rows[1] * mod_half[1]
    mod_w = full_one[..., :C_MOD].astype(F32)
    noise_part = jnp.einsum("ic,zyxrc->izxyr", mod_half, mod_w, precision=HIGHEST_PREC)
    noise_part = noise_part.reshape(2, D)

    rows_kept, rows_sent = rows_back_kernel(core_id, proj_wg, co_wg)
    rows_all = join(core, rows_kept, swap_core(rows_sent), 0)
    gains_wg = jnp.concatenate((gain_two_grad, gain_three_grad), axis=0).astype(BF)
    gains_wg = jnp.pad(
        gains_wg.reshape(2, 64, 16).transpose(1, 0, 2), ((0, 0), (0, 2), (0, C_TEXT - 16))
    )
    text_pack = jnp.concatenate((text_wg.astype(BF).reshape(64, 12, C_TEXT), gains_wg), axis=1)
    text_pack = text_pack.reshape(4, 2, 4, 32, C_TEXT).transpose(0, 2, 1, 3, 4)
    grads_one = scatter_chips(
        jnp.concatenate((mod_wg.astype(BF), qkv_wg, cq_wg, text_pack, rows_all), axis=4),
        xh,
        TEXT_COLS,
    )

    shared_cols = C_MOD + C_QKV + C_CQ + C_TEXT
    grads = jnp.concatenate((grads_one[:, :shared_cols], grads_two[:, :C_UP]), axis=1)
    grads = grads.reshape(2, 16, shared_cols + C_UP)
    got = swap_core(pick(grads, 1 - core, 0).astype(BF)).astype(F32)
    kept_cols = pick(grads, core, 0)
    by_core = in_order(core, kept_cols, got, 0)
    at = 0
    pieces = []
    for width in (C_MOD, C_QKV, C_CQ, C_TEXT, C_UP):
        pieces.append(by_core[:, :, at : at + width])
        at += width
    mod_g, qkv_g, cq_g, text_g, up_g = pieces
    mod_wgrad = mod_g.reshape(2, 16, 2, 512).transpose(1, 2, 0, 3).reshape(16, 2 * D)
    qkv_wgrad = qkv_g.reshape(2, 16, 3, 512).transpose(1, 2, 0, 3).reshape(16, 3, D)
    cq_wgrad = cq_g.transpose(1, 0, 2).reshape(16, D)
    text_wgrad = text_g[:, :12].reshape(2, 12, 2, 256).transpose(1, 2, 0, 3).reshape(12, 2, 512)
    gains_grad = kept_cols[12:14, C_MOD + C_QKV + C_CQ : C_MOD + C_QKV + C_CQ + 16]
    up_wgrad = up_g.reshape(2, 16, 32, 64).transpose(1, 2, 0, 3).reshape(16, FF)
    proj_wgrad = rows_as_halves(grads_one[:, shared_cols : shared_cols + C_PROJ])
    co_wgrad = rows_as_halves(grads_one[:, shared_cols + C_PROJ :])
    down_g = grads_two[:, C_UP:]
    down_wgrad = jnp.concatenate((down_g[:, :D], down_g[:, D:]), axis=0)

    small = jnp.concatenate((noise_part[:, None], jnp.pad(text_part, ((0, 0), (0, 0), (0, D - TEXT_W)))), axis=1)
    small = pick(small, core, 0) + swap_core(pick(small, 1 - core, 0))
    small = small + swap_seq(small)
    return (
        block_out,
        tokens_grad,
        small[:1],
        small[None, 1:, :TEXT_W],
        mod_wgrad,
        qkv_wgrad,
        proj_wgrad,
        cq_wgrad,
        text_wgrad,
        co_wgrad,
        gains_grad,
        up_wgrad,
        down_wgrad,
    )


def solution(mesh):
    split = Mesh(mesh.devices.reshape(SIZES), AXES)
    in_specs = (
        P(FSDP, "xl", None),
        P(FSDP, None),
        P(FSDP, None, None),
        P(FSDP),
        P(FSDP, None),
        P(FSDP, None, None),
        P(FSDP, None),
        P(FSDP, None),
        P(FSDP, None, "xl"),
        P(FSDP, None),
        P(None, FSDP),
        P(FSDP, None),
        P(FSDP, None),
        P(FSDP, "xl", None),
    )
    out_specs = (
        P(FSDP, "xl", None),
        P(FSDP, "xl", None),
        P(FSDP, None),
        P(FSDP, None, None),
        P(FSDP, None),
        P(FSDP, None, None),
        P(FSDP, None),
        P(FSDP, None),
        P(FSDP, None, "xl"),
        P(FSDP, None),
        P(None, FSDP),
        P(FSDP, None),
        P(FSDP, None),
    )
    return jax.shard_map(
        per_device, mesh=split, in_specs=in_specs, out_specs=out_specs, check_vma=False
    )
```

```python
import jax
import jax.numpy as jnp
from jax import lax
from jax.experimental import pallas as pl
from jax.experimental.pallas import tpu as pltpu
from jax.sharding import Mesh
from jax.sharding import PartitionSpec as P

HEAD_DIM = 64
EPSILON = 1e-06
HIGHEST_PREC = lax.Precision.HIGHEST
NEG_LARGE = -1e30
BF = jnp.bfloat16
F32 = jnp.float32

AXES = ("z", "xh", "y", "core", "xl")
SIZES = (4, 2, 4, 2, 2)
FSDP = ("z", "xh", "y", "core")
RING_X = ("xh", "xl")

D = 1024
FF = 4096
TEXT_W = 768
TXT = 8
CHIPS = 32

C_QKV, C_CQ, C_TEXT, C_PROJ, C_CO = 1536, 512, 512, 512, 512
TEXT_COLS = (C_QKV + C_CQ, C_QKV + C_CQ + C_TEXT)
C_UP, C_DOWN = 2048, 2048


def rms_norm(tensor):
    return tensor * lax.rsqrt(jnp.mean(tensor * tensor, axis=-1, keepdims=True) + EPSILON)


def modulated_norm(tensor, scale, shift):
    return rms_norm(tensor) * (1.0 + scale[:, None, :]) + shift[:, None, :]


def mm(a, b):
    return jnp.dot(a, b, preferred_element_type=F32)


def mm_nt(a, b):
    return lax.dot_general(a, b, (((1,), (1,)), ((), ())), preferred_element_type=F32)


def mm_tn(a, b):
    return lax.dot_general(a, b, (((0,), (0,)), ((), ())), preferred_element_type=F32)


CHIP_ORDER = [(z, xh, y) for z in range(4) for xh in range(2) for y in range(4)]


def nat(ref):
    return jnp.concatenate([ref[z, y, xh] for z, xh, y in CHIP_ORDER], axis=0)


def store_nat(ref, value):
    for i, (z, xh, y) in enumerate(CHIP_ORDER):
        ref[z, y, xh] = value[32 * i : 32 * i + 32].astype(ref.dtype)


def norm_of(x):
    inv = lax.rsqrt(jnp.mean(x * x, axis=-1, keepdims=True) + EPSILON)
    return x * inv, inv


def norm_grad(unit, inv, dh_w):
    return (dh_w - unit * jnp.mean(dh_w * unit, axis=-1, keepdims=True)) * inv


def call(body, outs, ins, scratch=(), specs=None, out_specs=None, grid=None, prefetch=0):
    whole = pl.BlockSpec(memory_space=pltpu.VMEM)
    return pl.pallas_call(
        body,
        out_shape=outs,
        grid_spec=pltpu.PrefetchScalarGridSpec(
            num_scalar_prefetch=prefetch,
            grid=grid or (),
            in_specs=specs or [whole] * len(ins),
            out_specs=out_specs or [whole] * len(outs),
            scratch_shapes=list(scratch),
        ),
        compiler_params=pltpu.CompilerParams(vmem_limit_bytes=60 * 1024 * 1024),
    )(*ins)


def shape(dims, dtype):
    return jax.ShapeDtypeStruct(dims, dtype)


WHOLE = pl.BlockSpec(memory_space=pltpu.VMEM)
SMEM = pl.BlockSpec(memory_space=pltpu.SMEM)


def cols_spec(block, width=512):
    return pl.BlockSpec((4, 4, 2, 32, width), lambda i: (0, 0, 0, 0, block))


def fixed(dims):
    return pl.BlockSpec(dims, lambda i: (0,) * len(dims))


def qkv_body(tok, scale, shift, wq, wk, wv, n1_out, q_out, kv_out):
    for b in range(2):
        r = slice(128 * b, 128 * b + 128)
        unit, _ = norm_of(tok[r].astype(F32))
        n1_out[r] = (unit * (1.0 + scale[b : b + 1]) + shift[b : b + 1]).astype(BF)
    n1 = n1_out[...]
    q_out[...] = mm(n1, nat(wq)).astype(BF)
    kv_out[:, :512] = mm(n1, nat(wk)).astype(BF)
    kv_out[:, 512:] = mm(n1, nat(wv)).astype(BF)


def qkv_kernel(tok, scale, shift, full):
    return call(
        qkv_body,
        [shape((256, D), BF), shape((256, 512), BF), shape((256, D), BF)],
        (tok, scale, shift, full, full, full),
        specs=[fixed((256, D)), fixed((2, D)), fixed((2, D)), cols_spec(0), cols_spec(1), cols_spec(2)],
        out_specs=[fixed((256, D)), fixed((256, 512)), fixed((256, D))],
        grid=(1,),
    )


def head_cols(h):
    return slice(64 * h, 64 * h + 64)


def self_probs(q, k):
    scores = mm_nt(q, k) * HEAD_DIM ** (-0.5)
    e = jnp.exp(scores - jnp.max(scores, axis=-1, keepdims=True))
    return e * (1.0 / jnp.sum(e, axis=-1, keepdims=True))


def attend_body(q, kv, kv_far, proj_w, att_out, part_out):
    for b in range(2):
        r = slice(128 * b, 128 * b + 128)
        for h in range(8):
            k = jnp.concatenate((kv[r, head_cols(h)], kv_far[r, head_cols(h)]), axis=0)
            v = jnp.concatenate((kv[r, head_cols(8 + h)], kv_far[r, head_cols(8 + h)]), axis=0)
            p = self_probs(q[r, head_cols(h)], k).astype(BF)
            att_out[r, head_cols(h)] = mm(p, v).astype(BF)
    part_out[...] = mm(att_out[...], proj_w[...])


def attend_kernel(q, kv, kv_far, proj_w):
    return call(
        attend_body, [shape((256, 512), BF), shape((256, D), F32)], (q, kv, kv_far, proj_w)
    )


def spread_heads(rows8):
    tall = jnp.concatenate([rows8.astype(F32)] * 16, axis=0)
    row = lax.broadcasted_iota(jnp.int32, tall.shape, 0) // 8
    col = lax.broadcasted_iota(jnp.int32, tall.shape, 1) // 64
    return jnp.where(row == col, tall, 0.0).astype(BF)


def fold_heads(tall):
    row = lax.broadcasted_iota(jnp.int32, tall.shape, 0) // 8
    col = lax.broadcasted_iota(jnp.int32, tall.shape, 1) // 64
    kept = jnp.where(row == col, tall, 0.0)
    total = kept[0:8]
    for h in range(1, 8):
        total = total + kept[8 * h : 8 * h + 8]
    return total


def by_eights(op, x):
    lane = lax.broadcasted_iota(jnp.int32, x.shape, 1)
    for step in (1, 2, 4):
        up = pltpu.roll(x, x.shape[1] - step, 1)
        down = pltpu.roll(x, step, 1)
        x = op(x, jnp.where((lane & step) == 0, up, down))
    return x


def cross_probs(q, keys, length):
    scores = mm_nt(q, keys) * HEAD_DIM ** (-0.5)
    lane = lax.broadcasted_iota(jnp.int32, scores.shape, 1)
    scores = jnp.where((lane & 7) < length, scores, NEG_LARGE)
    e = jnp.exp(scores - by_eights(jnp.maximum, scores))
    return e * (1.0 / by_eights(jnp.add, e))


def cross_body(
    tok, part, part_far, gains, cq_w, text_kv, lens, co_w, res_out, n2_out, cq_out, att_out, part_out
):
    res_out[...] = tok[...].astype(F32) + (part[...] + part_far[...])
    unit, _ = norm_of(res_out[...])
    n2_out[...] = (unit * gains[0:1]).astype(BF)
    cq_out[...] = mm(n2_out[...], nat(cq_w)).astype(BF)
    for b in range(2):
        r = slice(128 * b, 128 * b + 128)
        keys = spread_heads(text_kv[b, :, 0:512])
        vals = spread_heads(text_kv[b, :, 512:1024])
        p = cross_probs(cq_out[r], keys, lens[b]).astype(BF)
        att_out[r] = mm(p, vals).astype(BF)
    part_out[...] = mm(att_out[...], co_w[...])


def cross_kernel(tok, part, part_far, gains, full, text_kv, lens, co_w):
    f = fixed
    return call(
        cross_body,
        [
            shape((256, D), F32),
            shape((256, D), BF),
            shape((256, 512), BF),
            shape((256, 512), BF),
            shape((256, D), F32),
        ],
        (tok, part, part_far, gains, full, text_kv, lens, co_w),
        specs=[
            f((256, D)),
            f((256, D)),
            f((256, D)),
            f((2, D)),
            cols_spec(3),
            f((2, 8, D)),
            SMEM,
            f((512, D)),
        ],
        out_specs=[f((256, D)), f((256, D)), f((256, 512)), f((256, 512)), f((256, D))],
        grid=(1,),
    )


GELU_A = 0.7978845608028654
GELU_B = 0.044715


def ff_body(
    res, part, part_far, gains, og, up, down, res_out, grad_out, three_out, down_out, n3, g_up, g_down
):
    i = pl.program_id(0)

    @pl.when(i == 0)
    def _():
        res_out[...] = res[...] + (part[...] + part_far[...])
        unit, _ = norm_of(res_out[...])
        n3[...] = (unit * gains[1:2]).astype(BF)

    up_w = nat(up)
    down_w = jnp.concatenate(
        [
            down[0, y, xh, :, D * h : D * h + D]
            for xh in range(2)
            for y in range(4)
            for h in range(2)
        ],
        axis=0,
    )
    pre = mm(n3[...], up_w)
    t = jnp.tanh(GELU_A * (pre + GELU_B * (pre * pre * pre)))
    act = (0.5 * pre * (1.0 + t)).astype(BF)
    slope = 0.5 * (1.0 + t) + 0.5 * pre * (1.0 - t * t) * (
        GELU_A * (1.0 + 3.0 * GELU_B * (pre * pre))
    )
    pre_grad = (mm_nt(og[...], down_w) * slope).astype(BF)
    down_part = mm(act, down_w)
    three_part = mm_nt(pre_grad, up_w)

    @pl.when(i == 0)
    def _():
        down_out[...] = down_part
        three_out[...] = three_part

    @pl.when(i > 0)
    def _():
        down_out[...] += down_part
        three_out[...] += three_part

    up_wg = mm_tn(n3[...], pre_grad).astype(BF)
    down_wg = mm_tn(act, og[...]).astype(BF)
    for j, (z, xh, y) in enumerate(CHIP_ORDER):
        g_up[z, y, xh] = up_wg[32 * j : 32 * j + 32]
    j = 0
    for xh in range(2):
        for y in range(4):
            for h in range(2):
                g_down[0, y, xh, :, D * h : D * h + D] = down_wg[32 * j : 32 * j + 32]
                j += 1
    grad_out[:, :, :, :, pl.ds(pl.multiple_of(i * 512, 512), 512)] = g_up[...]
    grad_out[pl.ds(i, 1), :, :, :, C_UP:] = g_down[...]


def ff_kernel(res, part, part_far, gains, og, full):
    f = fixed
    return call(
        ff_body,
        [
            shape((256, D), F32),
            shape((4, 4, 2, 32, C_UP + C_DOWN), BF),
            shape((256, D), F32),
            shape((256, D), F32),
        ],
        (res, part, part_far, gains, og, full, full),
        scratch=[
            pltpu.VMEM((256, D), BF),
            pltpu.VMEM((4, 4, 2, 32, 512), BF),
            pltpu.VMEM((1, 4, 2, 32, 2048), BF),
        ],
        specs=[
            f((256, D)),
            f((256, D)),
            f((256, D)),
            f((2, D)),
            f((256, D)),
            pl.BlockSpec((4, 4, 2, 32, 512), lambda i: (0, 0, 0, 0, i)),
            pl.BlockSpec((1, 4, 2, 32, 2048), lambda i: (i, 0, 0, 0, 1)),
        ],
        out_specs=[f((256, D)), f((4, 4, 2, 32, C_UP + C_DOWN)), f((256, D)), f((256, D))],
        grid=(4,),
    )


def cross_back_body(
    part, part_far, res, og, gains, att, cq, n2, text_kv, lens, co_w, cq_w,
    grad_out, gain_out, co_out, cqw_out, text_out, two_out, ag, dq,
):
    unit, inv = norm_of(res[...])
    three = part[...] + part_far[...]
    gain_out[...] = jnp.sum(three * unit, axis=0, keepdims=True)
    grad_out[...] = og[...].astype(F32) + norm_grad(unit, inv, three * gains[1:2])
    low = grad_out[...].astype(BF)
    co_out[...] = mm_tn(att[...], low).astype(BF)
    ag[...] = mm_nt(low, co_w[...]).astype(BF)
    for b in range(2):
        r = slice(128 * b, 128 * b + 128)
        keys = spread_heads(text_kv[b, :, 0:512])
        vals = spread_heads(text_kv[b, :, 512:1024])
        p = cross_probs(cq[r], keys, lens[b])
        dp = mm_nt(ag[r], vals)
        ds = (p * (dp - by_eights(jnp.add, p * dp))).astype(BF)
        dq[r] = (mm(ds, keys) * HEAD_DIM ** (-0.5)).astype(BF)
        text_out[b, :, 0:512] = fold_heads(mm_tn(ds, cq[r])) * HEAD_DIM ** (-0.5)
        text_out[b, :, 512:1024] = fold_heads(mm_tn(p.astype(BF), ag[r]))
    store_nat(cqw_out, mm_tn(n2[...], dq[...]))
    two_out[...] = mm_nt(dq[...], nat(cq_w))


def cross_back_kernel(part, part_far, res, og, gains, att, cq, n2, text_kv, lens, co_w, full):
    f = fixed
    return call(
        cross_back_body,
        [
            shape((256, D), F32),
            shape((1, D), F32),
            shape((512, D), BF),
            shape((4, 4, 2, 32, 512), BF),
            shape((2, 8, D), F32),
            shape((256, D), F32),
        ],
        (part, part_far, res, og, gains, att, cq, n2, text_kv, lens, co_w, full),
        scratch=[pltpu.VMEM((256, 512), BF), pltpu.VMEM((256, 512), BF)],
        specs=[
            f((256, D)),
            f((256, D)),
            f((256, D)),
            f((256, D)),
            f((2, D)),
            f((256, 512)),
            f((256, 512)),
            f((256, D)),
            f((2, 8, D)),
            SMEM,
            f((512, D)),
            cols_spec(3),
        ],
        out_specs=[
            f((256, D)),
            f((1, D)),
            f((512, D)),
            f((4, 4, 2, 32, 512)),
            f((2, 8, D)),
            f((256, D)),
        ],
        grid=(1,),
    )


def self_back_body(
    part, part_far, res, res_grad, gains, att, q, kv, kv_far, proj_w,
    grad_out, gain_out, proj_out, dq_out, dkv_out, dfar_out, ag,
):
    unit, inv = norm_of(res[...])
    two = part[...] + part_far[...]
    gain_out[...] = jnp.sum(two * unit, axis=0, keepdims=True)
    grad_out[...] = res_grad[...] + norm_grad(unit, inv, two * gains[0:1])
    low = grad_out[...].astype(BF)
    proj_out[...] = mm_tn(att[...], low).astype(BF)
    ag[...] = mm_nt(low, proj_w[...]).astype(BF)
    factor = HEAD_DIM ** (-0.5)
    for b in range(2):
        r = slice(128 * b, 128 * b + 128)
        for h in range(8):
            kc, vc = head_cols(h), head_cols(8 + h)
            k = jnp.concatenate((kv[r, kc], kv_far[r, kc]), axis=0)
            v = jnp.concatenate((kv[r, vc], kv_far[r, vc]), axis=0)
            qh = q[r, kc]
            gh = ag[r, kc]
            p = self_probs(qh, k)
            dp = mm_nt(gh, v)
            ds = (p * (dp - jnp.sum(p * dp, axis=-1, keepdims=True))).astype(BF)
            dq_out[r, kc] = (mm(ds, k) * factor).astype(BF)
            dk = mm_tn(ds, qh) * factor
            dv = mm_tn(p.astype(BF), gh)
            dkv_out[r, kc] = dk[:128]
            dkv_out[r, vc] = dv[:128]
            dfar_out[r, kc] = dk[128:].astype(BF)
            dfar_out[r, vc] = dv[128:].astype(BF)


def self_back_kernel(part, part_far, res, res_grad, gains, att, q, kv, kv_far, proj_w):
    return call(
        self_back_body,
        [
            shape((256, D), F32),
            shape((1, D), F32),
            shape((512, D), BF),
            shape((256, 512), BF),
            shape((256, D), F32),
            shape((256, D), BF),
        ],
        (part, part_far, res, res_grad, gains, att, q, kv, kv_far, proj_w),
        scratch=[pltpu.VMEM((256, 512), BF)],
    )


def qkv_back_body(dq, dkv, dfar, n1, wq, wk, wv, wg_out, part_out):
    n = n1[...]
    dqv = dq[...]
    dkvv = (dkv[...] + dfar[...].astype(F32)).astype(BF)
    grads = (dqv, dkvv[:, :512], dkvv[:, 512:])
    total = None
    for i, (g, w) in enumerate(zip(grads, (wq, wk, wv))):
        wg = mm_tn(n, g).astype(BF)
        for j, (z, xh, y) in enumerate(CHIP_ORDER):
            wg_out[z, y, xh, :, 512 * i : 512 * i + 512] = wg[32 * j : 32 * j + 32]
        t = mm_nt(g, nat(w))
        total = t if total is None else total + t
    part_out[...] = total


def qkv_back_kernel(dq, dkv, dfar, n1, full):
    f = fixed
    return call(
        qkv_back_body,
        [shape((4, 4, 2, 32, 1536), BF), shape((256, D), F32)],
        (dq, dkv, dfar, n1, full, full, full),
        specs=[
            f((256, 512)),
            f((256, D)),
            f((256, D)),
            f((256, D)),
            cols_spec(0),
            cols_spec(1),
            cols_spec(2),
        ],
        out_specs=[f((4, 4, 2, 32, 1536)), f((256, D))],
        grid=(1,),
    )


def sum_body(*refs):
    total = refs[0][...].astype(F32)
    for r in refs[1:-1]:
        total = total + r[...].astype(F32)
    refs[-1][...] = total.astype(refs[-1].dtype)


def sum_kernel(*pieces):
    return call(sum_body, [shape(pieces[0].shape, BF)], pieces)[0]


LATE = C_QKV + C_TEXT + C_CQ + C_PROJ + C_CO
LATE_ROWS = LATE - C_PROJ - C_CO


def late_body(ids, text, qkv, cq, kept, came, out):
    out[:, :, :, :, :C_QKV] = qkv[...]
    at = C_QKV + C_TEXT
    out[:, :, :, :, C_QKV:at] = text[...]
    out[:, :, :, :, at : at + C_CQ] = cq[...]
    first = ids[0] == 0
    a, b = kept[...], came[...]
    out[:2, :, :, :, LATE_ROWS:] = jnp.where(first, a, b)
    out[2:, :, :, :, LATE_ROWS:] = jnp.where(first, b, a)


def late_kernel(ids, text, qkv, cq, kept, came):
    return call(
        late_body,
        [shape((4, 4, 2, 32, LATE), BF)],
        (ids, text, qkv, cq, kept, came),
        specs=[SMEM, *[WHOLE] * 5],
    )[0]


def late_sum_body(own, a, b, e, out):
    near = a[...].astype(F32) + b[...].astype(F32)
    row = lax.broadcasted_iota(jnp.int32, near.shape, 0) % 16
    col = lax.broadcasted_iota(jnp.int32, near.shape, 1)
    text = (col >= C_QKV) & (col < C_QKV + C_TEXT)
    near = jnp.where((row < 12) & text, 0.0, near)
    out[...] = (own[...].astype(F32) + e[...].astype(F32) + near).astype(BF)


def late_sum_kernel(own, a, b, e):
    return call(late_sum_body, [shape((32, LATE), BF)], (own, a, b, e))[0]


def rows_body(core, kept, came, proj_out, co_out):
    first = core[0] == 0
    i = 0
    for z in range(2):
        for xh in range(2):
            for y in range(4):
                a, b = kept[z, y, xh], came[z, y, xh]
                for bit in range(2):
                    t = jnp.where(first, a, b) if bit == 0 else jnp.where(first, b, a)
                    for out, c in ((proj_out, 0), (co_out, 512)):
                        out[16 * i : 16 * i + 16, :512] = t[:16, c : c + 512]
                        out[16 * i : 16 * i + 16, 512:] = t[16:, c : c + 512]
                    i += 1


def rows_kernel(core, kept, came):
    return call(
        rows_body,
        [shape((512, D), BF), shape((512, D), BF)],
        (core, kept, came),
        specs=[SMEM, WHOLE, WHOLE],
    )


def rows_back_body(core, proj_wg, co_wg, kept_out, sent_out):
    first = core[0] == 0
    i = 0
    for z in range(2):
        for xh in range(2):
            for y in range(4):
                t = []
                for bit in range(2):
                    r = slice(16 * i, 16 * i + 16)
                    t.append(
                        jnp.concatenate(
                            (
                                jnp.concatenate((proj_wg[r, :512], proj_wg[r, 512:]), axis=0),
                                jnp.concatenate((co_wg[r, :512], co_wg[r, 512:]), axis=0),
                            ),
                            axis=1,
                        )
                    )
                    i += 1
                kept_out[z, y, xh] = jnp.where(first, t[0], t[1])
                sent_out[z, y, xh] = jnp.where(first, t[1], t[0])


def rows_back_kernel(core, proj_wg, co_wg):
    dims = shape((2, 4, 2, 32, D), BF)
    return call(
        rows_back_body, [dims, dims], (core, proj_wg, co_wg), specs=[SMEM, WHOLE, WHOLE]
    )


def ff_unpack_body(ids, mine, came, down, up_out, down_out):
    first = ids[0] == 0
    a, b = mine[...].astype(F32), came[...].astype(F32)
    parts = (jnp.where(first, a, b), jnp.where(first, b, a))
    for i in range(32):
        for c in range(2):
            to = 128 * i + 64 * c
            up_out[:, to : to + 64] = parts[c][:, 64 * i : 64 * i + 64]
    down_out[:32] = down[:, :D].astype(F32)
    down_out[32:] = down[:, D:].astype(F32)


def ff_unpack_kernel(ids, mine, came, down):
    return call(
        ff_unpack_body,
        [shape((16, FF), F32), shape((64, D), F32)],
        (ids, mine, came, down),
        specs=[SMEM, WHOLE, WHOLE, WHOLE],
    )


def late_unpack_body(ids, mine, came, rows, qkv_out, cq_out, proj_out, co_out):
    first = ids[0] == 0
    a, b = mine[...].astype(F32), came[...].astype(F32)
    parts = (jnp.where(first, a, b), jnp.where(first, b, a))
    for c in range(2):
        to = slice(512 * c, 512 * c + 512)
        for i in range(3):
            qkv_out[i, :, to] = parts[c][:, 512 * i : 512 * i + 512]
        cq_out[:, to] = parts[c][:, LATE_ROWS - 512 : LATE_ROWS]
    for i, out in enumerate((proj_out, co_out)):
        for h in range(2):
            out[:, 512 * h : 512 * h + 512] = rows[
                16 * h : 16 * h + 16, 512 * i : 512 * i + 512
            ].astype(F32)


def late_unpack_kernel(ids, mine, came, rows):
    return call(
        late_unpack_body,
        [shape((3, 16, D), F32), shape((16, D), F32), shape((16, D), F32), shape((16, D), F32)],
        (ids, mine, came, rows),
        specs=[SMEM, WHOLE, WHOLE, WHOLE],
    )


def swap_core(value):
    return lax.ppermute(value, "core", [(0, 1), (1, 0)])


def swap_seq(value):
    return lax.ppermute(value, "xl", [(0, 1), (1, 0)])


def swap_x(value, pairs):
    return lax.ppermute(value, RING_X, [p for a, b in pairs for p in ((a, b), (b, a))])


def in_order(index, mine, other, axis):
    first = jnp.where(index == 0, mine, other)
    second = jnp.where(index == 0, other, mine)
    return jnp.stack((first, second), axis=axis)


def join(index, mine, other, axis):
    first = jnp.where(index == 0, mine, other)
    second = jnp.where(index == 0, other, mine)
    return jnp.concatenate((first, second), axis=axis)


def pick(value, index, axis):
    return jnp.where(
        index == 0, lax.index_in_dim(value, 0, axis, False), lax.index_in_dim(value, 1, axis, False)
    )


def gather_chips(block, other, xh):
    pair = in_order(xh, block, other, 0)
    full = lax.all_gather(pair, ("z", "y"), axis=0, tiled=False)
    cols = block.shape[-1]
    return full.reshape(4, 4, 2, 32, cols)


def ring(value, axis, size, step):
    return lax.ppermute(value, axis, [(i, (i + step) % size) for i in range(size)])


def exchange(value, axes):
    return lax.all_to_all(value, axes, 0, 0, tiled=True)


def zy_scatter(full):
    cols = full.shape[-1]
    part = lax.psum_scatter(full.reshape(D, cols), ("z", "y"), scatter_dimension=0, tiled=True)
    return part.reshape(2, 32, cols)


def halves_as_rows(value):
    k = value.shape[-1] // 2
    return jnp.concatenate((value[:, :k], value[:, k:]), axis=0)


def per_device(
    tokens_in,
    noise_emb,
    text_emb,
    prompt_len,
    mod_weight,
    qkv_weight,
    proj_weight,
    cq_weight,
    text_weight,
    co_weight,
    norm_gains,
    up_weight,
    down_weight,
    out_grad,
):
    core = lax.axis_index("core")
    xh = lax.axis_index("xh")
    xl = lax.axis_index("xl")
    rows = tokens_in.shape[1]

    misc = jnp.concatenate(
        (
            jnp.pad(text_emb[0], ((0, 0), (0, D - TEXT_W))),
            jnp.broadcast_to(prompt_len.astype(BF)[:, None], (8, D)),
        ),
        axis=0,
    )
    mine = jnp.concatenate((tokens_in[0], out_grad[0], misc), axis=0)
    both = in_order(core, mine, swap_core(mine), 0)
    tok = both[:, :rows].reshape(256, D)
    og = both[:, rows : 2 * rows].reshape(256, D)
    text = both[:, 2 * rows : 2 * rows + 8, :TEXT_W]
    lens = both[:, 2 * rows + 8, 0].astype(jnp.int32)

    def side(which):
        up = pick(up_weight.reshape(16, 32, 2, 64), which, 2).reshape(16, C_UP)
        qkv = pick(qkv_weight.reshape(16, 3, 2, 512), which, 2).reshape(16, C_QKV)
        cq = pick(cq_weight.reshape(16, 2, 512), which, 1)
        txt = pick(text_weight.reshape(12, 2, 2, 256), which, 2).reshape(12, C_TEXT)
        gains = jnp.pad(norm_gains, ((0, 2), (0, C_TEXT - 16)))
        return jnp.concatenate((qkv, cq, jnp.concatenate((txt, gains), axis=0), up), axis=1)

    shared = join(core, side(core), swap_core(side(1 - core)), 0)
    first = jnp.concatenate(
        (
            shared[:, : C_QKV + C_CQ + C_TEXT],
            halves_as_rows(proj_weight),
            halves_as_rows(co_weight),
        ),
        axis=1,
    )
    second = jnp.concatenate(
        (
            shared[:, C_QKV + C_CQ + C_TEXT :],
            jnp.concatenate((down_weight[:32], down_weight[32:]), axis=1),
        ),
        axis=1,
    )
    near, xl_pair, across = ((0, 3), (1, 2)), ((0, 1), (2, 3)), ((0, 2), (1, 3))
    lo, hi = TEXT_COLS
    first_far = swap_x(first, ((0, 3), (1, 2)))
    text_far = swap_x(first[:, lo:hi], ((0, 2), (1, 3)))
    second, first_far = lax.optimization_barrier((second, first_far))
    first_far = jnp.concatenate((first_far[:, :lo], text_far, first_far[:, hi:]), axis=1)
    full_one = gather_chips(first, first_far, xh)
    full_two = gather_chips(second, swap_x(second, ((0, 3), (1, 2))), xh)

    text_rows = full_one[..., TEXT_COLS[0] : TEXT_COLS[1]].transpose(0, 2, 1, 3, 4)
    text_rows = text_rows.reshape(64, 16, C_TEXT)
    text_w = text_rows[:, :12].reshape(TEXT_W, 2, 256)
    gains = text_rows[:, 12:14, :16].transpose(1, 0, 2).reshape(2, D).astype(F32)
    halves = full_one[..., TEXT_COLS[1] :].reshape(2, 2, 4, 2, 32, D)
    kept = pick(halves, core, 0)
    core_id = core.astype(jnp.int32)[None]
    y_id = lax.axis_index("y")
    ids = jnp.stack([core, 2 * xh + xl, y_id, xl]).astype(jnp.int32)
    proj_w, co_w = rows_kernel(core_id, kept, swap_core(pick(halves, 1 - core, 0)))

    noise_cols = exchange(noise_emb.reshape(64, 16), FSDP)
    mod_parts = jnp.dot(noise_cols, mod_weight, preferred_element_type=F32)
    mod_own = jnp.sum(exchange(mod_parts, FSDP), axis=0, keepdims=True)
    mod_all = in_order(core, mod_own, swap_core(mod_own), 0).reshape(2, 2, D)
    mod_scale, mod_shift = mod_all[:, 0], mod_all[:, 1]
    normed_one, queries, kv_own = qkv_kernel(tok, mod_scale, mod_shift, full_one)
    kv_far = swap_seq(kv_own)
    attended, proj_part = attend_kernel(queries, kv_own, kv_far, proj_w)
    text_own = jnp.einsum("ijt,tcn->ijcn", text, text_w, preferred_element_type=F32).astype(BF)
    text_xl = in_order(xl, text_own, swap_seq(text_own), 0)
    text_kv = join(core, pick(text_xl, core, 0), swap_core(pick(text_xl, 1 - core, 0)), 3)
    text_kv = text_kv.reshape(2, TXT, D)
    after_self, normed_two, cross_q, cross_att, co_part = cross_kernel(
        tok, proj_part, swap_core(proj_part), gains, full_one, text_kv, lens, co_w
    )
    after_cross, ff_wg, three_part, down_part = ff_kernel(
        after_self, co_part, swap_core(co_part), gains, og, full_two
    )
    ff_sc = zy_scatter(ff_wg)
    down_part = down_part.reshape(2, rows, D)
    down_own = pick(down_part, core, 0) + swap_core(pick(down_part, 1 - core, 0))
    block_out = (pick(after_cross.reshape(2, rows, D), core, 0) + down_own).astype(BF)[None]

    cross_res_grad, gain_three_grad, co_wg, cq_wg, text_sum, two_part = cross_back_kernel(
        three_part, swap_core(three_part), after_cross, og, gains, cross_att, cross_q,
        normed_two, text_kv, lens, co_w, full_one,
    )
    self_res_grad, gain_two_grad, proj_wg, dq, dkv, dkv_far = self_back_kernel(
        two_part, swap_core(two_part), after_self, cross_res_grad, gains, attended, queries,
        kv_own, kv_far, proj_w,
    )
    rows_kept, rows_sent = rows_back_kernel(core_id, proj_wg, co_wg)
    dkv_came = swap_seq(dkv_far)
    rows_came = swap_core(rows_sent)
    qkv_wg, one_part = qkv_back_kernel(dq, dkv, dkv_came, normed_one, full_one)

    text_sum = (text_sum + swap_seq(text_sum.astype(BF)).astype(F32)).astype(BF)
    text_quarters = text_sum.reshape(2, TXT, 2, 2, 256)
    text_kept = pick(text_quarters, core, 3)
    text_came = swap_core(pick(text_quarters, 1 - core, 3))
    text_kv_grad = jnp.where(core == xl, text_kept, text_came)
    text_wg = jnp.einsum("ijt,ijcn->tcn", text, text_kv_grad, preferred_element_type=F32)
    text_part = jnp.einsum("ijcn,tcn->ijt", text_kv_grad, text_w, preferred_element_type=F32)

    one_part = one_part.reshape(2, rows, D)
    one_grad = pick(one_part, core, 0) + swap_core(pick(one_part, 1 - core, 0))
    own_tokens = tokens_in.astype(F32)
    _, mod_back = jax.vjp(
        modulated_norm, own_tokens, pick(mod_scale, core, 0)[None], pick(mod_shift, core, 0)[None]
    )
    input_part, scale_grad, shift_grad = mod_back(one_grad[None])
    tokens_grad = pick(self_res_grad.reshape(2, rows, D), core, 0)[None] + input_part
    mod_grad = jnp.concatenate((scale_grad, shift_grad), axis=1)
    mod_grad = (mod_grad + swap_seq(mod_grad)).astype(BF)
    mod_grads = exchange(jnp.broadcast_to(mod_grad, (64, 2 * D)), FSDP)
    mod_wgrad = jnp.einsum("if,ic->fc", noise_cols, mod_grads, preferred_element_type=F32)
    noise_parts = jnp.einsum("ic,fc->if", mod_grads, mod_weight, preferred_element_type=F32)
    noise_grad = exchange(noise_parts, FSDP).reshape(1, D)

    gains_wg = jnp.concatenate((gain_two_grad, gain_three_grad), axis=0).astype(BF)
    gains_wg = jnp.pad(
        gains_wg.reshape(2, 64, 16).transpose(1, 0, 2), ((0, 0), (0, 2), (0, C_TEXT - 16))
    )
    text_pack = jnp.concatenate((text_wg.astype(BF).reshape(64, 12, C_TEXT), gains_wg), axis=1)
    text_pack = text_pack.reshape(4, 2, 4, 32, C_TEXT).transpose(0, 2, 1, 3, 4)
    late_wg = late_kernel(ids, text_pack, qkv_wg, cq_wg, rows_kept, rows_came)
    late_wg, ff_sc = lax.optimization_barrier((late_wg, ff_sc))
    late_sc = zy_scatter(late_wg)

    own, far = pick(ff_sc, xh, 0), pick(ff_sc, 1 - xh, 0)
    ff_g = sum_kernel(own, swap_x(own, xl_pair), swap_x(far, near), swap_x(far, across))
    up_rows = ff_g[:, :C_UP].reshape(2, 16, C_UP)
    up_wgrad, down_wgrad = ff_unpack_kernel(
        ids, pick(up_rows, core, 0), swap_core(pick(up_rows, 1 - core, 0)), ff_g[:, C_UP:]
    )

    own, far = pick(late_sc, xh, 0), pick(late_sc, 1 - xh, 0)
    late_g = late_sum_kernel(own, swap_x(own, xl_pair), swap_x(far, near), swap_x(far, across))
    late_rows = late_g[:, :LATE_ROWS].reshape(2, 16, LATE_ROWS)
    kept_rows = pick(late_rows, core, 0)
    came_rows = swap_core(pick(late_rows, 1 - core, 0))
    qkv_wgrad, cq_wgrad, proj_wgrad, co_wgrad = late_unpack_kernel(
        ids, kept_rows, came_rows, late_g[:, LATE_ROWS:]
    )
    qkv_wgrad = qkv_wgrad.transpose(1, 0, 2)
    lo, hi = C_QKV, C_QKV + C_TEXT
    text_both = in_order(core, kept_rows[:, lo:hi], came_rows[:, lo:hi], 0).astype(F32)
    text_wgrad = text_both[:, :12].reshape(2, 12, 2, 256).transpose(1, 2, 0, 3).reshape(12, 2, 512)
    gains_grad = kept_rows[12:14, lo : lo + 16].astype(F32)

    text_grad = pick(text_part, core, 0) + swap_core(pick(text_part, 1 - core, 0))
    text_grad = text_grad + swap_seq(text_grad)
    return (
        block_out,
        tokens_grad,
        noise_grad,
        text_grad[None],
        mod_wgrad,
        qkv_wgrad,
        proj_wgrad,
        cq_wgrad,
        text_wgrad,
        co_wgrad,
        gains_grad,
        up_wgrad,
        down_wgrad,
    )


def solution(mesh):
    split = Mesh(mesh.devices.reshape(SIZES), AXES)
    in_specs = (
        P(FSDP, "xl", None),
        P(FSDP, None),
        P(FSDP, None, None),
        P(FSDP),
        P(FSDP, None),
        P(FSDP, None, None),
        P(FSDP, None),
        P(FSDP, None),
        P(FSDP, None, "xl"),
        P(FSDP, None),
        P(None, FSDP),
        P(FSDP, None),
        P(FSDP, None),
        P(FSDP, "xl", None),
    )
    out_specs = (
        P(FSDP, "xl", None),
        P(FSDP, "xl", None),
        P(FSDP, None),
        P(FSDP, None, None),
        P(FSDP, None),
        P(FSDP, None, None),
        P(FSDP, None),
        P(FSDP, None),
        P(FSDP, None, "xl"),
        P(FSDP, None),
        P(None, FSDP),
        P(FSDP, None),
        P(FSDP, None),
    )
    return jax.shard_map(
        per_device, mesh=split, in_specs=in_specs, out_specs=out_specs, check_vma=False
    )
```

```python
import jax
import jax.numpy as jnp
from jax import lax
from jax.experimental import pallas as pl
from jax.experimental.pallas import tpu as pltpu
from jax.sharding import Mesh
from jax.sharding import PartitionSpec as P

HEAD_DIM = 64
EPSILON = 1e-06
HIGHEST_PREC = lax.Precision.HIGHEST
NEG_LARGE = -1e30
BF = jnp.bfloat16
F32 = jnp.float32

AXES = ("z", "xh", "y", "core", "xl")
SIZES = (4, 2, 4, 2, 2)
FSDP = ("z", "xh", "y", "core")
RING_X = ("xh", "xl")

D = 1024
FF = 4096
TEXT_W = 768
TXT = 8
CHIPS = 32

C_X = 768
C_QKV, C_CQ, C_TEXT, C_PROJ, C_CO = 1536, 512, 512, 512, 512
TEXT_COLS = (C_QKV + C_CQ, C_QKV + C_CQ + C_TEXT)
C_UP, C_DOWN = 2048, 2048


def rms_norm(tensor):
    return tensor * lax.rsqrt(jnp.mean(tensor * tensor, axis=-1, keepdims=True) + EPSILON)


def modulated_norm(tensor, scale, shift):
    return rms_norm(tensor) * (1.0 + scale[:, None, :]) + shift[:, None, :]


def mm(a, b):
    return jnp.dot(a, b, preferred_element_type=F32)


def mm_nt(a, b):
    return lax.dot_general(a, b, (((1,), (1,)), ((), ())), preferred_element_type=F32)


def mm_tn(a, b):
    return lax.dot_general(a, b, (((0,), (0,)), ((), ())), preferred_element_type=F32)


CHIP_ORDER = [(z, xh, y) for z in range(4) for xh in range(2) for y in range(4)]


def nat(ref):
    return jnp.concatenate([ref[z, y, xh] for z, xh, y in CHIP_ORDER], axis=0)


def store_nat(ref, value):
    for i, (z, xh, y) in enumerate(CHIP_ORDER):
        ref[z, y, xh] = value[32 * i : 32 * i + 32].astype(ref.dtype)


def norm_of(x):
    inv = lax.rsqrt(jnp.mean(x * x, axis=-1, keepdims=True) + EPSILON)
    return x * inv, inv


def norm_grad(unit, inv, dh_w):
    return (dh_w - unit * jnp.mean(dh_w * unit, axis=-1, keepdims=True)) * inv


def call(body, outs, ins, scratch=(), specs=None, out_specs=None, grid=None, prefetch=0):
    whole = pl.BlockSpec(memory_space=pltpu.VMEM)
    return pl.pallas_call(
        body,
        out_shape=outs,
        grid_spec=pltpu.PrefetchScalarGridSpec(
            num_scalar_prefetch=prefetch,
            grid=grid or (),
            in_specs=specs or [whole] * len(ins),
            out_specs=out_specs or [whole] * len(outs),
            scratch_shapes=list(scratch),
        ),
        compiler_params=pltpu.CompilerParams(vmem_limit_bytes=60 * 1024 * 1024),
    )(*ins)


def shape(dims, dtype):
    return jax.ShapeDtypeStruct(dims, dtype)


WHOLE = pl.BlockSpec(memory_space=pltpu.VMEM)
SMEM = pl.BlockSpec(memory_space=pltpu.SMEM)


def cols_spec(block, width=512):
    return pl.BlockSpec((4, 4, 2, 32, width), lambda i: (0, 0, 0, 0, block))


def fixed(dims):
    return pl.BlockSpec(dims, lambda i: (0,) * len(dims))


def qkv_body(tok, scale, shift, wq, wk, wv, n1_out, q_out, kv_out):
    for b in range(2):
        r = slice(128 * b, 128 * b + 128)
        unit, _ = norm_of(tok[r].astype(F32))
        n1_out[r] = (unit * (1.0 + scale[b : b + 1]) + shift[b : b + 1]).astype(BF)
    n1 = n1_out[...]
    q_out[...] = mm(n1, nat(wq)).astype(BF)
    kv_out[:, :512] = mm(n1, nat(wk)).astype(BF)
    kv_out[:, 512:] = mm(n1, nat(wv)).astype(BF)


def qkv_kernel(tok, scale, shift, full):
    return call(
        qkv_body,
        [shape((256, D), BF), shape((256, 512), BF), shape((256, D), BF)],
        (tok, scale, shift, full, full, full),
        specs=[fixed((256, D)), fixed((2, D)), fixed((2, D)), cols_spec(0), cols_spec(1), cols_spec(2)],
        out_specs=[fixed((256, D)), fixed((256, 512)), fixed((256, D))],
        grid=(1,),
    )


def head_cols(h):
    return slice(64 * h, 64 * h + 64)


def self_probs(q, k):
    scores = mm_nt(q, k) * HEAD_DIM ** (-0.5)
    e = jnp.exp(scores - jnp.max(scores, axis=-1, keepdims=True))
    return e * (1.0 / jnp.sum(e, axis=-1, keepdims=True))


def attend_body(q, kv, kv_far, proj_w, att_out, part_out):
    for b in range(2):
        r = slice(128 * b, 128 * b + 128)
        for h in range(8):
            k = jnp.concatenate((kv[r, head_cols(h)], kv_far[r, head_cols(h)]), axis=0)
            v = jnp.concatenate((kv[r, head_cols(8 + h)], kv_far[r, head_cols(8 + h)]), axis=0)
            p = self_probs(q[r, head_cols(h)], k).astype(BF)
            att_out[r, head_cols(h)] = mm(p, v).astype(BF)
    part_out[...] = mm(att_out[...], proj_w[...])


def attend_kernel(q, kv, kv_far, proj_w):
    return call(
        attend_body, [shape((256, 512), BF), shape((256, D), F32)], (q, kv, kv_far, proj_w)
    )


def spread_heads(rows8):
    tall = jnp.concatenate([rows8.astype(F32)] * 16, axis=0)
    row = lax.broadcasted_iota(jnp.int32, tall.shape, 0) // 8
    col = lax.broadcasted_iota(jnp.int32, tall.shape, 1) // 64
    return jnp.where(row == col, tall, 0.0).astype(BF)


def fold_heads(tall):
    row = lax.broadcasted_iota(jnp.int32, tall.shape, 0) // 8
    col = lax.broadcasted_iota(jnp.int32, tall.shape, 1) // 64
    kept = jnp.where(row == col, tall, 0.0)
    total = kept[0:8]
    for h in range(1, 8):
        total = total + kept[8 * h : 8 * h + 8]
    return total


def by_eights(op, x):
    lane = lax.broadcasted_iota(jnp.int32, x.shape, 1)
    for step in (1, 2, 4):
        up = pltpu.roll(x, x.shape[1] - step, 1)
        down = pltpu.roll(x, step, 1)
        x = op(x, jnp.where((lane & step) == 0, up, down))
    return x


def cross_probs(q, keys, length):
    scores = mm_nt(q, keys) * HEAD_DIM ** (-0.5)
    lane = lax.broadcasted_iota(jnp.int32, scores.shape, 1)
    scores = jnp.where((lane & 7) < length, scores, NEG_LARGE)
    e = jnp.exp(scores - by_eights(jnp.maximum, scores))
    return e * (1.0 / by_eights(jnp.add, e))


def cross_body(
    tok, part, part_far, gains, cq_w, text_kv, lens, co_w, res_out, n2_out, cq_out, att_out, part_out
):
    res_out[...] = tok[...].astype(F32) + (part[...] + part_far[...])
    unit, _ = norm_of(res_out[...])
    n2_out[...] = (unit * gains[0:1]).astype(BF)
    cq_out[...] = mm(n2_out[...], nat(cq_w)).astype(BF)
    for b in range(2):
        r = slice(128 * b, 128 * b + 128)
        keys = spread_heads(text_kv[b, :, 0:512])
        vals = spread_heads(text_kv[b, :, 512:1024])
        p = cross_probs(cq_out[r], keys, lens[b]).astype(BF)
        att_out[r] = mm(p, vals).astype(BF)
    part_out[...] = mm(att_out[...], co_w[...])


def cross_kernel(tok, part, part_far, gains, full, text_kv, lens, co_w):
    f = fixed
    return call(
        cross_body,
        [
            shape((256, D), F32),
            shape((256, D), BF),
            shape((256, 512), BF),
            shape((256, 512), BF),
            shape((256, D), F32),
        ],
        (tok, part, part_far, gains, full, text_kv, lens, co_w),
        specs=[
            f((256, D)),
            f((256, D)),
            f((256, D)),
            f((2, D)),
            cols_spec(3),
            f((2, 8, D)),
            SMEM,
            f((512, D)),
        ],
        out_specs=[f((256, D)), f((256, D)), f((256, 512)), f((256, 512)), f((256, D))],
        grid=(1,),
    )


GELU_A = 0.7978845608028654
GELU_B = 0.044715


def ff_copies(g_up, g_down, grad, sem, i):
    at = pl.ds(pl.multiple_of(i * 512, 512), 512)
    return (
        pltpu.make_async_copy(g_up.at[i], grad.at[:, :, :, :, at], sem.at[0, i]),
        pltpu.make_async_copy(g_down.at[i], grad.at[i, :, :, :, C_UP:], sem.at[1, i]),
    )


def ff_body(
    ids, res, part, part_far, gains, og, up, down, down_far, rest,
    res_out, grad_out, three_out, down_out, n3, n3_t, g_up, g_down, sem,
):
    i = pl.program_id(0)

    @pl.when(i == 0)
    def _():
        res_out[...] = res[...] + (part[...] + part_far[...])
        unit, _ = norm_of(res_out[...])
        low = (unit * gains[1:2]).astype(BF)
        n3[...] = low
        n3_t[...] = low.T

    up_w = nat(up)
    low_xh = ids[1] < 2
    own, far = down[0].reshape(256, C_X), down_far[0].reshape(256, C_X)
    left = jnp.concatenate((jnp.where(low_xh, own, far), jnp.where(low_xh, far, own)), axis=0)
    k = D - C_X
    right = jnp.concatenate(
        [
            rest[0, y, xh, :, k * h : k * h + k]
            for xh in range(2)
            for y in range(4)
            for h in range(2)
        ],
        axis=0,
    )
    down_w = jnp.concatenate((left, right), axis=1)
    pre = mm(n3[...], up_w)
    t = jnp.tanh(GELU_A * (pre + GELU_B * (pre * pre * pre)))
    act = (0.5 * pre * (1.0 + t)).astype(BF)
    slope = 0.5 * (1.0 + t) + 0.5 * pre * (1.0 - t * t) * (
        GELU_A * (1.0 + 3.0 * GELU_B * (pre * pre))
    )
    pre_grad = (mm_nt(og[...], down_w) * slope).astype(BF)
    up_wg = mm(n3_t[...], pre_grad).astype(BF)
    for j, (z, xh, y) in enumerate(CHIP_ORDER):
        g_up[i, z, y, xh] = up_wg[32 * j : 32 * j + 32]
    down_wg = mm_tn(act, og[...]).astype(BF)
    j = 0
    for xh in range(2):
        for y in range(4):
            for h in range(2):
                g_down[i, y, xh, :, D * h : D * h + D] = down_wg[32 * j : 32 * j + 32]
                j += 1
    for copy in ff_copies(g_up, g_down, grad_out, sem, i):
        copy.start()
    down_part = mm(act, down_w)
    three_part = mm_nt(pre_grad, up_w)

    @pl.when(i == 0)
    def _():
        down_out[...] = down_part
        three_out[...] = three_part

    @pl.when(i > 0)
    def _():
        down_out[...] += down_part
        three_out[...] += three_part

    @pl.when(i == 3)
    def _():
        for k in range(4):
            for copy in ff_copies(g_up, g_down, grad_out, sem, k):
                copy.wait()


def ff_kernel(ids, res, part, part_far, gains, og, down, down_far, full):
    f = fixed
    return call(
        ff_body,
        [
            shape((256, D), F32),
            shape((4, 4, 2, 32, C_UP + C_DOWN), BF),
            shape((256, D), F32),
            shape((256, D), F32),
        ],
        (ids, res, part, part_far, gains, og, full, down, down_far, full),
        scratch=[
            pltpu.VMEM((256, D), BF),
            pltpu.VMEM((D, 256), BF),
            pltpu.VMEM((4, 4, 4, 2, 32, 512), BF),
            pltpu.VMEM((4, 4, 2, 32, 2048), BF),
            pltpu.SemaphoreType.DMA((2, 4)),
        ],
        specs=[
            SMEM,
            f((256, D)),
            f((256, D)),
            f((256, D)),
            f((2, D)),
            f((256, D)),
            pl.BlockSpec((4, 4, 2, 32, 512), lambda i: (0, 0, 0, 0, i)),
            pl.BlockSpec((1, 4, 2, 32, C_X), lambda i: (i, 0, 0, 0, 0)),
            pl.BlockSpec((1, 4, 2, 32, C_X), lambda i: (i, 0, 0, 0, 0)),
            pl.BlockSpec((1, 4, 2, 32, 512), lambda i: (i, 0, 0, 0, 4)),
        ],
        out_specs=[f((256, D)), pl.BlockSpec(memory_space=pl.ANY), f((256, D)), f((256, D))],
        grid=(4,),
    )

def cross_back_body(
    part, part_far, res, og, gains, att, cq, n2, text_kv, lens, co_w, cq_w,
    grad_out, gain_out, co_out, cqw_out, text_out, two_out, ag, dq,
):
    unit, inv = norm_of(res[...])
    three = part[...] + part_far[...]
    gain_out[...] = jnp.sum(three * unit, axis=0, keepdims=True)
    grad_out[...] = og[...].astype(F32) + norm_grad(unit, inv, three * gains[1:2])
    low = grad_out[...].astype(BF)
    co_out[...] = mm_tn(att[...], low).astype(BF)
    ag[...] = mm_nt(low, co_w[...]).astype(BF)
    for b in range(2):
        r = slice(128 * b, 128 * b + 128)
        keys = spread_heads(text_kv[b, :, 0:512])
        vals = spread_heads(text_kv[b, :, 512:1024])
        p = cross_probs(cq[r], keys, lens[b])
        dp = mm_nt(ag[r], vals)
        ds = (p * (dp - by_eights(jnp.add, p * dp))).astype(BF)
        dq[r] = (mm(ds, keys) * HEAD_DIM ** (-0.5)).astype(BF)
        text_out[b, :, 0:512] = fold_heads(mm_tn(ds, cq[r])) * HEAD_DIM ** (-0.5)
        text_out[b, :, 512:1024] = fold_heads(mm_tn(p.astype(BF), ag[r]))
    store_nat(cqw_out, mm_tn(n2[...], dq[...]))
    two_out[...] = mm_nt(dq[...], nat(cq_w))


def cross_back_kernel(part, part_far, res, og, gains, att, cq, n2, text_kv, lens, co_w, full):
    f = fixed
    return call(
        cross_back_body,
        [
            shape((256, D), F32),
            shape((1, D), F32),
            shape((512, D), BF),
            shape((4, 4, 2, 32, 512), BF),
            shape((2, 8, D), F32),
            shape((256, D), F32),
        ],
        (part, part_far, res, og, gains, att, cq, n2, text_kv, lens, co_w, full),
        scratch=[pltpu.VMEM((256, 512), BF), pltpu.VMEM((256, 512), BF)],
        specs=[
            f((256, D)),
            f((256, D)),
            f((256, D)),
            f((256, D)),
            f((2, D)),
            f((256, 512)),
            f((256, 512)),
            f((256, D)),
            f((2, 8, D)),
            SMEM,
            f((512, D)),
            cols_spec(3),
        ],
        out_specs=[
            f((256, D)),
            f((1, D)),
            f((512, D)),
            f((4, 4, 2, 32, 512)),
            f((2, 8, D)),
            f((256, D)),
        ],
        grid=(1,),
    )


def self_back_body(
    part, part_far, res, res_grad, gains, att, q, kv, kv_far, proj_w,
    grad_out, gain_out, proj_out, dq_out, dkv_out, dfar_out, ag,
):
    unit, inv = norm_of(res[...])
    two = part[...] + part_far[...]
    gain_out[...] = jnp.sum(two * unit, axis=0, keepdims=True)
    grad_out[...] = res_grad[...] + norm_grad(unit, inv, two * gains[0:1])
    low = grad_out[...].astype(BF)
    proj_out[...] = mm_tn(att[...], low).astype(BF)
    ag[...] = mm_nt(low, proj_w[...]).astype(BF)
    factor = HEAD_DIM ** (-0.5)
    for b in range(2):
        r = slice(128 * b, 128 * b + 128)
        for h in range(8):
            kc, vc = head_cols(h), head_cols(8 + h)
            k = jnp.concatenate((kv[r, kc], kv_far[r, kc]), axis=0)
            v = jnp.concatenate((kv[r, vc], kv_far[r, vc]), axis=0)
            qh = q[r, kc]
            gh = ag[r, kc]
            p = self_probs(qh, k)
            dp = mm_nt(gh, v)
            ds = (p * (dp - jnp.sum(p * dp, axis=-1, keepdims=True))).astype(BF)
            dq_out[r, kc] = (mm(ds, k) * factor).astype(BF)
            dk = mm_tn(ds, qh) * factor
            dv = mm_tn(p.astype(BF), gh)
            dkv_out[r, kc] = dk[:128]
            dkv_out[r, vc] = dv[:128]
            dfar_out[r, kc] = dk[128:].astype(BF)
            dfar_out[r, vc] = dv[128:].astype(BF)


def self_back_kernel(part, part_far, res, res_grad, gains, att, q, kv, kv_far, proj_w):
    return call(
        self_back_body,
        [
            shape((256, D), F32),
            shape((1, D), F32),
            shape((512, D), BF),
            shape((256, 512), BF),
            shape((256, D), F32),
            shape((256, D), BF),
        ],
        (part, part_far, res, res_grad, gains, att, q, kv, kv_far, proj_w),
        scratch=[pltpu.VMEM((256, 512), BF)],
    )


def qkv_back_body(dq, dkv, dfar, n1, wq, wk, wv, wg_out, part_out):
    n = n1[...]
    dqv = dq[...]
    dkvv = (dkv[...] + dfar[...].astype(F32)).astype(BF)
    grads = (dqv, dkvv[:, :512], dkvv[:, 512:])
    total = None
    for i, (g, w) in enumerate(zip(grads, (wq, wk, wv))):
        wg = mm_tn(n, g).astype(BF)
        for j, (z, xh, y) in enumerate(CHIP_ORDER):
            wg_out[z, y, xh, :, 512 * i : 512 * i + 512] = wg[32 * j : 32 * j + 32]
        t = mm_nt(g, nat(w))
        total = t if total is None else total + t
    part_out[...] = total


def qkv_back_kernel(dq, dkv, dfar, n1, full):
    f = fixed
    return call(
        qkv_back_body,
        [shape((4, 4, 2, 32, 1536), BF), shape((256, D), F32)],
        (dq, dkv, dfar, n1, full, full, full),
        specs=[
            f((256, 512)),
            f((256, D)),
            f((256, D)),
            f((256, D)),
            cols_spec(0),
            cols_spec(1),
            cols_spec(2),
        ],
        out_specs=[f((4, 4, 2, 32, 1536)), f((256, D))],
        grid=(1,),
    )


def sum_body(*refs):
    total = refs[0][...].astype(F32)
    for r in refs[1:-1]:
        total = total + r[...].astype(F32)
    refs[-1][...] = total.astype(refs[-1].dtype)


def sum_kernel(*pieces):
    return call(sum_body, [shape(pieces[0].shape, BF)], pieces)[0]


LATE = C_QKV + C_TEXT + C_CQ + C_PROJ + C_CO
LATE_ROWS = LATE - C_PROJ - C_CO


def late_body(ids, text, qkv, cq, kept, came, out):
    out[:, :, :, :, :C_QKV] = qkv[...]
    at = C_QKV + C_TEXT
    out[:, :, :, :, C_QKV:at] = text[...]
    out[:, :, :, :, at : at + C_CQ] = cq[...]
    first = ids[0] == 0
    a, b = kept[...], came[...]
    out[:2, :, :, :, LATE_ROWS:] = jnp.where(first, a, b)
    out[2:, :, :, :, LATE_ROWS:] = jnp.where(first, b, a)


def late_kernel(ids, text, qkv, cq, kept, came):
    return call(
        late_body,
        [shape((4, 4, 2, 32, LATE), BF)],
        (ids, text, qkv, cq, kept, came),
        specs=[SMEM, *[WHOLE] * 5],
    )[0]


def late_sum_body(own, a, b, e, out):
    near = a[...].astype(F32) + b[...].astype(F32)
    row = lax.broadcasted_iota(jnp.int32, near.shape, 0) % 16
    col = lax.broadcasted_iota(jnp.int32, near.shape, 1)
    text = (col >= C_QKV) & (col < C_QKV + C_TEXT)
    near = jnp.where((row < 12) & text, 0.0, near)
    out[...] = (own[...].astype(F32) + e[...].astype(F32) + near).astype(BF)


def late_sum_kernel(own, a, b, e):
    return call(late_sum_body, [shape((32, LATE), BF)], (own, a, b, e))[0]


def rows_body(core, kept, came, proj_out, co_out):
    first = core[0] == 0
    i = 0
    for z in range(2):
        for xh in range(2):
            for y in range(4):
                a, b = kept[z, y, xh], came[z, y, xh]
                for bit in range(2):
                    t = jnp.where(first, a, b) if bit == 0 else jnp.where(first, b, a)
                    for out, c in ((proj_out, 0), (co_out, 512)):
                        out[16 * i : 16 * i + 16, :512] = t[:16, c : c + 512]
                        out[16 * i : 16 * i + 16, 512:] = t[16:, c : c + 512]
                    i += 1


def rows_kernel(core, kept, came):
    return call(
        rows_body,
        [shape((512, D), BF), shape((512, D), BF)],
        (core, kept, came),
        specs=[SMEM, WHOLE, WHOLE],
    )


def rows_back_body(core, proj_wg, co_wg, kept_out, sent_out):
    first = core[0] == 0
    i = 0
    for z in range(2):
        for xh in range(2):
            for y in range(4):
                t = []
                for bit in range(2):
                    r = slice(16 * i, 16 * i + 16)
                    t.append(
                        jnp.concatenate(
                            (
                                jnp.concatenate((proj_wg[r, :512], proj_wg[r, 512:]), axis=0),
                                jnp.concatenate((co_wg[r, :512], co_wg[r, 512:]), axis=0),
                            ),
                            axis=1,
                        )
                    )
                    i += 1
                kept_out[z, y, xh] = jnp.where(first, t[0], t[1])
                sent_out[z, y, xh] = jnp.where(first, t[1], t[0])


def rows_back_kernel(core, proj_wg, co_wg):
    dims = shape((2, 4, 2, 32, D), BF)
    return call(
        rows_back_body, [dims, dims], (core, proj_wg, co_wg), specs=[SMEM, WHOLE, WHOLE]
    )


def ff_unpack_body(ids, mine, came, down, up_out, down_out):
    first = ids[0] == 0
    a, b = mine[...].astype(F32), came[...].astype(F32)
    parts = (jnp.where(first, a, b), jnp.where(first, b, a))
    for i in range(32):
        for c in range(2):
            to = 128 * i + 64 * c
            up_out[:, to : to + 64] = parts[c][:, 64 * i : 64 * i + 64]
    down_out[:32] = down[:, :D].astype(F32)
    down_out[32:] = down[:, D:].astype(F32)


def ff_unpack_kernel(ids, mine, came, down):
    return call(
        ff_unpack_body,
        [shape((16, FF), F32), shape((64, D), F32)],
        (ids, mine, came, down),
        specs=[SMEM, WHOLE, WHOLE, WHOLE],
    )


def late_unpack_body(ids, mine, came, rows, qkv_out, cq_out, proj_out, co_out):
    first = ids[0] == 0
    a, b = mine[...].astype(F32), came[...].astype(F32)
    parts = (jnp.where(first, a, b), jnp.where(first, b, a))
    for c in range(2):
        to = slice(512 * c, 512 * c + 512)
        for i in range(3):
            qkv_out[i, :, to] = parts[c][:, 512 * i : 512 * i + 512]
        cq_out[:, to] = parts[c][:, LATE_ROWS - 512 : LATE_ROWS]
    for i, out in enumerate((proj_out, co_out)):
        for h in range(2):
            out[:, 512 * h : 512 * h + 512] = rows[
                16 * h : 16 * h + 16, 512 * i : 512 * i + 512
            ].astype(F32)


def late_unpack_kernel(ids, mine, came, rows):
    return call(
        late_unpack_body,
        [shape((3, 16, D), F32), shape((16, D), F32), shape((16, D), F32), shape((16, D), F32)],
        (ids, mine, came, rows),
        specs=[SMEM, WHOLE, WHOLE, WHOLE],
    )


def swap_core(value):
    return lax.ppermute(value, "core", [(0, 1), (1, 0)])


def swap_seq(value):
    return lax.ppermute(value, "xl", [(0, 1), (1, 0)])


def swap_x(value, pairs):
    return lax.ppermute(value, RING_X, [p for a, b in pairs for p in ((a, b), (b, a))])


def in_order(index, mine, other, axis):
    first = jnp.where(index == 0, mine, other)
    second = jnp.where(index == 0, other, mine)
    return jnp.stack((first, second), axis=axis)


def join(index, mine, other, axis):
    first = jnp.where(index == 0, mine, other)
    second = jnp.where(index == 0, other, mine)
    return jnp.concatenate((first, second), axis=axis)


def pick(value, index, axis):
    return jnp.where(
        index == 0, lax.index_in_dim(value, 0, axis, False), lax.index_in_dim(value, 1, axis, False)
    )


def gather_chips(pair):
    full = lax.all_gather(pair, ("z", "y"), axis=0, tiled=False)
    return full.reshape(4, 4, *pair.shape)


def ring(value, axis, size, step):
    return lax.ppermute(value, axis, [(i, (i + step) % size) for i in range(size)])


def exchange(value, axes):
    return lax.all_to_all(value, axes, 0, 0, tiled=True)


def zy_scatter(full):
    cols = full.shape[-1]
    part = lax.psum_scatter(full.reshape(D, cols), ("z", "y"), scatter_dimension=0, tiled=True)
    return part.reshape(2, 32, cols)


def halves_as_rows(value):
    k = value.shape[-1] // 2
    return jnp.concatenate((value[:, :k], value[:, k:]), axis=0)


def per_device(
    tokens_in,
    noise_emb,
    text_emb,
    prompt_len,
    mod_weight,
    qkv_weight,
    proj_weight,
    cq_weight,
    text_weight,
    co_weight,
    norm_gains,
    up_weight,
    down_weight,
    out_grad,
):
    core = lax.axis_index("core")
    xh = lax.axis_index("xh")
    xl = lax.axis_index("xl")
    rows = tokens_in.shape[1]

    misc = jnp.concatenate(
        (
            jnp.pad(text_emb[0], ((0, 0), (0, D - TEXT_W))),
            jnp.broadcast_to(prompt_len.astype(BF)[:, None], (8, D)),
        ),
        axis=0,
    )
    mine = jnp.concatenate((tokens_in[0], out_grad[0], misc), axis=0)
    both = in_order(core, mine, swap_core(mine), 0)
    tok = both[:, :rows].reshape(256, D)
    og = both[:, rows : 2 * rows].reshape(256, D)
    text = both[:, 2 * rows : 2 * rows + 8, :TEXT_W]
    lens = both[:, 2 * rows + 8, 0].astype(jnp.int32)

    def side(which):
        up = pick(up_weight.reshape(16, 32, 2, 64), which, 2).reshape(16, C_UP)
        qkv = pick(qkv_weight.reshape(16, 3, 2, 512), which, 2).reshape(16, C_QKV)
        cq = pick(cq_weight.reshape(16, 2, 512), which, 1)
        txt = pick(text_weight.reshape(12, 2, 2, 256), which, 2).reshape(12, C_TEXT)
        gains = jnp.pad(norm_gains, ((0, 2), (0, C_TEXT - 16)))
        return jnp.concatenate((qkv, cq, jnp.concatenate((txt, gains), axis=0), up), axis=1)

    shared = join(core, side(core), swap_core(side(1 - core)), 0)
    first = jnp.concatenate(
        (
            shared[:, : C_QKV + C_CQ + C_TEXT],
            halves_as_rows(proj_weight),
            halves_as_rows(co_weight),
        ),
        axis=1,
    )
    second = jnp.concatenate(
        (shared[:, C_QKV + C_CQ + C_TEXT :], down_weight[:32, C_X:], down_weight[32:, C_X:]), axis=1
    )
    near, xl_pair, across = ((0, 3), (1, 2)), ((0, 1), (2, 3)), ((0, 2), (1, 3))
    lo, hi = TEXT_COLS
    first_far = swap_x(first, ((0, 3), (1, 2)))
    text_far = swap_x(first[:, lo:hi], ((0, 2), (1, 3)))
    second, first_far = lax.optimization_barrier((second, first_far))
    first_far = jnp.concatenate((first_far[:, :lo], text_far, first_far[:, hi:]), axis=1)
    down_halves = down_weight.reshape(2, 32, D)
    first_pair = jnp.concatenate(
        (in_order(xh, first, first_far, 0), down_halves[..., :C_X]), axis=2
    )
    full_one = gather_chips(first_pair)
    full_two = gather_chips(in_order(xh, second, swap_x(second, near), 0))
    full_one, down_own = lax.optimization_barrier((full_one, full_one[..., -C_X:]))
    down_far = swap_x(down_own, near)

    text_rows = full_one[..., lo:hi].transpose(0, 2, 1, 3, 4)
    text_rows = text_rows.reshape(64, 16, C_TEXT)
    text_w = text_rows[:, :12].reshape(TEXT_W, 2, 256)
    gains = text_rows[:, 12:14, :16].transpose(1, 0, 2).reshape(2, D).astype(F32)
    core_id = core.astype(jnp.int32)[None]
    y_id = lax.axis_index("y")
    ids = jnp.stack([core, 2 * xh + xl, y_id, xl]).astype(jnp.int32)

    noise_cols = exchange(noise_emb.reshape(64, 16), FSDP)
    mod_parts = jnp.dot(noise_cols, mod_weight, preferred_element_type=F32)
    mod_own = jnp.sum(exchange(mod_parts, FSDP), axis=0, keepdims=True)
    mod_all = in_order(core, mod_own, swap_core(mod_own), 0).reshape(2, 2, D)
    mod_scale, mod_shift = mod_all[:, 0], mod_all[:, 1]
    normed_one, queries, kv_own = qkv_kernel(tok, mod_scale, mod_shift, full_one)
    kv_far = swap_seq(kv_own)
    later, kv_own = lax.optimization_barrier((full_one, kv_own))
    halves = later[..., hi : hi + 2 * 512].reshape(2, 2, 4, 2, 32, D)
    kept = pick(halves, core, 0)
    proj_w, co_w = rows_kernel(core_id, kept, swap_core(pick(halves, 1 - core, 0)))
    attended, proj_part = attend_kernel(queries, kv_own, kv_far, proj_w)
    proj_part, down_far = lax.optimization_barrier((proj_part, down_far))
    text_own = jnp.einsum("ijt,tcn->ijcn", text, text_w, preferred_element_type=F32).astype(BF)
    text_xl = in_order(xl, text_own, swap_seq(text_own), 0)
    text_kv = join(core, pick(text_xl, core, 0), swap_core(pick(text_xl, 1 - core, 0)), 3)
    text_kv = text_kv.reshape(2, TXT, D)
    after_self, normed_two, cross_q, cross_att, co_part = cross_kernel(
        tok, proj_part, swap_core(proj_part), gains, full_one, text_kv, lens, co_w
    )
    after_cross, ff_wg, three_part, down_part = ff_kernel(
        ids, after_self, co_part, swap_core(co_part), gains, og, down_own, down_far, full_two
    )
    ff_sc = zy_scatter(ff_wg)
    down_part = down_part.reshape(2, rows, D)
    down_own = pick(down_part, core, 0) + swap_core(pick(down_part, 1 - core, 0))
    block_out = (pick(after_cross.reshape(2, rows, D), core, 0) + down_own).astype(BF)[None]

    cross_res_grad, gain_three_grad, co_wg, cq_wg, text_sum, two_part = cross_back_kernel(
        three_part, swap_core(three_part), after_cross, og, gains, cross_att, cross_q,
        normed_two, text_kv, lens, co_w, full_one,
    )
    self_res_grad, gain_two_grad, proj_wg, dq, dkv, dkv_far = self_back_kernel(
        two_part, swap_core(two_part), after_self, cross_res_grad, gains, attended, queries,
        kv_own, kv_far, proj_w,
    )
    rows_kept, rows_sent = rows_back_kernel(core_id, proj_wg, co_wg)
    dkv_came = swap_seq(dkv_far)
    rows_came = swap_core(rows_sent)
    qkv_wg, one_part = qkv_back_kernel(dq, dkv, dkv_came, normed_one, full_one)

    text_sum = (text_sum + swap_seq(text_sum.astype(BF)).astype(F32)).astype(BF)
    text_quarters = text_sum.reshape(2, TXT, 2, 2, 256)
    text_kept = pick(text_quarters, core, 3)
    text_came = swap_core(pick(text_quarters, 1 - core, 3))
    text_kv_grad = jnp.where(core == xl, text_kept, text_came)
    text_wg = jnp.einsum("ijt,ijcn->tcn", text, text_kv_grad, preferred_element_type=F32)
    text_part = jnp.einsum("ijcn,tcn->ijt", text_kv_grad, text_w, preferred_element_type=F32)

    one_part = one_part.reshape(2, rows, D)
    one_grad = pick(one_part, core, 0) + swap_core(pick(one_part, 1 - core, 0))
    own_tokens = tokens_in.astype(F32)
    _, mod_back = jax.vjp(
        modulated_norm, own_tokens, pick(mod_scale, core, 0)[None], pick(mod_shift, core, 0)[None]
    )
    input_part, scale_grad, shift_grad = mod_back(one_grad[None])
    tokens_grad = pick(self_res_grad.reshape(2, rows, D), core, 0)[None] + input_part
    mod_grad = jnp.concatenate((scale_grad, shift_grad), axis=1)
    mod_grad = (mod_grad + swap_seq(mod_grad)).astype(BF)
    mod_grads = exchange(jnp.broadcast_to(mod_grad, (64, 2 * D)), FSDP)
    mod_wgrad = jnp.einsum("if,ic->fc", noise_cols, mod_grads, preferred_element_type=F32)
    noise_parts = jnp.einsum("ic,fc->if", mod_grads, mod_weight, preferred_element_type=F32)
    noise_grad = exchange(noise_parts, FSDP).reshape(1, D)

    gains_wg = jnp.concatenate((gain_two_grad, gain_three_grad), axis=0).astype(BF)
    gains_wg = jnp.pad(
        gains_wg.reshape(2, 64, 16).transpose(1, 0, 2), ((0, 0), (0, 2), (0, C_TEXT - 16))
    )
    text_pack = jnp.concatenate((text_wg.astype(BF).reshape(64, 12, C_TEXT), gains_wg), axis=1)
    text_pack = text_pack.reshape(4, 2, 4, 32, C_TEXT).transpose(0, 2, 1, 3, 4)
    late_wg = late_kernel(ids, text_pack, qkv_wg, cq_wg, rows_kept, rows_came)
    late_wg, ff_sc = lax.optimization_barrier((late_wg, ff_sc))
    late_sc = zy_scatter(late_wg)

    own, far = pick(ff_sc, xh, 0), pick(ff_sc, 1 - xh, 0)
    ff_g = sum_kernel(own, swap_x(own, xl_pair), swap_x(far, near), swap_x(far, across))
    up_rows = ff_g[:, :C_UP].reshape(2, 16, C_UP)
    up_wgrad, down_wgrad = ff_unpack_kernel(
        ids, pick(up_rows, core, 0), swap_core(pick(up_rows, 1 - core, 0)), ff_g[:, C_UP:]
    )

    own, far = pick(late_sc, xh, 0), pick(late_sc, 1 - xh, 0)
    late_g = late_sum_kernel(own, swap_x(own, xl_pair), swap_x(far, near), swap_x(far, across))
    late_rows = late_g[:, :LATE_ROWS].reshape(2, 16, LATE_ROWS)
    kept_rows = pick(late_rows, core, 0)
    came_rows = swap_core(pick(late_rows, 1 - core, 0))
    qkv_wgrad, cq_wgrad, proj_wgrad, co_wgrad = late_unpack_kernel(
        ids, kept_rows, came_rows, late_g[:, LATE_ROWS:]
    )
    qkv_wgrad = qkv_wgrad.transpose(1, 0, 2)
    lo, hi = C_QKV, C_QKV + C_TEXT
    text_both = in_order(core, kept_rows[:, lo:hi], came_rows[:, lo:hi], 0).astype(F32)
    text_wgrad = text_both[:, :12].reshape(2, 12, 2, 256).transpose(1, 2, 0, 3).reshape(12, 2, 512)
    gains_grad = kept_rows[12:14, lo : lo + 16].astype(F32)

    text_grad = pick(text_part, core, 0) + swap_core(pick(text_part, 1 - core, 0))
    text_grad = text_grad + swap_seq(text_grad)
    return (
        block_out,
        tokens_grad,
        noise_grad,
        text_grad[None],
        mod_wgrad,
        qkv_wgrad,
        proj_wgrad,
        cq_wgrad,
        text_wgrad,
        co_wgrad,
        gains_grad,
        up_wgrad,
        down_wgrad,
    )


def solution(mesh):
    split = Mesh(mesh.devices.reshape(SIZES), AXES)
    in_specs = (
        P(FSDP, "xl", None),
        P(FSDP, None),
        P(FSDP, None, None),
        P(FSDP),
        P(FSDP, None),
        P(FSDP, None, None),
        P(FSDP, None),
        P(FSDP, None),
        P(FSDP, None, "xl"),
        P(FSDP, None),
        P(None, FSDP),
        P(FSDP, None),
        P(FSDP, None),
        P(FSDP, "xl", None),
    )
    out_specs = (
        P(FSDP, "xl", None),
        P(FSDP, "xl", None),
        P(FSDP, None),
        P(FSDP, None, None),
        P(FSDP, None),
        P(FSDP, None, None),
        P(FSDP, None),
        P(FSDP, None),
        P(FSDP, None, "xl"),
        P(FSDP, None),
        P(None, FSDP),
        P(FSDP, None),
        P(FSDP, None),
    )
    return jax.shard_map(
        per_device, mesh=split, in_specs=in_specs, out_specs=out_specs, check_vma=False
    )
```

```python
import jax
import jax.numpy as jnp
from jax import lax
from jax.experimental import pallas as pl
from jax.experimental.pallas import tpu as pltpu
from jax.sharding import Mesh
from jax.sharding import PartitionSpec as P

HEAD_DIM = 64
EPSILON = 1e-06
HIGHEST_PREC = lax.Precision.HIGHEST
NEG_LARGE = -1e30
BF = jnp.bfloat16
F32 = jnp.float32

AXES = ("z", "xh", "y", "core", "xl")
SIZES = (4, 2, 4, 2, 2)
FSDP = ("z", "xh", "y", "core")
RING_X = ("xh", "xl")

D = 1024
FF = 4096
TEXT_W = 768
TXT = 8
CHIPS = 32

C_X = 768
C_QKV, C_CQ, C_TEXT, C_PROJ, C_CO = 1536, 512, 512, 512, 512
TEXT_COLS = (C_QKV + C_CQ, C_QKV + C_CQ + C_TEXT)
C_UP, C_DOWN = 2048, 2048


def rms_norm(tensor):
    return tensor * lax.rsqrt(jnp.mean(tensor * tensor, axis=-1, keepdims=True) + EPSILON)


def modulated_norm(tensor, scale, shift):
    return rms_norm(tensor) * (1.0 + scale[:, None, :]) + shift[:, None, :]


def mm(a, b):
    return jnp.dot(a, b, preferred_element_type=F32)


def mm_nt(a, b):
    return lax.dot_general(a, b, (((1,), (1,)), ((), ())), preferred_element_type=F32)


def mm_tn(a, b):
    return lax.dot_general(a, b, (((0,), (0,)), ((), ())), preferred_element_type=F32)


CHIP_ORDER = [(z, xh, y) for z in range(4) for xh in range(2) for y in range(4)]


def nat(ref):
    return jnp.concatenate([ref[z, y, xh] for z, xh, y in CHIP_ORDER], axis=0)


def store_nat(ref, value):
    for i, (z, xh, y) in enumerate(CHIP_ORDER):
        ref[z, y, xh] = value[32 * i : 32 * i + 32].astype(ref.dtype)


def norm_of(x):
    inv = lax.rsqrt(jnp.mean(x * x, axis=-1, keepdims=True) + EPSILON)
    return x * inv, inv


def norm_grad(unit, inv, dh_w):
    return (dh_w - unit * jnp.mean(dh_w * unit, axis=-1, keepdims=True)) * inv


def call(body, outs, ins, scratch=(), specs=None, out_specs=None, grid=None, prefetch=0):
    whole = pl.BlockSpec(memory_space=pltpu.VMEM)
    return pl.pallas_call(
        body,
        out_shape=outs,
        grid_spec=pltpu.PrefetchScalarGridSpec(
            num_scalar_prefetch=prefetch,
            grid=grid or (),
            in_specs=specs or [whole] * len(ins),
            out_specs=out_specs or [whole] * len(outs),
            scratch_shapes=list(scratch),
        ),
        compiler_params=pltpu.CompilerParams(vmem_limit_bytes=60 * 1024 * 1024),
    )(*ins)


def shape(dims, dtype):
    return jax.ShapeDtypeStruct(dims, dtype)


WHOLE = pl.BlockSpec(memory_space=pltpu.VMEM)
SMEM = pl.BlockSpec(memory_space=pltpu.SMEM)


def cols_spec(block, width=512):
    return pl.BlockSpec((4, 4, 2, 32, width), lambda i: (0, 0, 0, 0, block))


def fixed(dims):
    return pl.BlockSpec(dims, lambda i: (0,) * len(dims))


def qkv_body(tok, scale, shift, wq, wk, wv, n1_out, q_out, kv_out):
    for b in range(2):
        r = slice(128 * b, 128 * b + 128)
        unit, _ = norm_of(tok[r].astype(F32))
        n1_out[r] = (unit * (1.0 + scale[b : b + 1]) + shift[b : b + 1]).astype(BF)
    n1 = n1_out[...]
    q_out[...] = mm(n1, nat(wq)).astype(BF)
    kv_out[:, :512] = mm(n1, nat(wk)).astype(BF)
    kv_out[:, 512:] = mm(n1, nat(wv)).astype(BF)


def qkv_kernel(tok, scale, shift, full):
    return call(
        qkv_body,
        [shape((256, D), BF), shape((256, 512), BF), shape((256, D), BF)],
        (tok, scale, shift, full, full, full),
        specs=[fixed((256, D)), fixed((2, D)), fixed((2, D)), cols_spec(0), cols_spec(1), cols_spec(2)],
        out_specs=[fixed((256, D)), fixed((256, 512)), fixed((256, D))],
        grid=(1,),
    )


def head_cols(h):
    return slice(64 * h, 64 * h + 64)


def self_probs(q, k):
    scores = mm_nt(q, k) * HEAD_DIM ** (-0.5)
    e = jnp.exp(scores - jnp.max(scores, axis=-1, keepdims=True))
    return e * (1.0 / jnp.sum(e, axis=-1, keepdims=True))


def attend_body(q, kv, kv_far, proj_w, att_out, part_out):
    for b in range(2):
        r = slice(128 * b, 128 * b + 128)
        for h in range(8):
            k = jnp.concatenate((kv[r, head_cols(h)], kv_far[r, head_cols(h)]), axis=0)
            v = jnp.concatenate((kv[r, head_cols(8 + h)], kv_far[r, head_cols(8 + h)]), axis=0)
            p = self_probs(q[r, head_cols(h)], k).astype(BF)
            att_out[r, head_cols(h)] = mm(p, v).astype(BF)
    part_out[...] = mm(att_out[...], proj_w[...])


def attend_kernel(q, kv, kv_far, proj_w):
    return call(
        attend_body, [shape((256, 512), BF), shape((256, D), F32)], (q, kv, kv_far, proj_w)
    )


def spread_heads(rows8):
    tall = jnp.concatenate([rows8.astype(F32)] * 16, axis=0)
    row = lax.broadcasted_iota(jnp.int32, tall.shape, 0) // 8
    col = lax.broadcasted_iota(jnp.int32, tall.shape, 1) // 64
    return jnp.where(row == col, tall, 0.0).astype(BF)


def fold_heads(tall):
    row = lax.broadcasted_iota(jnp.int32, tall.shape, 0) // 8
    col = lax.broadcasted_iota(jnp.int32, tall.shape, 1) // 64
    kept = jnp.where(row == col, tall, 0.0)
    total = kept[0:8]
    for h in range(1, 8):
        total = total + kept[8 * h : 8 * h + 8]
    return total


def by_eights(op, x):
    lane = lax.broadcasted_iota(jnp.int32, x.shape, 1)
    for step in (1, 2, 4):
        up = pltpu.roll(x, x.shape[1] - step, 1)
        down = pltpu.roll(x, step, 1)
        x = op(x, jnp.where((lane & step) == 0, up, down))
    return x


def cross_probs(q, keys, length):
    scores = mm_nt(q, keys) * HEAD_DIM ** (-0.5)
    lane = lax.broadcasted_iota(jnp.int32, scores.shape, 1)
    scores = jnp.where((lane & 7) < length, scores, NEG_LARGE)
    e = jnp.exp(scores - by_eights(jnp.maximum, scores))
    return e * (1.0 / by_eights(jnp.add, e))


def cross_body(
    tok, part, part_far, gains, cq_w, text_kv, lens, co_w, res_out, n2_out, cq_out, att_out, part_out
):
    res_out[...] = tok[...].astype(F32) + (part[...] + part_far[...])
    unit, _ = norm_of(res_out[...])
    n2_out[...] = (unit * gains[0:1]).astype(BF)
    cq_out[...] = mm(n2_out[...], nat(cq_w)).astype(BF)
    for b in range(2):
        r = slice(128 * b, 128 * b + 128)
        keys = spread_heads(text_kv[b, :, 0:512])
        vals = spread_heads(text_kv[b, :, 512:1024])
        p = cross_probs(cq_out[r], keys, lens[b]).astype(BF)
        att_out[r] = mm(p, vals).astype(BF)
    part_out[...] = mm(att_out[...], co_w[...])


def cross_kernel(tok, part, part_far, gains, full, text_kv, lens, co_w):
    f = fixed
    return call(
        cross_body,
        [
            shape((256, D), F32),
            shape((256, D), BF),
            shape((256, 512), BF),
            shape((256, 512), BF),
            shape((256, D), F32),
        ],
        (tok, part, part_far, gains, full, text_kv, lens, co_w),
        specs=[
            f((256, D)),
            f((256, D)),
            f((256, D)),
            f((2, D)),
            cols_spec(3),
            f((2, 8, D)),
            SMEM,
            f((512, D)),
        ],
        out_specs=[f((256, D)), f((256, D)), f((256, 512)), f((256, 512)), f((256, D))],
        grid=(1,),
    )


GELU_A = 0.7978845608028654
GELU_B = 0.044715


def ff_copies(g_up, g_down, grad, sem, i):
    at = pl.ds(pl.multiple_of(i * 512, 512), 512)
    return (
        pltpu.make_async_copy(g_up.at[i], grad.at[:, :, :, :, at], sem.at[0, i]),
        pltpu.make_async_copy(g_down.at[i], grad.at[i, :, :, :, C_UP:], sem.at[1, i]),
    )


def ff_body(
    ids, res, part, part_far, gains, og, up, down, down_far, rest,
    res_out, grad_out, three_out, down_out, n3, n3_t, g_up, g_down, sem,
):
    i = pl.program_id(0)

    @pl.when(i == 0)
    def _():
        res_out[...] = res[...] + (part[...] + part_far[...])
        unit, _ = norm_of(res_out[...])
        low = (unit * gains[1:2]).astype(BF)
        n3[...] = low
        n3_t[...] = low.T

    up_w = nat(up)
    low_xh = ids[1] < 2
    own, far = down[0].reshape(256, C_X), down_far[0].reshape(256, C_X)
    left = jnp.concatenate((jnp.where(low_xh, own, far), jnp.where(low_xh, far, own)), axis=0)
    k = D - C_X
    right = jnp.concatenate(
        [
            rest[0, y, xh, :, k * h : k * h + k]
            for xh in range(2)
            for y in range(4)
            for h in range(2)
        ],
        axis=0,
    )
    down_w = jnp.concatenate((left, right), axis=1)
    pre = mm(n3[...], up_w)
    t = jnp.tanh(GELU_A * (pre + GELU_B * (pre * pre * pre)))
    act = (0.5 * pre * (1.0 + t)).astype(BF)
    slope = 0.5 * (1.0 + t) + 0.5 * pre * (1.0 - t * t) * (
        GELU_A * (1.0 + 3.0 * GELU_B * (pre * pre))
    )
    pre_grad = (mm_nt(og[...], down_w) * slope).astype(BF)
    up_wg = mm(n3_t[...], pre_grad).astype(BF)
    for j, (z, xh, y) in enumerate(CHIP_ORDER):
        g_up[i, z, y, xh] = up_wg[32 * j : 32 * j + 32]
    down_wg = mm_tn(act, og[...]).astype(BF)
    j = 0
    for xh in range(2):
        for y in range(4):
            for h in range(2):
                g_down[i, y, xh, :, D * h : D * h + D] = down_wg[32 * j : 32 * j + 32]
                j += 1
    for copy in ff_copies(g_up, g_down, grad_out, sem, i):
        copy.start()
    down_part = mm(act, down_w)
    three_part = mm_nt(pre_grad, up_w)

    @pl.when(i == 0)
    def _():
        down_out[...] = down_part
        three_out[...] = three_part

    @pl.when(i > 0)
    def _():
        down_out[...] += down_part
        three_out[...] += three_part

    @pl.when(i == 3)
    def _():
        for k in range(4):
            for copy in ff_copies(g_up, g_down, grad_out, sem, k):
                copy.wait()


def ff_kernel(ids, res, part, part_far, gains, og, down, down_far, full):
    f = fixed
    return call(
        ff_body,
        [
            shape((256, D), F32),
            shape((4, 4, 2, 32, C_UP + C_DOWN), BF),
            shape((256, D), F32),
            shape((256, D), F32),
        ],
        (ids, res, part, part_far, gains, og, full, down, down_far, full),
        scratch=[
            pltpu.VMEM((256, D), BF),
            pltpu.VMEM((D, 256), BF),
            pltpu.VMEM((4, 4, 4, 2, 32, 512), BF),
            pltpu.VMEM((4, 4, 2, 32, 2048), BF),
            pltpu.SemaphoreType.DMA((2, 4)),
        ],
        specs=[
            SMEM,
            f((256, D)),
            f((256, D)),
            f((256, D)),
            f((2, D)),
            f((256, D)),
            pl.BlockSpec((4, 4, 2, 32, 512), lambda i: (0, 0, 0, 0, i)),
            pl.BlockSpec((1, 4, 2, 32, C_X), lambda i: (i, 0, 0, 0, 0)),
            pl.BlockSpec((1, 4, 2, 32, C_X), lambda i: (i, 0, 0, 0, 0)),
            pl.BlockSpec((1, 4, 2, 32, 512), lambda i: (i, 0, 0, 0, 4)),
        ],
        out_specs=[f((256, D)), pl.BlockSpec(memory_space=pl.ANY), f((256, D)), f((256, D))],
        grid=(4,),
    )

def cross_back_body(
    part, part_far, res, og, gains, att, cq, n2, text_kv, lens, co_w, cq_w,
    grad_out, gain_out, co_out, cqw_out, text_out, two_out, ag, dq,
):
    unit, inv = norm_of(res[...])
    three = part[...] + part_far[...]
    gain_out[...] = jnp.sum(three * unit, axis=0, keepdims=True)
    grad_out[...] = og[...].astype(F32) + norm_grad(unit, inv, three * gains[1:2])
    low = grad_out[...].astype(BF)
    co_out[...] = mm_tn(att[...], low).astype(BF)
    ag[...] = mm_nt(low, co_w[...]).astype(BF)
    for b in range(2):
        r = slice(128 * b, 128 * b + 128)
        keys = spread_heads(text_kv[b, :, 0:512])
        vals = spread_heads(text_kv[b, :, 512:1024])
        p = cross_probs(cq[r], keys, lens[b])
        dp = mm_nt(ag[r], vals)
        ds = (p * (dp - by_eights(jnp.add, p * dp))).astype(BF)
        dq[r] = (mm(ds, keys) * HEAD_DIM ** (-0.5)).astype(BF)
        text_out[b, :, 0:512] = fold_heads(mm_tn(ds, cq[r])) * HEAD_DIM ** (-0.5)
        text_out[b, :, 512:1024] = fold_heads(mm_tn(p.astype(BF), ag[r]))
    store_nat(cqw_out, mm_tn(n2[...], dq[...]))
    two_out[...] = mm_nt(dq[...], nat(cq_w))


def cross_back_kernel(part, part_far, res, og, gains, att, cq, n2, text_kv, lens, co_w, full):
    f = fixed
    return call(
        cross_back_body,
        [
            shape((256, D), F32),
            shape((1, D), F32),
            shape((512, D), BF),
            shape((4, 4, 2, 32, 512), BF),
            shape((2, 8, D), F32),
            shape((256, D), F32),
        ],
        (part, part_far, res, og, gains, att, cq, n2, text_kv, lens, co_w, full),
        scratch=[pltpu.VMEM((256, 512), BF), pltpu.VMEM((256, 512), BF)],
        specs=[
            f((256, D)),
            f((256, D)),
            f((256, D)),
            f((256, D)),
            f((2, D)),
            f((256, 512)),
            f((256, 512)),
            f((256, D)),
            f((2, 8, D)),
            SMEM,
            f((512, D)),
            cols_spec(3),
        ],
        out_specs=[
            f((256, D)),
            f((1, D)),
            f((512, D)),
            f((4, 4, 2, 32, 512)),
            f((2, 8, D)),
            f((256, D)),
        ],
        grid=(1,),
    )


def self_back_body(
    part, part_far, res, res_grad, gains, att, q, kv, kv_far, proj_w,
    grad_out, gain_out, proj_out, dq_out, dkv_out, dfar_out, ag,
):
    unit, inv = norm_of(res[...])
    two = part[...] + part_far[...]
    gain_out[...] = jnp.sum(two * unit, axis=0, keepdims=True)
    grad_out[...] = res_grad[...] + norm_grad(unit, inv, two * gains[0:1])
    low = grad_out[...].astype(BF)
    proj_out[...] = mm_tn(att[...], low).astype(BF)
    ag[...] = mm_nt(low, proj_w[...]).astype(BF)
    factor = HEAD_DIM ** (-0.5)
    for b in range(2):
        r = slice(128 * b, 128 * b + 128)
        for h in range(8):
            kc, vc = head_cols(h), head_cols(8 + h)
            k = jnp.concatenate((kv[r, kc], kv_far[r, kc]), axis=0)
            v = jnp.concatenate((kv[r, vc], kv_far[r, vc]), axis=0)
            qh = q[r, kc]
            gh = ag[r, kc]
            p = self_probs(qh, k)
            dp = mm_nt(gh, v)
            ds = (p * (dp - jnp.sum(p * dp, axis=-1, keepdims=True))).astype(BF)
            dq_out[r, kc] = (mm(ds, k) * factor).astype(BF)
            dk = mm_tn(ds, qh) * factor
            dv = mm_tn(p.astype(BF), gh)
            dkv_out[r, kc] = dk[:128]
            dkv_out[r, vc] = dv[:128]
            dfar_out[r, kc] = dk[128:].astype(BF)
            dfar_out[r, vc] = dv[128:].astype(BF)


def self_back_kernel(part, part_far, res, res_grad, gains, att, q, kv, kv_far, proj_w):
    return call(
        self_back_body,
        [
            shape((256, D), F32),
            shape((1, D), F32),
            shape((512, D), BF),
            shape((256, 512), BF),
            shape((256, D), F32),
            shape((256, D), BF),
        ],
        (part, part_far, res, res_grad, gains, att, q, kv, kv_far, proj_w),
        scratch=[pltpu.VMEM((256, 512), BF)],
    )


def qkv_back_body(dq, dkv, dfar, n1, wq, wk, wv, wg_out, part_out):
    n = n1[...]
    dqv = dq[...]
    dkvv = (dkv[...] + dfar[...].astype(F32)).astype(BF)
    grads = (dqv, dkvv[:, :512], dkvv[:, 512:])
    total = None
    for i, (g, w) in enumerate(zip(grads, (wq, wk, wv))):
        wg = mm_tn(n, g).astype(BF)
        for j, (z, xh, y) in enumerate(CHIP_ORDER):
            wg_out[z, y, xh, :, 512 * i : 512 * i + 512] = wg[32 * j : 32 * j + 32]
        t = mm_nt(g, nat(w))
        total = t if total is None else total + t
    part_out[...] = total


def qkv_back_kernel(dq, dkv, dfar, n1, full):
    f = fixed
    return call(
        qkv_back_body,
        [shape((4, 4, 2, 32, 1536), BF), shape((256, D), F32)],
        (dq, dkv, dfar, n1, full, full, full),
        specs=[
            f((256, 512)),
            f((256, D)),
            f((256, D)),
            f((256, D)),
            cols_spec(0),
            cols_spec(1),
            cols_spec(2),
        ],
        out_specs=[f((4, 4, 2, 32, 1536)), f((256, D))],
        grid=(1,),
    )


def sum_body(*refs):
    total = refs[0][...].astype(F32)
    for r in refs[1:-1]:
        total = total + r[...].astype(F32)
    refs[-1][...] = total.astype(refs[-1].dtype)


def sum_kernel(*pieces):
    return call(sum_body, [shape(pieces[0].shape, BF)], pieces)[0]


LATE = C_QKV + C_TEXT + C_CQ + C_PROJ + C_CO
LATE_ROWS = LATE - C_PROJ - C_CO


def late_body(ids, text, qkv, cq, kept, came, out):
    out[:, :, :, :, :C_QKV] = qkv[...]
    at = C_QKV + C_TEXT
    out[:, :, :, :, C_QKV:at] = text[...]
    out[:, :, :, :, at : at + C_CQ] = cq[...]
    first = ids[0] == 0
    a, b = kept[...], came[...]
    out[:2, :, :, :, LATE_ROWS:] = jnp.where(first, a, b)
    out[2:, :, :, :, LATE_ROWS:] = jnp.where(first, b, a)


def late_kernel(ids, text, qkv, cq, kept, came):
    return call(
        late_body,
        [shape((4, 4, 2, 32, LATE), BF)],
        (ids, text, qkv, cq, kept, came),
        specs=[SMEM, *[WHOLE] * 5],
    )[0]


def late_sum_body(own, a, b, e, out):
    near = a[...].astype(F32) + b[...].astype(F32)
    row = lax.broadcasted_iota(jnp.int32, near.shape, 0) % 16
    col = lax.broadcasted_iota(jnp.int32, near.shape, 1)
    text = (col >= C_QKV) & (col < C_QKV + C_TEXT)
    near = jnp.where((row < 12) & text, 0.0, near)
    out[...] = (own[...].astype(F32) + e[...].astype(F32) + near).astype(BF)


def late_sum_kernel(own, a, b, e):
    return call(late_sum_body, [shape((32, LATE), BF)], (own, a, b, e))[0]


def rows_body(core, kept, came, proj_out, co_out):
    first = core[0] == 0
    i = 0
    for z in range(2):
        for xh in range(2):
            for y in range(4):
                a, b = kept[z, y, xh], came[z, y, xh]
                for bit in range(2):
                    t = jnp.where(first, a, b) if bit == 0 else jnp.where(first, b, a)
                    for out, c in ((proj_out, 0), (co_out, 512)):
                        out[16 * i : 16 * i + 16, :512] = t[:16, c : c + 512]
                        out[16 * i : 16 * i + 16, 512:] = t[16:, c : c + 512]
                    i += 1


def rows_kernel(core, kept, came):
    return call(
        rows_body,
        [shape((512, D), BF), shape((512, D), BF)],
        (core, kept, came),
        specs=[SMEM, WHOLE, WHOLE],
    )


def rows_back_body(core, proj_wg, co_wg, kept_out, sent_out):
    first = core[0] == 0
    i = 0
    for z in range(2):
        for xh in range(2):
            for y in range(4):
                t = []
                for bit in range(2):
                    r = slice(16 * i, 16 * i + 16)
                    t.append(
                        jnp.concatenate(
                            (
                                jnp.concatenate((proj_wg[r, :512], proj_wg[r, 512:]), axis=0),
                                jnp.concatenate((co_wg[r, :512], co_wg[r, 512:]), axis=0),
                            ),
                            axis=1,
                        )
                    )
                    i += 1
                kept_out[z, y, xh] = jnp.where(first, t[0], t[1])
                sent_out[z, y, xh] = jnp.where(first, t[1], t[0])


def rows_back_kernel(core, proj_wg, co_wg):
    dims = shape((2, 4, 2, 32, D), BF)
    return call(
        rows_back_body, [dims, dims], (core, proj_wg, co_wg), specs=[SMEM, WHOLE, WHOLE]
    )


def ff_unpack_body(ids, mine, came, down, up_out, down_out):
    first = ids[0] == 0
    a, b = mine[...].astype(F32), came[...].astype(F32)
    parts = (jnp.where(first, a, b), jnp.where(first, b, a))
    for i in range(32):
        for c in range(2):
            to = 128 * i + 64 * c
            up_out[:, to : to + 64] = parts[c][:, 64 * i : 64 * i + 64]
    down_out[:32] = down[:, :D].astype(F32)
    down_out[32:] = down[:, D:].astype(F32)


def ff_unpack_kernel(ids, mine, came, down):
    return call(
        ff_unpack_body,
        [shape((16, FF), F32), shape((64, D), F32)],
        (ids, mine, came, down),
        specs=[SMEM, WHOLE, WHOLE, WHOLE],
    )


def late_unpack_body(ids, mine, came, rows, qkv_out, cq_out, proj_out, co_out):
    first = ids[0] == 0
    a, b = mine[...].astype(F32), came[...].astype(F32)
    parts = (jnp.where(first, a, b), jnp.where(first, b, a))
    for c in range(2):
        to = slice(512 * c, 512 * c + 512)
        for i in range(3):
            qkv_out[i, :, to] = parts[c][:, 512 * i : 512 * i + 512]
        cq_out[:, to] = parts[c][:, LATE_ROWS - 512 : LATE_ROWS]
    for i, out in enumerate((proj_out, co_out)):
        for h in range(2):
            out[:, 512 * h : 512 * h + 512] = rows[
                16 * h : 16 * h + 16, 512 * i : 512 * i + 512
            ].astype(F32)


def late_unpack_kernel(ids, mine, came, rows):
    return call(
        late_unpack_body,
        [shape((3, 16, D), F32), shape((16, D), F32), shape((16, D), F32), shape((16, D), F32)],
        (ids, mine, came, rows),
        specs=[SMEM, WHOLE, WHOLE, WHOLE],
    )


def swap_core(value):
    return lax.ppermute(value, "core", [(0, 1), (1, 0)])


def swap_seq(value):
    return lax.ppermute(value, "xl", [(0, 1), (1, 0)])


def swap_x(value, pairs):
    return lax.ppermute(value, RING_X, [p for a, b in pairs for p in ((a, b), (b, a))])


def in_order(index, mine, other, axis):
    first = jnp.where(index == 0, mine, other)
    second = jnp.where(index == 0, other, mine)
    return jnp.stack((first, second), axis=axis)


def join(index, mine, other, axis):
    first = jnp.where(index == 0, mine, other)
    second = jnp.where(index == 0, other, mine)
    return jnp.concatenate((first, second), axis=axis)


def pick(value, index, axis):
    return jnp.where(
        index == 0, lax.index_in_dim(value, 0, axis, False), lax.index_in_dim(value, 1, axis, False)
    )


def gather_chips(pair):
    full = lax.all_gather(pair, ("z", "y"), axis=0, tiled=False)
    return full.reshape(4, 4, *pair.shape)


def ring(value, axis, size, step):
    return lax.ppermute(value, axis, [(i, (i + step) % size) for i in range(size)])


def exchange(value, axes):
    return lax.all_to_all(value, axes, 0, 0, tiled=True)


def zy_scatter(full):
    cols = full.shape[-1]
    part = lax.psum_scatter(full.reshape(D, cols), ("z", "y"), scatter_dimension=0, tiled=True)
    return part.reshape(2, 32, cols)


def halves_as_rows(value):
    k = value.shape[-1] // 2
    return jnp.concatenate((value[:, :k], value[:, k:]), axis=0)


def per_device(
    tokens_in,
    noise_emb,
    text_emb,
    prompt_len,
    mod_weight,
    qkv_weight,
    proj_weight,
    cq_weight,
    text_weight,
    co_weight,
    norm_gains,
    up_weight,
    down_weight,
    out_grad,
):
    core = lax.axis_index("core")
    xh = lax.axis_index("xh")
    xl = lax.axis_index("xl")
    rows = tokens_in.shape[1]

    misc = jnp.concatenate(
        (
            jnp.pad(text_emb[0], ((0, 0), (0, D - TEXT_W))),
            jnp.broadcast_to(prompt_len.astype(BF)[:, None], (8, D)),
        ),
        axis=0,
    )
    mine = jnp.concatenate((tokens_in[0], out_grad[0], misc), axis=0)
    both = in_order(core, mine, swap_core(mine), 0)
    tok = both[:, :rows].reshape(256, D)
    og = both[:, rows : 2 * rows].reshape(256, D)
    text = both[:, 2 * rows : 2 * rows + 8, :TEXT_W]
    lens = both[:, 2 * rows + 8, 0].astype(jnp.int32)

    def side(which):
        up = pick(up_weight.reshape(16, 32, 2, 64), which, 2).reshape(16, C_UP)
        qkv = pick(qkv_weight.reshape(16, 3, 2, 512), which, 2).reshape(16, C_QKV)
        cq = pick(cq_weight.reshape(16, 2, 512), which, 1)
        txt = pick(text_weight.reshape(12, 2, 2, 256), which, 2).reshape(12, C_TEXT)
        gains = jnp.pad(norm_gains, ((0, 2), (0, C_TEXT - 16)))
        return jnp.concatenate((qkv, cq, jnp.concatenate((txt, gains), axis=0), up), axis=1)

    shared = join(core, side(core), swap_core(side(1 - core)), 0)
    first = jnp.concatenate(
        (
            shared[:, : C_QKV + C_CQ + C_TEXT],
            halves_as_rows(proj_weight),
            halves_as_rows(co_weight),
        ),
        axis=1,
    )
    second = jnp.concatenate(
        (shared[:, C_QKV + C_CQ + C_TEXT :], down_weight[:32, C_X:], down_weight[32:, C_X:]), axis=1
    )
    near, xl_pair, across = ((0, 3), (1, 2)), ((0, 1), (2, 3)), ((0, 2), (1, 3))
    lo, hi = TEXT_COLS
    first_far = swap_x(first, ((0, 3), (1, 2)))
    text_far = swap_x(first[:, lo:hi], ((0, 2), (1, 3)))
    second, first_far = lax.optimization_barrier((second, first_far))
    first_far = jnp.concatenate((first_far[:, :lo], text_far, first_far[:, hi:]), axis=1)
    down_halves = down_weight.reshape(2, 32, D)
    first_pair = jnp.concatenate(
        (in_order(xh, first, first_far, 0), down_halves[..., :C_X]), axis=2
    )
    full_one = gather_chips(first_pair)
    full_two = gather_chips(in_order(xh, second, swap_x(second, near), 0))
    full_one, down_own = lax.optimization_barrier((full_one, full_one[..., -C_X:]))
    down_far = swap_x(down_own, near)

    text_rows = full_one[..., lo:hi].transpose(0, 2, 1, 3, 4)
    text_rows = text_rows.reshape(64, 16, C_TEXT)
    text_w = text_rows[:, :12].reshape(TEXT_W, 2, 256)
    gains = text_rows[:, 12:14, :16].transpose(1, 0, 2).reshape(2, D).astype(F32)
    core_id = core.astype(jnp.int32)[None]
    y_id = lax.axis_index("y")
    ids = jnp.stack([core, 2 * xh + xl, y_id, xl]).astype(jnp.int32)

    noise_cols = exchange(noise_emb.reshape(64, 16), FSDP)
    half = pick(mod_weight.reshape(16, 2, D), xl, 1)
    mod_parts = jnp.dot(noise_cols, half, preferred_element_type=F32)
    mod_part = jnp.sum(exchange(mod_parts, FSDP), axis=0, keepdims=True)
    mod_own = join(xl, mod_part, swap_seq(mod_part), 1)
    mod_all = in_order(core, mod_own, swap_core(mod_own), 0).reshape(2, 2, D)
    mod_scale, mod_shift = mod_all[:, 0], mod_all[:, 1]
    normed_one, queries, kv_own = qkv_kernel(tok, mod_scale, mod_shift, full_one)
    kv_far = swap_seq(kv_own)
    later, kv_own = lax.optimization_barrier((full_one, kv_own))
    halves = later[..., hi : hi + 2 * 512].reshape(2, 2, 4, 2, 32, D)
    kept = pick(halves, core, 0)
    proj_w, co_w = rows_kernel(core_id, kept, swap_core(pick(halves, 1 - core, 0)))
    attended, proj_part = attend_kernel(queries, kv_own, kv_far, proj_w)
    proj_part, down_far = lax.optimization_barrier((proj_part, down_far))
    text_own = jnp.einsum("ijt,tcn->ijcn", text, text_w, preferred_element_type=F32).astype(BF)
    text_xl = in_order(xl, text_own, swap_seq(text_own), 0)
    text_kv = join(core, pick(text_xl, core, 0), swap_core(pick(text_xl, 1 - core, 0)), 3)
    text_kv = text_kv.reshape(2, TXT, D)
    after_self, normed_two, cross_q, cross_att, co_part = cross_kernel(
        tok, proj_part, swap_core(proj_part), gains, full_one, text_kv, lens, co_w
    )
    after_cross, ff_wg, three_part, down_part = ff_kernel(
        ids, after_self, co_part, swap_core(co_part), gains, og, down_own, down_far, full_two
    )
    ff_sc = zy_scatter(ff_wg)
    down_part = down_part.reshape(2, rows, D)
    down_own = pick(down_part, core, 0) + swap_core(pick(down_part, 1 - core, 0))
    block_out = (pick(after_cross.reshape(2, rows, D), core, 0) + down_own).astype(BF)[None]

    cross_res_grad, gain_three_grad, co_wg, cq_wg, text_sum, two_part = cross_back_kernel(
        three_part, swap_core(three_part), after_cross, og, gains, cross_att, cross_q,
        normed_two, text_kv, lens, co_w, full_one,
    )
    self_res_grad, gain_two_grad, proj_wg, dq, dkv, dkv_far = self_back_kernel(
        two_part, swap_core(two_part), after_self, cross_res_grad, gains, attended, queries,
        kv_own, kv_far, proj_w,
    )
    rows_kept, rows_sent = rows_back_kernel(core_id, proj_wg, co_wg)
    dkv_came = swap_seq(dkv_far)
    rows_came = swap_core(rows_sent)
    qkv_wg, one_part = qkv_back_kernel(dq, dkv, dkv_came, normed_one, full_one)

    text_sum = (text_sum + swap_seq(text_sum.astype(BF)).astype(F32)).astype(BF)
    text_quarters = text_sum.reshape(2, TXT, 2, 2, 256)
    text_kept = pick(text_quarters, core, 3)
    text_came = swap_core(pick(text_quarters, 1 - core, 3))
    text_kv_grad = jnp.where(core == xl, text_kept, text_came)
    text_wg = jnp.einsum("ijt,ijcn->tcn", text, text_kv_grad, preferred_element_type=F32)
    text_part = jnp.einsum("ijcn,tcn->ijt", text_kv_grad, text_w, preferred_element_type=F32)

    one_part = one_part.reshape(2, rows, D)
    one_grad = pick(one_part, core, 0) + swap_core(pick(one_part, 1 - core, 0))
    own_tokens = tokens_in.astype(F32)
    _, mod_back = jax.vjp(
        modulated_norm, own_tokens, pick(mod_scale, core, 0)[None], pick(mod_shift, core, 0)[None]
    )
    input_part, scale_grad, shift_grad = mod_back(one_grad[None])
    tokens_grad = pick(self_res_grad.reshape(2, rows, D), core, 0)[None] + input_part
    mod_grad = jnp.concatenate((scale_grad, shift_grad), axis=1)
    mod_grad = (mod_grad + swap_seq(mod_grad)).astype(BF)
    mod_grads = exchange(jnp.broadcast_to(mod_grad, (64, 2 * D)), FSDP)
    mod_wgrad = jnp.einsum("if,ic->fc", noise_cols, mod_grads, preferred_element_type=F32)
    noise_parts = jnp.einsum("ic,fc->if", mod_grads, mod_weight, preferred_element_type=F32)
    noise_grad = exchange(noise_parts, FSDP).reshape(1, D)

    gains_wg = jnp.concatenate((gain_two_grad, gain_three_grad), axis=0).astype(BF)
    gains_wg = jnp.pad(
        gains_wg.reshape(2, 64, 16).transpose(1, 0, 2), ((0, 0), (0, 2), (0, C_TEXT - 16))
    )
    text_pack = jnp.concatenate((text_wg.astype(BF).reshape(64, 12, C_TEXT), gains_wg), axis=1)
    text_pack = text_pack.reshape(4, 2, 4, 32, C_TEXT).transpose(0, 2, 1, 3, 4)
    late_wg = late_kernel(ids, text_pack, qkv_wg, cq_wg, rows_kept, rows_came)
    late_wg, ff_sc = lax.optimization_barrier((late_wg, ff_sc))
    late_sc = zy_scatter(late_wg)

    own, far = pick(ff_sc, xh, 0), pick(ff_sc, 1 - xh, 0)
    ff_g = sum_kernel(own, swap_x(own, xl_pair), swap_x(far, near), swap_x(far, across))
    up_rows = ff_g[:, :C_UP].reshape(2, 16, C_UP)
    up_wgrad, down_wgrad = ff_unpack_kernel(
        ids, pick(up_rows, core, 0), swap_core(pick(up_rows, 1 - core, 0)), ff_g[:, C_UP:]
    )

    own, far = pick(late_sc, xh, 0), pick(late_sc, 1 - xh, 0)
    late_g = late_sum_kernel(own, swap_x(own, xl_pair), swap_x(far, near), swap_x(far, across))
    late_rows = late_g[:, :LATE_ROWS].reshape(2, 16, LATE_ROWS)
    kept_rows = pick(late_rows, core, 0)
    came_rows = swap_core(pick(late_rows, 1 - core, 0))
    qkv_wgrad, cq_wgrad, proj_wgrad, co_wgrad = late_unpack_kernel(
        ids, kept_rows, came_rows, late_g[:, LATE_ROWS:]
    )
    qkv_wgrad = qkv_wgrad.transpose(1, 0, 2)
    lo, hi = C_QKV, C_QKV + C_TEXT
    text_both = in_order(core, kept_rows[:, lo:hi], came_rows[:, lo:hi], 0).astype(F32)
    text_wgrad = text_both[:, :12].reshape(2, 12, 2, 256).transpose(1, 2, 0, 3).reshape(12, 2, 512)
    gains_grad = kept_rows[12:14, lo : lo + 16].astype(F32)

    text_grad = pick(text_part, core, 0) + swap_core(pick(text_part, 1 - core, 0))
    text_grad = text_grad + swap_seq(text_grad)
    return (
        block_out,
        tokens_grad,
        noise_grad,
        text_grad[None],
        mod_wgrad,
        qkv_wgrad,
        proj_wgrad,
        cq_wgrad,
        text_wgrad,
        co_wgrad,
        gains_grad,
        up_wgrad,
        down_wgrad,
    )


def solution(mesh):
    split = Mesh(mesh.devices.reshape(SIZES), AXES)
    in_specs = (
        P(FSDP, "xl", None),
        P(FSDP, None),
        P(FSDP, None, None),
        P(FSDP),
        P(FSDP, None),
        P(FSDP, None, None),
        P(FSDP, None),
        P(FSDP, None),
        P(FSDP, None, "xl"),
        P(FSDP, None),
        P(None, FSDP),
        P(FSDP, None),
        P(FSDP, None),
        P(FSDP, "xl", None),
    )
    out_specs = (
        P(FSDP, "xl", None),
        P(FSDP, "xl", None),
        P(FSDP, None),
        P(FSDP, None, None),
        P(FSDP, None),
        P(FSDP, None, None),
        P(FSDP, None),
        P(FSDP, None),
        P(FSDP, None, "xl"),
        P(FSDP, None),
        P(None, FSDP),
        P(FSDP, None),
        P(FSDP, None),
    )
    return jax.shard_map(
        per_device, mesh=split, in_specs=in_specs, out_specs=out_specs, check_vma=False
    )
```

```python
import jax
import jax.numpy as jnp
from jax import lax
from jax.experimental import pallas as pl
from jax.experimental.pallas import tpu as pltpu
from jax.sharding import Mesh
from jax.sharding import PartitionSpec as P

HEAD_DIM = 64
EPSILON = 1e-06
HIGHEST_PREC = lax.Precision.HIGHEST
NEG_LARGE = -1e30
BF = jnp.bfloat16
F32 = jnp.float32

AXES = ("z", "xh", "y", "core", "xl")
SIZES = (4, 2, 4, 2, 2)
FSDP = ("z", "xh", "y", "core")
RING_X = ("xh", "xl")

D = 1024
FF = 4096
TEXT_W = 768
TXT = 8
CHIPS = 32

C_X = 768
C_QKV, C_CQ, C_TEXT, C_PROJ, C_CO = 1536, 512, 512, 512, 512
TEXT_COLS = (C_QKV + C_CQ, C_QKV + C_CQ + C_TEXT)
C_UP, C_DOWN = 2048, 2048


def rms_norm(tensor):
    return tensor * lax.rsqrt(jnp.mean(tensor * tensor, axis=-1, keepdims=True) + EPSILON)


def modulated_norm(tensor, scale, shift):
    return rms_norm(tensor) * (1.0 + scale[:, None, :]) + shift[:, None, :]


def mm(a, b):
    return jnp.dot(a, b, preferred_element_type=F32)


def mm_nt(a, b):
    return lax.dot_general(a, b, (((1,), (1,)), ((), ())), preferred_element_type=F32)


def mm_tn(a, b):
    return lax.dot_general(a, b, (((0,), (0,)), ((), ())), preferred_element_type=F32)


CHIP_ORDER = [(z, xh, y) for z in range(4) for xh in range(2) for y in range(4)]


def nat(ref):
    return jnp.concatenate([ref[z, y, xh] for z, xh, y in CHIP_ORDER], axis=0)


def store_nat(ref, value):
    for i, (z, xh, y) in enumerate(CHIP_ORDER):
        ref[z, y, xh] = value[32 * i : 32 * i + 32].astype(ref.dtype)


def norm_of(x):
    inv = lax.rsqrt(jnp.mean(x * x, axis=-1, keepdims=True) + EPSILON)
    return x * inv, inv


def norm_grad(unit, inv, dh_w):
    return (dh_w - unit * jnp.mean(dh_w * unit, axis=-1, keepdims=True)) * inv


def call(body, outs, ins, scratch=(), specs=None, out_specs=None, grid=None, prefetch=0):
    whole = pl.BlockSpec(memory_space=pltpu.VMEM)
    return pl.pallas_call(
        body,
        out_shape=outs,
        grid_spec=pltpu.PrefetchScalarGridSpec(
            num_scalar_prefetch=prefetch,
            grid=grid or (),
            in_specs=specs or [whole] * len(ins),
            out_specs=out_specs or [whole] * len(outs),
            scratch_shapes=list(scratch),
        ),
        compiler_params=pltpu.CompilerParams(vmem_limit_bytes=60 * 1024 * 1024),
    )(*ins)


def shape(dims, dtype):
    return jax.ShapeDtypeStruct(dims, dtype)


WHOLE = pl.BlockSpec(memory_space=pltpu.VMEM)
SMEM = pl.BlockSpec(memory_space=pltpu.SMEM)


def cols_spec(block, width=512):
    return pl.BlockSpec((4, 4, 2, 32, width), lambda i: (0, 0, 0, 0, block))


def fixed(dims):
    return pl.BlockSpec(dims, lambda i: (0,) * len(dims))


def qkv_body(tok, scale, shift, wq, wk, wv, n1_out, q_out, kv_out):
    for b in range(2):
        r = slice(128 * b, 128 * b + 128)
        unit, _ = norm_of(tok[r].astype(F32))
        n1_out[r] = (unit * (1.0 + scale[b : b + 1]) + shift[b : b + 1]).astype(BF)
    n1 = n1_out[...]
    q_out[...] = mm(n1, nat(wq)).astype(BF)
    kv_out[:, :512] = mm(n1, nat(wk)).astype(BF)
    kv_out[:, 512:] = mm(n1, nat(wv)).astype(BF)


def qkv_kernel(tok, scale, shift, full):
    return call(
        qkv_body,
        [shape((256, D), BF), shape((256, 512), BF), shape((256, D), BF)],
        (tok, scale, shift, full, full, full),
        specs=[fixed((256, D)), fixed((2, D)), fixed((2, D)), cols_spec(0), cols_spec(1), cols_spec(2)],
        out_specs=[fixed((256, D)), fixed((256, 512)), fixed((256, D))],
        grid=(1,),
    )


def head_cols(h):
    return slice(64 * h, 64 * h + 64)


def self_probs(q, k):
    scores = mm_nt(q, k) * HEAD_DIM ** (-0.5)
    e = jnp.exp(scores - jnp.max(scores, axis=-1, keepdims=True))
    return e * (1.0 / jnp.sum(e, axis=-1, keepdims=True))


def attend_body(q, kv, kv_far, proj_w, att_out, part_out):
    for b in range(2):
        r = slice(128 * b, 128 * b + 128)
        for h in range(8):
            k = jnp.concatenate((kv[r, head_cols(h)], kv_far[r, head_cols(h)]), axis=0)
            v = jnp.concatenate((kv[r, head_cols(8 + h)], kv_far[r, head_cols(8 + h)]), axis=0)
            p = self_probs(q[r, head_cols(h)], k).astype(BF)
            att_out[r, head_cols(h)] = mm(p, v).astype(BF)
    part_out[...] = mm(att_out[...], proj_w[...])


def attend_kernel(q, kv, kv_far, proj_w):
    return call(
        attend_body, [shape((256, 512), BF), shape((256, D), F32)], (q, kv, kv_far, proj_w)
    )


def spread_heads(rows8):
    tall = jnp.concatenate([rows8.astype(F32)] * 16, axis=0)
    row = lax.broadcasted_iota(jnp.int32, tall.shape, 0) // 8
    col = lax.broadcasted_iota(jnp.int32, tall.shape, 1) // 64
    return jnp.where(row == col, tall, 0.0).astype(BF)


def fold_heads(tall):
    row = lax.broadcasted_iota(jnp.int32, tall.shape, 0) // 8
    col = lax.broadcasted_iota(jnp.int32, tall.shape, 1) // 64
    kept = jnp.where(row == col, tall, 0.0)
    total = kept[0:8]
    for h in range(1, 8):
        total = total + kept[8 * h : 8 * h + 8]
    return total


def by_eights(op, x):
    lane = lax.broadcasted_iota(jnp.int32, x.shape, 1)
    for step in (1, 2, 4):
        up = pltpu.roll(x, x.shape[1] - step, 1)
        down = pltpu.roll(x, step, 1)
        x = op(x, jnp.where((lane & step) == 0, up, down))
    return x


def cross_probs(q, keys, length):
    scores = mm_nt(q, keys) * HEAD_DIM ** (-0.5)
    lane = lax.broadcasted_iota(jnp.int32, scores.shape, 1)
    scores = jnp.where((lane & 7) < length, scores, NEG_LARGE)
    e = jnp.exp(scores - by_eights(jnp.maximum, scores))
    return e * (1.0 / by_eights(jnp.add, e))


def cross_body(
    tok, part, part_far, gains, cq_w, text_kv, lens, co_w, res_out, n2_out, cq_out, att_out, part_out
):
    res_out[...] = tok[...].astype(F32) + (part[...] + part_far[...])
    unit, _ = norm_of(res_out[...])
    n2_out[...] = (unit * gains[0:1]).astype(BF)
    cq_out[...] = mm(n2_out[...], nat(cq_w)).astype(BF)
    for b in range(2):
        r = slice(128 * b, 128 * b + 128)
        keys = spread_heads(text_kv[b, :, 0:512])
        vals = spread_heads(text_kv[b, :, 512:1024])
        p = cross_probs(cq_out[r], keys, lens[b]).astype(BF)
        att_out[r] = mm(p, vals).astype(BF)
    part_out[...] = mm(att_out[...], co_w[...])


def cross_kernel(tok, part, part_far, gains, full, text_kv, lens, co_w):
    f = fixed
    return call(
        cross_body,
        [
            shape((256, D), F32),
            shape((256, D), BF),
            shape((256, 512), BF),
            shape((256, 512), BF),
            shape((256, D), F32),
        ],
        (tok, part, part_far, gains, full, text_kv, lens, co_w),
        specs=[
            f((256, D)),
            f((256, D)),
            f((256, D)),
            f((2, D)),
            cols_spec(3),
            f((2, 8, D)),
            SMEM,
            f((512, D)),
        ],
        out_specs=[f((256, D)), f((256, D)), f((256, 512)), f((256, 512)), f((256, D))],
        grid=(1,),
    )


GELU_A = 0.7978845608028654
GELU_B = 0.044715


def ff_copies(g_up, g_down, grad, sem, i):
    at = pl.ds(pl.multiple_of(i * 512, 512), 512)
    return (
        pltpu.make_async_copy(g_up.at[i], grad.at[:, :, :, :, at], sem.at[0, i]),
        pltpu.make_async_copy(g_down.at[i], grad.at[i, :, :, :, C_UP:], sem.at[1, i]),
    )


def ff_body(
    ids, res, part, part_far, gains, og, up, down, down_far, rest,
    res_out, grad_out, three_out, down_out, n3, n3_t, g_up, g_down, sem,
):
    i = pl.program_id(0)

    @pl.when(i == 0)
    def _():
        res_out[...] = res[...] + (part[...] + part_far[...])
        unit, _ = norm_of(res_out[...])
        low = (unit * gains[1:2]).astype(BF)
        n3[...] = low
        n3_t[...] = low.T

    up_w = nat(up)
    low_xh = ids[1] < 2
    own, far = down[0].reshape(256, C_X), down_far[0].reshape(256, C_X)
    left = jnp.concatenate((jnp.where(low_xh, own, far), jnp.where(low_xh, far, own)), axis=0)
    k = D - C_X
    right = jnp.concatenate(
        [
            rest[0, y, xh, :, k * h : k * h + k]
            for xh in range(2)
            for y in range(4)
            for h in range(2)
        ],
        axis=0,
    )
    down_w = jnp.concatenate((left, right), axis=1)
    pre = mm(n3[...], up_w)
    t = jnp.tanh(GELU_A * (pre + GELU_B * (pre * pre * pre)))
    act = (0.5 * pre * (1.0 + t)).astype(BF)
    slope = 0.5 * (1.0 + t) + 0.5 * pre * (1.0 - t * t) * (
        GELU_A * (1.0 + 3.0 * GELU_B * (pre * pre))
    )
    pre_grad = (mm_nt(og[...], down_w) * slope).astype(BF)
    up_wg = mm(n3_t[...], pre_grad).astype(BF)
    for j, (z, xh, y) in enumerate(CHIP_ORDER):
        g_up[i, z, y, xh] = up_wg[32 * j : 32 * j + 32]
    down_wg = mm_tn(act, og[...]).astype(BF)
    j = 0
    for xh in range(2):
        for y in range(4):
            for h in range(2):
                g_down[i, y, xh, :, D * h : D * h + D] = down_wg[32 * j : 32 * j + 32]
                j += 1
    for copy in ff_copies(g_up, g_down, grad_out, sem, i):
        copy.start()
    down_part = mm(act, down_w)
    three_part = mm_nt(pre_grad, up_w)

    @pl.when(i == 0)
    def _():
        down_out[...] = down_part
        three_out[...] = three_part

    @pl.when(i > 0)
    def _():
        down_out[...] += down_part
        three_out[...] += three_part

    @pl.when(i == 3)
    def _():
        for k in range(4):
            for copy in ff_copies(g_up, g_down, grad_out, sem, k):
                copy.wait()


def ff_kernel(ids, res, part, part_far, gains, og, down, down_far, full):
    f = fixed
    return call(
        ff_body,
        [
            shape((256, D), F32),
            shape((4, 4, 2, 32, C_UP + C_DOWN), BF),
            shape((256, D), F32),
            shape((256, D), F32),
        ],
        (ids, res, part, part_far, gains, og, full, down, down_far, full),
        scratch=[
            pltpu.VMEM((256, D), BF),
            pltpu.VMEM((D, 256), BF),
            pltpu.VMEM((4, 4, 4, 2, 32, 512), BF),
            pltpu.VMEM((4, 4, 2, 32, 2048), BF),
            pltpu.SemaphoreType.DMA((2, 4)),
        ],
        specs=[
            SMEM,
            f((256, D)),
            f((256, D)),
            f((256, D)),
            f((2, D)),
            f((256, D)),
            pl.BlockSpec((4, 4, 2, 32, 512), lambda i: (0, 0, 0, 0, i)),
            pl.BlockSpec((1, 4, 2, 32, C_X), lambda i: (i, 0, 0, 0, 0)),
            pl.BlockSpec((1, 4, 2, 32, C_X), lambda i: (i, 0, 0, 0, 0)),
            pl.BlockSpec((1, 4, 2, 32, 512), lambda i: (i, 0, 0, 0, 4)),
        ],
        out_specs=[f((256, D)), pl.BlockSpec(memory_space=pl.ANY), f((256, D)), f((256, D))],
        grid=(4,),
    )

def cross_back_body(
    part, part_far, res, og, gains, att, cq, n2, text_kv, lens, co_w, cq_w,
    grad_out, gain_out, co_out, cqw_out, text_out, two_out, ag, dq,
):
    unit, inv = norm_of(res[...])
    three = part[...] + part_far[...]
    gain_out[...] = jnp.sum(three * unit, axis=0, keepdims=True)
    grad_out[...] = og[...].astype(F32) + norm_grad(unit, inv, three * gains[1:2])
    low = grad_out[...].astype(BF)
    co_out[...] = mm_tn(att[...], low).astype(BF)
    ag[...] = mm_nt(low, co_w[...]).astype(BF)
    for b in range(2):
        r = slice(128 * b, 128 * b + 128)
        keys = spread_heads(text_kv[b, :, 0:512])
        vals = spread_heads(text_kv[b, :, 512:1024])
        p = cross_probs(cq[r], keys, lens[b])
        dp = mm_nt(ag[r], vals)
        ds = (p * (dp - by_eights(jnp.add, p * dp))).astype(BF)
        dq[r] = (mm(ds, keys) * HEAD_DIM ** (-0.5)).astype(BF)
        text_out[b, :, 0:512] = fold_heads(mm_tn(ds, cq[r])) * HEAD_DIM ** (-0.5)
        text_out[b, :, 512:1024] = fold_heads(mm_tn(p.astype(BF), ag[r]))
    store_nat(cqw_out, mm_tn(n2[...], dq[...]))
    two_out[...] = mm_nt(dq[...], nat(cq_w))


def cross_back_kernel(part, part_far, res, og, gains, att, cq, n2, text_kv, lens, co_w, full):
    f = fixed
    return call(
        cross_back_body,
        [
            shape((256, D), F32),
            shape((1, D), F32),
            shape((512, D), BF),
            shape((4, 4, 2, 32, 512), BF),
            shape((2, 8, D), F32),
            shape((256, D), F32),
        ],
        (part, part_far, res, og, gains, att, cq, n2, text_kv, lens, co_w, full),
        scratch=[pltpu.VMEM((256, 512), BF), pltpu.VMEM((256, 512), BF)],
        specs=[
            f((256, D)),
            f((256, D)),
            f((256, D)),
            f((256, D)),
            f((2, D)),
            f((256, 512)),
            f((256, 512)),
            f((256, D)),
            f((2, 8, D)),
            SMEM,
            f((512, D)),
            cols_spec(3),
        ],
        out_specs=[
            f((256, D)),
            f((1, D)),
            f((512, D)),
            f((4, 4, 2, 32, 512)),
            f((2, 8, D)),
            f((256, D)),
        ],
        grid=(1,),
    )


def self_back_body(
    part, part_far, res, res_grad, gains, att, q, kv, kv_far, proj_w,
    grad_out, gain_out, proj_out, dq_out, dkv_out, dfar_out, ag,
):
    unit, inv = norm_of(res[...])
    two = part[...] + part_far[...]
    gain_out[...] = jnp.sum(two * unit, axis=0, keepdims=True)
    grad_out[...] = res_grad[...] + norm_grad(unit, inv, two * gains[0:1])
    low = grad_out[...].astype(BF)
    proj_out[...] = mm_tn(att[...], low).astype(BF)
    ag[...] = mm_nt(low, proj_w[...]).astype(BF)
    factor = HEAD_DIM ** (-0.5)
    for b in range(2):
        r = slice(128 * b, 128 * b + 128)
        for h in range(8):
            kc, vc = head_cols(h), head_cols(8 + h)
            k = jnp.concatenate((kv[r, kc], kv_far[r, kc]), axis=0)
            v = jnp.concatenate((kv[r, vc], kv_far[r, vc]), axis=0)
            qh = q[r, kc]
            gh = ag[r, kc]
            p = self_probs(qh, k)
            dp = mm_nt(gh, v)
            ds = (p * (dp - jnp.sum(p * dp, axis=-1, keepdims=True))).astype(BF)
            dq_out[r, kc] = (mm(ds, k) * factor).astype(BF)
            dk = mm_tn(ds, qh) * factor
            dv = mm_tn(p.astype(BF), gh)
            dkv_out[r, kc] = dk[:128]
            dkv_out[r, vc] = dv[:128]
            dfar_out[r, kc] = dk[128:].astype(BF)
            dfar_out[r, vc] = dv[128:].astype(BF)


def self_back_kernel(part, part_far, res, res_grad, gains, att, q, kv, kv_far, proj_w):
    return call(
        self_back_body,
        [
            shape((256, D), F32),
            shape((1, D), F32),
            shape((512, D), BF),
            shape((256, 512), BF),
            shape((256, D), F32),
            shape((256, D), BF),
        ],
        (part, part_far, res, res_grad, gains, att, q, kv, kv_far, proj_w),
        scratch=[pltpu.VMEM((256, 512), BF)],
    )


def qkv_back_body(dq, dkv, dfar, n1, wq, wk, wv, wg_out, part_out):
    n = n1[...]
    dqv = dq[...]
    dkvv = (dkv[...] + dfar[...].astype(F32)).astype(BF)
    grads = (dqv, dkvv[:, :512], dkvv[:, 512:])
    total = None
    for i, (g, w) in enumerate(zip(grads, (wq, wk, wv))):
        wg = mm_tn(n, g).astype(BF)
        for j, (z, xh, y) in enumerate(CHIP_ORDER):
            wg_out[z, y, xh, :, 512 * i : 512 * i + 512] = wg[32 * j : 32 * j + 32]
        t = mm_nt(g, nat(w))
        total = t if total is None else total + t
    part_out[...] = total


def qkv_back_kernel(dq, dkv, dfar, n1, full):
    f = fixed
    return call(
        qkv_back_body,
        [shape((4, 4, 2, 32, 1536), BF), shape((256, D), F32)],
        (dq, dkv, dfar, n1, full, full, full),
        specs=[
            f((256, 512)),
            f((256, D)),
            f((256, D)),
            f((256, D)),
            cols_spec(0),
            cols_spec(1),
            cols_spec(2),
        ],
        out_specs=[f((4, 4, 2, 32, 1536)), f((256, D))],
        grid=(1,),
    )


def sum_body(*refs):
    total = refs[0][...].astype(F32)
    for r in refs[1:-1]:
        total = total + r[...].astype(F32)
    refs[-1][...] = total.astype(refs[-1].dtype)


def sum_kernel(*pieces):
    return call(sum_body, [shape(pieces[0].shape, BF)], pieces)[0]


LATE = C_QKV + C_TEXT + C_CQ + C_PROJ + C_CO
LATE_ROWS = LATE - C_PROJ - C_CO


def late_body(ids, text, qkv, cq, kept, came, out):
    out[:, :, :, :, :C_QKV] = qkv[...]
    at = C_QKV + C_TEXT
    out[:, :, :, :, C_QKV:at] = text[...]
    out[:, :, :, :, at : at + C_CQ] = cq[...]
    first = ids[0] == 0
    a, b = kept[...], came[...]
    out[:2, :, :, :, LATE_ROWS:] = jnp.where(first, a, b)
    out[2:, :, :, :, LATE_ROWS:] = jnp.where(first, b, a)


def late_kernel(ids, text, qkv, cq, kept, came):
    return call(
        late_body,
        [shape((4, 4, 2, 32, LATE), BF)],
        (ids, text, qkv, cq, kept, came),
        specs=[SMEM, *[WHOLE] * 5],
    )[0]


def late_sum_body(own, a, b, e, out):
    near = a[...].astype(F32) + b[...].astype(F32)
    row = lax.broadcasted_iota(jnp.int32, near.shape, 0) % 16
    col = lax.broadcasted_iota(jnp.int32, near.shape, 1)
    text = (col >= C_QKV) & (col < C_QKV + C_TEXT)
    near = jnp.where((row < 12) & text, 0.0, near)
    out[...] = (own[...].astype(F32) + e[...].astype(F32) + near).astype(BF)


def late_sum_kernel(own, a, b, e):
    return call(late_sum_body, [shape((32, LATE), BF)], (own, a, b, e))[0]


def rows_body(core, kept, came, proj_out, co_out):
    first = core[0] == 0
    i = 0
    for z in range(2):
        for xh in range(2):
            for y in range(4):
                a, b = kept[z, y, xh], came[z, y, xh]
                for bit in range(2):
                    t = jnp.where(first, a, b) if bit == 0 else jnp.where(first, b, a)
                    for out, c in ((proj_out, 0), (co_out, 512)):
                        out[16 * i : 16 * i + 16, :512] = t[:16, c : c + 512]
                        out[16 * i : 16 * i + 16, 512:] = t[16:, c : c + 512]
                    i += 1


def rows_kernel(core, kept, came):
    return call(
        rows_body,
        [shape((512, D), BF), shape((512, D), BF)],
        (core, kept, came),
        specs=[SMEM, WHOLE, WHOLE],
    )


def rows_back_body(core, proj_wg, co_wg, kept_out, sent_out):
    first = core[0] == 0
    i = 0
    for z in range(2):
        for xh in range(2):
            for y in range(4):
                t = []
                for bit in range(2):
                    r = slice(16 * i, 16 * i + 16)
                    t.append(
                        jnp.concatenate(
                            (
                                jnp.concatenate((proj_wg[r, :512], proj_wg[r, 512:]), axis=0),
                                jnp.concatenate((co_wg[r, :512], co_wg[r, 512:]), axis=0),
                            ),
                            axis=1,
                        )
                    )
                    i += 1
                kept_out[z, y, xh] = jnp.where(first, t[0], t[1])
                sent_out[z, y, xh] = jnp.where(first, t[1], t[0])


def rows_back_kernel(core, proj_wg, co_wg):
    dims = shape((2, 4, 2, 32, D), BF)
    return call(
        rows_back_body, [dims, dims], (core, proj_wg, co_wg), specs=[SMEM, WHOLE, WHOLE]
    )


def ff_unpack_body(ids, mine, came, down, up_out, down_out):
    first = ids[0] == 0
    a, b = mine[...].astype(F32), came[...].astype(F32)
    parts = (jnp.where(first, a, b), jnp.where(first, b, a))
    for i in range(32):
        for c in range(2):
            to = 128 * i + 64 * c
            up_out[:, to : to + 64] = parts[c][:, 64 * i : 64 * i + 64]
    down_out[:32] = down[:, :D].astype(F32)
    down_out[32:] = down[:, D:].astype(F32)


def ff_unpack_kernel(ids, mine, came, down):
    return call(
        ff_unpack_body,
        [shape((16, FF), F32), shape((64, D), F32)],
        (ids, mine, came, down),
        specs=[SMEM, WHOLE, WHOLE, WHOLE],
    )


def late_unpack_body(ids, mine, came, rows, qkv_out, cq_out, proj_out, co_out):
    first = ids[0] == 0
    a, b = mine[...].astype(F32), came[...].astype(F32)
    parts = (jnp.where(first, a, b), jnp.where(first, b, a))
    for c in range(2):
        to = slice(512 * c, 512 * c + 512)
        for i in range(3):
            qkv_out[i, :, to] = parts[c][:, 512 * i : 512 * i + 512]
        cq_out[:, to] = parts[c][:, LATE_ROWS - 512 : LATE_ROWS]
    for i, out in enumerate((proj_out, co_out)):
        for h in range(2):
            out[:, 512 * h : 512 * h + 512] = rows[
                16 * h : 16 * h + 16, 512 * i : 512 * i + 512
            ].astype(F32)


def late_unpack_kernel(ids, mine, came, rows):
    return call(
        late_unpack_body,
        [shape((3, 16, D), F32), shape((16, D), F32), shape((16, D), F32), shape((16, D), F32)],
        (ids, mine, came, rows),
        specs=[SMEM, WHOLE, WHOLE, WHOLE],
    )


def swap_core(value):
    return lax.ppermute(value, "core", [(0, 1), (1, 0)])


def swap_seq(value):
    return lax.ppermute(value, "xl", [(0, 1), (1, 0)])


def swap_x(value, pairs):
    return lax.ppermute(value, RING_X, [p for a, b in pairs for p in ((a, b), (b, a))])


def in_order(index, mine, other, axis):
    first = jnp.where(index == 0, mine, other)
    second = jnp.where(index == 0, other, mine)
    return jnp.stack((first, second), axis=axis)


def join(index, mine, other, axis):
    first = jnp.where(index == 0, mine, other)
    second = jnp.where(index == 0, other, mine)
    return jnp.concatenate((first, second), axis=axis)


def pick(value, index, axis):
    return jnp.where(
        index == 0, lax.index_in_dim(value, 0, axis, False), lax.index_in_dim(value, 1, axis, False)
    )


def gather_chips(pair):
    full = lax.all_gather(pair, ("z", "y"), axis=0, tiled=False)
    return full.reshape(4, 4, *pair.shape)


def ring(value, axis, size, step):
    return lax.ppermute(value, axis, [(i, (i + step) % size) for i in range(size)])


def exchange(value, axes):
    return lax.all_to_all(value, axes, 0, 0, tiled=True)


def zy_scatter(full):
    cols = full.shape[-1]
    part = lax.psum_scatter(full.reshape(D, cols), ("z", "y"), scatter_dimension=0, tiled=True)
    return part.reshape(2, 32, cols)


def halves_as_rows(value):
    k = value.shape[-1] // 2
    return jnp.concatenate((value[:, :k], value[:, k:]), axis=0)


def per_device(
    tokens_in,
    noise_emb,
    text_emb,
    prompt_len,
    mod_weight,
    qkv_weight,
    proj_weight,
    cq_weight,
    text_weight,
    co_weight,
    norm_gains,
    up_weight,
    down_weight,
    out_grad,
):
    core = lax.axis_index("core")
    xh = lax.axis_index("xh")
    xl = lax.axis_index("xl")
    rows = tokens_in.shape[1]

    misc = jnp.concatenate(
        (
            jnp.pad(text_emb[0], ((0, 0), (0, D - TEXT_W))),
            jnp.broadcast_to(prompt_len.astype(BF)[:, None], (8, D)),
        ),
        axis=0,
    )
    mine = jnp.concatenate((tokens_in[0], out_grad[0], misc), axis=0)
    both = in_order(core, mine, swap_core(mine), 0)
    tok = both[:, :rows].reshape(256, D)
    og = both[:, rows : 2 * rows].reshape(256, D)
    text = both[:, 2 * rows : 2 * rows + 8, :TEXT_W]
    lens = both[:, 2 * rows + 8, 0].astype(jnp.int32)

    def side(which):
        qkv = pick(qkv_weight.reshape(16, 3, 2, 512), which, 2).reshape(16, C_QKV)
        cq = pick(cq_weight.reshape(16, 2, 512), which, 1)
        txt = pick(text_weight.reshape(12, 2, 2, 256), which, 2).reshape(12, C_TEXT)
        gains = jnp.pad(norm_gains, ((0, 2), (0, C_TEXT - 16)))
        return jnp.concatenate((qkv, cq, jnp.concatenate((txt, gains), axis=0)), axis=1)

    shared = join(core, side(core), swap_core(side(1 - core)), 0)
    first = jnp.concatenate(
        (
            shared[:, : C_QKV + C_CQ + C_TEXT],
            halves_as_rows(proj_weight),
            halves_as_rows(co_weight),
        ),
        axis=1,
    )
    near, xl_pair, across = ((0, 3), (1, 2)), ((0, 1), (2, 3)), ((0, 2), (1, 3))
    lo, hi = TEXT_COLS
    first_far = swap_x(first, ((0, 3), (1, 2)))
    text_far = swap_x(first[:, lo:hi], ((0, 2), (1, 3)))
    first_far, up_late = lax.optimization_barrier((first_far, up_weight))

    def up_side(which):
        return pick(up_late.reshape(16, 32, 2, 64), which, 2).reshape(16, C_UP)

    second = jnp.concatenate(
        (
            join(core, up_side(core), swap_core(up_side(1 - core)), 0),
            down_weight[:32, C_X:],
            down_weight[32:, C_X:],
        ),
        axis=1,
    )
    first_far = jnp.concatenate((first_far[:, :lo], text_far, first_far[:, hi:]), axis=1)
    down_halves = down_weight.reshape(2, 32, D)
    first_pair = jnp.concatenate(
        (in_order(xh, first, first_far, 0), down_halves[..., :C_X]), axis=2
    )
    full_one = gather_chips(first_pair)
    full_two = gather_chips(in_order(xh, second, swap_x(second, near), 0))
    full_one, down_own = lax.optimization_barrier((full_one, full_one[..., -C_X:]))
    down_far = swap_x(down_own, near)

    text_rows = full_one[..., lo:hi].transpose(0, 2, 1, 3, 4)
    text_rows = text_rows.reshape(64, 16, C_TEXT)
    text_w = text_rows[:, :12].reshape(TEXT_W, 2, 256)
    gains = text_rows[:, 12:14, :16].transpose(1, 0, 2).reshape(2, D).astype(F32)
    core_id = core.astype(jnp.int32)[None]
    y_id = lax.axis_index("y")
    ids = jnp.stack([core, 2 * xh + xl, y_id, xl]).astype(jnp.int32)

    noise_cols = exchange(noise_emb.reshape(64, 16), FSDP)
    half = pick(mod_weight.reshape(16, 2, D), xl, 1)
    mod_parts = jnp.dot(noise_cols, half, preferred_element_type=F32)
    mod_part = jnp.sum(exchange(mod_parts, FSDP), axis=0, keepdims=True)
    mod_own = join(xl, mod_part, swap_seq(mod_part), 1)
    mod_all = in_order(core, mod_own, swap_core(mod_own), 0).reshape(2, 2, D)
    mod_scale, mod_shift = mod_all[:, 0], mod_all[:, 1]
    normed_one, queries, kv_own = qkv_kernel(tok, mod_scale, mod_shift, full_one)
    kv_far = swap_seq(kv_own)
    later, kv_own = lax.optimization_barrier((full_one, kv_own))
    halves = later[..., hi : hi + 2 * 512].reshape(2, 2, 4, 2, 32, D)
    kept = pick(halves, core, 0)
    proj_w, co_w = rows_kernel(core_id, kept, swap_core(pick(halves, 1 - core, 0)))
    attended, proj_part = attend_kernel(queries, kv_own, kv_far, proj_w)
    proj_part, down_far = lax.optimization_barrier((proj_part, down_far))
    text_own = jnp.einsum("ijt,tcn->ijcn", text, text_w, preferred_element_type=F32).astype(BF)
    text_xl = in_order(xl, text_own, swap_seq(text_own), 0)
    text_kv = join(core, pick(text_xl, core, 0), swap_core(pick(text_xl, 1 - core, 0)), 3)
    text_kv = text_kv.reshape(2, TXT, D)
    after_self, normed_two, cross_q, cross_att, co_part = cross_kernel(
        tok, proj_part, swap_core(proj_part), gains, full_one, text_kv, lens, co_w
    )
    after_cross, ff_wg, three_part, down_part = ff_kernel(
        ids, after_self, co_part, swap_core(co_part), gains, og, down_own, down_far, full_two
    )
    ff_sc = zy_scatter(ff_wg)
    down_part = down_part.reshape(2, rows, D)
    down_own = pick(down_part, core, 0) + swap_core(pick(down_part, 1 - core, 0))
    block_out = (pick(after_cross.reshape(2, rows, D), core, 0) + down_own).astype(BF)[None]

    cross_res_grad, gain_three_grad, co_wg, cq_wg, text_sum, two_part = cross_back_kernel(
        three_part, swap_core(three_part), after_cross, og, gains, cross_att, cross_q,
        normed_two, text_kv, lens, co_w, full_one,
    )
    self_res_grad, gain_two_grad, proj_wg, dq, dkv, dkv_far = self_back_kernel(
        two_part, swap_core(two_part), after_self, cross_res_grad, gains, attended, queries,
        kv_own, kv_far, proj_w,
    )
    rows_kept, rows_sent = rows_back_kernel(core_id, proj_wg, co_wg)
    dkv_came = swap_seq(dkv_far)
    rows_came = swap_core(rows_sent)
    qkv_wg, one_part = qkv_back_kernel(dq, dkv, dkv_came, normed_one, full_one)

    text_sum = (text_sum + swap_seq(text_sum.astype(BF)).astype(F32)).astype(BF)
    text_quarters = text_sum.reshape(2, TXT, 2, 2, 256)
    text_kept = pick(text_quarters, core, 3)
    text_came = swap_core(pick(text_quarters, 1 - core, 3))
    text_kv_grad = jnp.where(core == xl, text_kept, text_came)
    text_wg = jnp.einsum("ijt,ijcn->tcn", text, text_kv_grad, preferred_element_type=F32)
    text_part = jnp.einsum("ijcn,tcn->ijt", text_kv_grad, text_w, preferred_element_type=F32)

    one_part = one_part.reshape(2, rows, D)
    one_grad = pick(one_part, core, 0) + swap_core(pick(one_part, 1 - core, 0))
    own_tokens = tokens_in.astype(F32)
    _, mod_back = jax.vjp(
        modulated_norm, own_tokens, pick(mod_scale, core, 0)[None], pick(mod_shift, core, 0)[None]
    )
    input_part, scale_grad, shift_grad = mod_back(one_grad[None])
    tokens_grad = pick(self_res_grad.reshape(2, rows, D), core, 0)[None] + input_part
    mod_grad = jnp.concatenate((scale_grad, shift_grad), axis=1)
    mod_grad = (mod_grad + swap_seq(mod_grad)).astype(BF)
    mod_grads = exchange(jnp.broadcast_to(mod_grad, (64, 2 * D)), FSDP)
    mod_wgrad = jnp.einsum("if,ic->fc", noise_cols, mod_grads, preferred_element_type=F32)
    noise_parts = jnp.einsum("ic,fc->if", mod_grads, mod_weight, preferred_element_type=F32)
    noise_grad = exchange(noise_parts, FSDP).reshape(1, D)

    gains_wg = jnp.concatenate((gain_two_grad, gain_three_grad), axis=0).astype(BF)
    gains_wg = jnp.pad(
        gains_wg.reshape(2, 64, 16).transpose(1, 0, 2), ((0, 0), (0, 2), (0, C_TEXT - 16))
    )
    text_pack = jnp.concatenate((text_wg.astype(BF).reshape(64, 12, C_TEXT), gains_wg), axis=1)
    text_pack = text_pack.reshape(4, 2, 4, 32, C_TEXT).transpose(0, 2, 1, 3, 4)
    late_wg = late_kernel(ids, text_pack, qkv_wg, cq_wg, rows_kept, rows_came)
    late_wg, ff_sc = lax.optimization_barrier((late_wg, ff_sc))
    late_sc = zy_scatter(late_wg)

    own, far = pick(ff_sc, xh, 0), pick(ff_sc, 1 - xh, 0)
    ff_g = sum_kernel(own, swap_x(own, xl_pair), swap_x(far, near), swap_x(far, across))
    up_rows = ff_g[:, :C_UP].reshape(2, 16, C_UP)
    up_wgrad, down_wgrad = ff_unpack_kernel(
        ids, pick(up_rows, core, 0), swap_core(pick(up_rows, 1 - core, 0)), ff_g[:, C_UP:]
    )

    own, far = pick(late_sc, xh, 0), pick(late_sc, 1 - xh, 0)
    late_g = late_sum_kernel(own, swap_x(own, xl_pair), swap_x(far, near), swap_x(far, across))
    late_rows = late_g[:, :LATE_ROWS].reshape(2, 16, LATE_ROWS)
    kept_rows = pick(late_rows, core, 0)
    came_rows = swap_core(pick(late_rows, 1 - core, 0))
    qkv_wgrad, cq_wgrad, proj_wgrad, co_wgrad = late_unpack_kernel(
        ids, kept_rows, came_rows, late_g[:, LATE_ROWS:]
    )
    qkv_wgrad = qkv_wgrad.transpose(1, 0, 2)
    lo, hi = C_QKV, C_QKV + C_TEXT
    text_both = in_order(core, kept_rows[:, lo:hi], came_rows[:, lo:hi], 0).astype(F32)
    text_wgrad = text_both[:, :12].reshape(2, 12, 2, 256).transpose(1, 2, 0, 3).reshape(12, 2, 512)
    gains_grad = kept_rows[12:14, lo : lo + 16].astype(F32)

    text_grad = pick(text_part, core, 0) + swap_core(pick(text_part, 1 - core, 0))
    text_grad = text_grad + swap_seq(text_grad)
    return (
        block_out,
        tokens_grad,
        noise_grad,
        text_grad[None],
        mod_wgrad,
        qkv_wgrad,
        proj_wgrad,
        cq_wgrad,
        text_wgrad,
        co_wgrad,
        gains_grad,
        up_wgrad,
        down_wgrad,
    )


def solution(mesh):
    split = Mesh(mesh.devices.reshape(SIZES), AXES)
    in_specs = (
        P(FSDP, "xl", None),
        P(FSDP, None),
        P(FSDP, None, None),
        P(FSDP),
        P(FSDP, None),
        P(FSDP, None, None),
        P(FSDP, None),
        P(FSDP, None),
        P(FSDP, None, "xl"),
        P(FSDP, None),
        P(None, FSDP),
        P(FSDP, None),
        P(FSDP, None),
        P(FSDP, "xl", None),
    )
    out_specs = (
        P(FSDP, "xl", None),
        P(FSDP, "xl", None),
        P(FSDP, None),
        P(FSDP, None, None),
        P(FSDP, None),
        P(FSDP, None, None),
        P(FSDP, None),
        P(FSDP, None),
        P(FSDP, None, "xl"),
        P(FSDP, None),
        P(None, FSDP),
        P(FSDP, None),
        P(FSDP, None),
    )
    return jax.shard_map(
        per_device, mesh=split, in_specs=in_specs, out_specs=out_specs, check_vma=False
    )
```

```python
import jax
import jax.numpy as jnp
from jax import lax
from jax.experimental import pallas as pl
from jax.experimental.pallas import tpu as pltpu
from jax.sharding import Mesh
from jax.sharding import PartitionSpec as P

HEAD_DIM = 64
EPSILON = 1e-06
HIGHEST_PREC = lax.Precision.HIGHEST
NEG_LARGE = -1e30
BF = jnp.bfloat16
F32 = jnp.float32

AXES = ("z", "xh", "y", "core", "xl")
SIZES = (4, 2, 4, 2, 2)
FSDP = ("z", "xh", "y", "core")
RING_X = ("xh", "xl")

D = 1024
FF = 4096
TEXT_W = 768
TXT = 8
CHIPS = 32

C_X = 768
C_QKV, C_CQ, C_TEXT, C_PROJ, C_CO = 1536, 512, 512, 512, 512
TEXT_COLS = (C_QKV + C_CQ, C_QKV + C_CQ + C_TEXT)
C_UP, C_DOWN = 2048, 2048


def rms_norm(tensor):
    return tensor * lax.rsqrt(jnp.mean(tensor * tensor, axis=-1, keepdims=True) + EPSILON)


def modulated_norm(tensor, scale, shift):
    return rms_norm(tensor) * (1.0 + scale[:, None, :]) + shift[:, None, :]


def mm(a, b):
    return jnp.dot(a, b, preferred_element_type=F32)


def mm_nt(a, b):
    return lax.dot_general(a, b, (((1,), (1,)), ((), ())), preferred_element_type=F32)


def mm_tn(a, b):
    return lax.dot_general(a, b, (((0,), (0,)), ((), ())), preferred_element_type=F32)


CHIP_ORDER = [(z, xh, y) for z in range(4) for xh in range(2) for y in range(4)]


def nat(ref):
    return jnp.concatenate([ref[z, y, xh] for z, xh, y in CHIP_ORDER], axis=0)


def store_nat(ref, value):
    for i, (z, xh, y) in enumerate(CHIP_ORDER):
        ref[z, y, xh] = value[32 * i : 32 * i + 32].astype(ref.dtype)


def norm_of(x):
    inv = lax.rsqrt(jnp.mean(x * x, axis=-1, keepdims=True) + EPSILON)
    return x * inv, inv


def norm_grad(unit, inv, dh_w):
    return (dh_w - unit * jnp.mean(dh_w * unit, axis=-1, keepdims=True)) * inv


def call(body, outs, ins, scratch=(), specs=None, out_specs=None, grid=None, prefetch=0):
    whole = pl.BlockSpec(memory_space=pltpu.VMEM)
    return pl.pallas_call(
        body,
        out_shape=outs,
        grid_spec=pltpu.PrefetchScalarGridSpec(
            num_scalar_prefetch=prefetch,
            grid=grid or (),
            in_specs=specs or [whole] * len(ins),
            out_specs=out_specs or [whole] * len(outs),
            scratch_shapes=list(scratch),
        ),
        compiler_params=pltpu.CompilerParams(vmem_limit_bytes=60 * 1024 * 1024),
    )(*ins)


def shape(dims, dtype):
    return jax.ShapeDtypeStruct(dims, dtype)


WHOLE = pl.BlockSpec(memory_space=pltpu.VMEM)
SMEM = pl.BlockSpec(memory_space=pltpu.SMEM)


def cols_spec(block, width=512):
    return pl.BlockSpec((4, 4, 2, 32, width), lambda i: (0, 0, 0, 0, block))


def fixed(dims):
    return pl.BlockSpec(dims, lambda i: (0,) * len(dims))


def qkv_body(tok, scale, shift, wq, wk, wv, n1_out, q_out, kv_out):
    for b in range(2):
        r = slice(128 * b, 128 * b + 128)
        unit, _ = norm_of(tok[r].astype(F32))
        n1_out[r] = (unit * (1.0 + scale[b : b + 1]) + shift[b : b + 1]).astype(BF)
    n1 = n1_out[...]
    q_out[...] = mm(n1, nat(wq)).astype(BF)
    kv_out[:, :512] = mm(n1, nat(wk)).astype(BF)
    kv_out[:, 512:] = mm(n1, nat(wv)).astype(BF)


def qkv_kernel(tok, scale, shift, full):
    return call(
        qkv_body,
        [shape((256, D), BF), shape((256, 512), BF), shape((256, D), BF)],
        (tok, scale, shift, full, full, full),
        specs=[fixed((256, D)), fixed((2, D)), fixed((2, D)), cols_spec(0), cols_spec(1), cols_spec(2)],
        out_specs=[fixed((256, D)), fixed((256, 512)), fixed((256, D))],
        grid=(1,),
    )


def head_cols(h):
    return slice(64 * h, 64 * h + 64)


def self_probs(q, k):
    scores = mm_nt(q, k) * HEAD_DIM ** (-0.5)
    e = jnp.exp(scores - jnp.max(scores, axis=-1, keepdims=True))
    return e * (1.0 / jnp.sum(e, axis=-1, keepdims=True))


def attend_body(q, kv, kv_far, proj_w, att_out, part_out):
    for b in range(2):
        r = slice(128 * b, 128 * b + 128)
        for h in range(8):
            k = jnp.concatenate((kv[r, head_cols(h)], kv_far[r, head_cols(h)]), axis=0)
            v = jnp.concatenate((kv[r, head_cols(8 + h)], kv_far[r, head_cols(8 + h)]), axis=0)
            p = self_probs(q[r, head_cols(h)], k).astype(BF)
            att_out[r, head_cols(h)] = mm(p, v).astype(BF)
    part_out[...] = mm(att_out[...], proj_w[...])


def attend_kernel(q, kv, kv_far, proj_w):
    return call(
        attend_body, [shape((256, 512), BF), shape((256, D), F32)], (q, kv, kv_far, proj_w)
    )


def spread_heads(rows8):
    tall = jnp.concatenate([rows8.astype(F32)] * 16, axis=0)
    row = lax.broadcasted_iota(jnp.int32, tall.shape, 0) // 8
    col = lax.broadcasted_iota(jnp.int32, tall.shape, 1) // 64
    return jnp.where(row == col, tall, 0.0).astype(BF)


def fold_heads(tall):
    row = lax.broadcasted_iota(jnp.int32, tall.shape, 0) // 8
    col = lax.broadcasted_iota(jnp.int32, tall.shape, 1) // 64
    kept = jnp.where(row == col, tall, 0.0)
    total = kept[0:8]
    for h in range(1, 8):
        total = total + kept[8 * h : 8 * h + 8]
    return total


def by_eights(op, x):
    lane = lax.broadcasted_iota(jnp.int32, x.shape, 1)
    for step in (1, 2, 4):
        up = pltpu.roll(x, x.shape[1] - step, 1)
        down = pltpu.roll(x, step, 1)
        x = op(x, jnp.where((lane & step) == 0, up, down))
    return x


def cross_probs(q, keys, length):
    scores = mm_nt(q, keys) * HEAD_DIM ** (-0.5)
    lane = lax.broadcasted_iota(jnp.int32, scores.shape, 1)
    scores = jnp.where((lane & 7) < length, scores, NEG_LARGE)
    e = jnp.exp(scores - by_eights(jnp.maximum, scores))
    return e * (1.0 / by_eights(jnp.add, e))


def cross_body(
    tok, part, part_far, gains, cq_w, text_kv, lens, co_w, res_out, n2_out, cq_out, att_out, part_out
):
    res_out[...] = tok[...].astype(F32) + (part[...] + part_far[...])
    unit, _ = norm_of(res_out[...])
    n2_out[...] = (unit * gains[0:1]).astype(BF)
    cq_out[...] = mm(n2_out[...], nat(cq_w)).astype(BF)
    for b in range(2):
        r = slice(128 * b, 128 * b + 128)
        keys = spread_heads(text_kv[b, :, 0:512])
        vals = spread_heads(text_kv[b, :, 512:1024])
        p = cross_probs(cq_out[r], keys, lens[b]).astype(BF)
        att_out[r] = mm(p, vals).astype(BF)
    part_out[...] = mm(att_out[...], co_w[...])


def cross_kernel(tok, part, part_far, gains, full, text_kv, lens, co_w):
    f = fixed
    return call(
        cross_body,
        [
            shape((256, D), F32),
            shape((256, D), BF),
            shape((256, 512), BF),
            shape((256, 512), BF),
            shape((256, D), F32),
        ],
        (tok, part, part_far, gains, full, text_kv, lens, co_w),
        specs=[
            f((256, D)),
            f((256, D)),
            f((256, D)),
            f((2, D)),
            cols_spec(3),
            f((2, 8, D)),
            SMEM,
            f((512, D)),
        ],
        out_specs=[f((256, D)), f((256, D)), f((256, 512)), f((256, 512)), f((256, D))],
        grid=(1,),
    )


GELU_A = 0.7978845608028654
GELU_B = 0.044715


def ff_copies(g_up, g_down, grad, sem, i):
    at = pl.ds(pl.multiple_of(i * 512, 512), 512)
    return (
        pltpu.make_async_copy(g_up.at[i], grad.at[:, :, :, :, at], sem.at[0, i]),
        pltpu.make_async_copy(g_down.at[i], grad.at[i, :, :, :, C_UP:], sem.at[1, i]),
    )


def ff_body(
    ids, res, part, part_far, gains, og, up, down, down_far, rest,
    res_out, grad_out, three_out, down_out, n3, n3_t, g_up, g_down, sem,
):
    i = pl.program_id(0)

    @pl.when(i == 0)
    def _():
        res_out[...] = res[...] + (part[...] + part_far[...])
        unit, _ = norm_of(res_out[...])
        low = (unit * gains[1:2]).astype(BF)
        n3[...] = low
        n3_t[...] = low.T

    up_w = nat(up)
    low_xh = ids[1] < 2
    own, far = down[0].reshape(256, C_X), down_far[0].reshape(256, C_X)
    left = jnp.concatenate((jnp.where(low_xh, own, far), jnp.where(low_xh, far, own)), axis=0)
    k = D - C_X
    right = jnp.concatenate(
        [
            rest[0, y, xh, :, k * h : k * h + k]
            for xh in range(2)
            for y in range(4)
            for h in range(2)
        ],
        axis=0,
    )
    down_w = jnp.concatenate((left, right), axis=1)
    pre = mm(n3[...], up_w)
    t = jnp.tanh(GELU_A * (pre + GELU_B * (pre * pre * pre)))
    act = (0.5 * pre * (1.0 + t)).astype(BF)
    slope = 0.5 * (1.0 + t) + 0.5 * pre * (1.0 - t * t) * (
        GELU_A * (1.0 + 3.0 * GELU_B * (pre * pre))
    )
    pre_grad = (mm_nt(og[...], down_w) * slope).astype(BF)
    up_wg = mm(n3_t[...], pre_grad).astype(BF)
    for j, (z, xh, y) in enumerate(CHIP_ORDER):
        g_up[i, z, y, xh] = up_wg[32 * j : 32 * j + 32]
    down_wg = mm_tn(act, og[...]).astype(BF)
    j = 0
    for xh in range(2):
        for y in range(4):
            for h in range(2):
                g_down[i, y, xh, :, D * h : D * h + D] = down_wg[32 * j : 32 * j + 32]
                j += 1
    for copy in ff_copies(g_up, g_down, grad_out, sem, i):
        copy.start()
    down_part = mm(act, down_w)
    three_part = mm_nt(pre_grad, up_w)

    @pl.when(i == 0)
    def _():
        down_out[...] = down_part
        three_out[...] = three_part

    @pl.when(i > 0)
    def _():
        down_out[...] += down_part
        three_out[...] += three_part

    @pl.when(i == 3)
    def _():
        for k in range(4):
            for copy in ff_copies(g_up, g_down, grad_out, sem, k):
                copy.wait()


def ff_kernel(ids, res, part, part_far, gains, og, down, down_far, full):
    f = fixed
    return call(
        ff_body,
        [
            shape((256, D), F32),
            shape((4, 4, 2, 32, C_UP + C_DOWN), BF),
            shape((256, D), F32),
            shape((256, D), F32),
        ],
        (ids, res, part, part_far, gains, og, full, down, down_far, full),
        scratch=[
            pltpu.VMEM((256, D), BF),
            pltpu.VMEM((D, 256), BF),
            pltpu.VMEM((4, 4, 4, 2, 32, 512), BF),
            pltpu.VMEM((4, 4, 2, 32, 2048), BF),
            pltpu.SemaphoreType.DMA((2, 4)),
        ],
        specs=[
            SMEM,
            f((256, D)),
            f((256, D)),
            f((256, D)),
            f((2, D)),
            f((256, D)),
            pl.BlockSpec((4, 4, 2, 32, 512), lambda i: (0, 0, 0, 0, i)),
            pl.BlockSpec((1, 4, 2, 32, C_X), lambda i: (i, 0, 0, 0, 0)),
            pl.BlockSpec((1, 4, 2, 32, C_X), lambda i: (i, 0, 0, 0, 0)),
            pl.BlockSpec((1, 4, 2, 32, 512), lambda i: (i, 0, 0, 0, 4)),
        ],
        out_specs=[f((256, D)), pl.BlockSpec(memory_space=pl.ANY), f((256, D)), f((256, D))],
        grid=(4,),
    )

def cross_back_body(
    part, part_far, res, og, gains, att, cq, n2, text_kv, lens, co_w, cq_w,
    grad_out, gain_out, co_out, cqw_out, text_out, two_out, ag, dq,
):
    unit, inv = norm_of(res[...])
    three = part[...] + part_far[...]
    gain_out[...] = jnp.sum(three * unit, axis=0, keepdims=True)
    grad_out[...] = og[...].astype(F32) + norm_grad(unit, inv, three * gains[1:2])
    low = grad_out[...].astype(BF)
    co_out[...] = mm_tn(att[...], low).astype(BF)
    ag[...] = mm_nt(low, co_w[...]).astype(BF)
    for b in range(2):
        r = slice(128 * b, 128 * b + 128)
        keys = spread_heads(text_kv[b, :, 0:512])
        vals = spread_heads(text_kv[b, :, 512:1024])
        p = cross_probs(cq[r], keys, lens[b])
        dp = mm_nt(ag[r], vals)
        ds = (p * (dp - by_eights(jnp.add, p * dp))).astype(BF)
        dq[r] = (mm(ds, keys) * HEAD_DIM ** (-0.5)).astype(BF)
        text_out[b, :, 0:512] = fold_heads(mm_tn(ds, cq[r])) * HEAD_DIM ** (-0.5)
        text_out[b, :, 512:1024] = fold_heads(mm_tn(p.astype(BF), ag[r]))
    store_nat(cqw_out, mm_tn(n2[...], dq[...]))
    two_out[...] = mm_nt(dq[...], nat(cq_w))


def cross_back_kernel(part, part_far, res, og, gains, att, cq, n2, text_kv, lens, co_w, full):
    f = fixed
    return call(
        cross_back_body,
        [
            shape((256, D), F32),
            shape((1, D), F32),
            shape((512, D), BF),
            shape((4, 4, 2, 32, 512), BF),
            shape((2, 8, D), F32),
            shape((256, D), F32),
        ],
        (part, part_far, res, og, gains, att, cq, n2, text_kv, lens, co_w, full),
        scratch=[pltpu.VMEM((256, 512), BF), pltpu.VMEM((256, 512), BF)],
        specs=[
            f((256, D)),
            f((256, D)),
            f((256, D)),
            f((256, D)),
            f((2, D)),
            f((256, 512)),
            f((256, 512)),
            f((256, D)),
            f((2, 8, D)),
            SMEM,
            f((512, D)),
            cols_spec(3),
        ],
        out_specs=[
            f((256, D)),
            f((1, D)),
            f((512, D)),
            f((4, 4, 2, 32, 512)),
            f((2, 8, D)),
            f((256, D)),
        ],
        grid=(1,),
    )


def pair_slices(i):
    rows = pl.ds(pl.multiple_of(i // 4 * 128, 128), 128)
    cols = pl.ds(pl.multiple_of(i % 4 * 128, 128), 128)
    vals = pl.ds(pl.multiple_of(i % 4 * 128 + 512, 128), 128)
    return rows, cols, vals


def self_back_body(
    part, part_far, res, res_grad, gains, att, q, kv, kv_far, proj_w,
    grad_out, gain_out, proj_out, dq_out, dkv_out, dfar_out, ag,
):
    unit, inv = norm_of(res[...])
    two = part[...] + part_far[...]
    gain_out[...] = jnp.sum(two * unit, axis=0, keepdims=True)
    grad_out[...] = res_grad[...] + norm_grad(unit, inv, two * gains[0:1])
    low = grad_out[...].astype(BF)
    proj_out[...] = mm_tn(att[...], low).astype(BF)
    ag[...] = mm_nt(low, proj_w[...]).astype(BF)
    factor = HEAD_DIM ** (-0.5)

    def step(i, carry):
        r, kc, vc = pair_slices(i)
        q2, g2 = q[r, kc], ag[r, kc]
        k2 = jnp.concatenate((kv[r, kc], kv_far[r, kc]), axis=0)
        v2 = jnp.concatenate((kv[r, vc], kv_far[r, vc]), axis=0)
        dq, dk, dv = [], [], []
        for h in (slice(0, 64), slice(64, 128)):
            k = k2[:, h]
            qh, gh = q2[:, h], g2[:, h]
            p = self_probs(qh, k)
            dp = mm_nt(gh, v2[:, h])
            ds = (p * (dp - jnp.sum(p * dp, axis=-1, keepdims=True))).astype(BF)
            dq.append(mm(ds, k))
            dk.append(mm_tn(ds, qh))
            dv.append(mm_tn(p.astype(BF), gh))
        dk = jnp.concatenate(dk, axis=1) * factor
        dv = jnp.concatenate(dv, axis=1)
        dq_out[r, kc] = (jnp.concatenate(dq, axis=1) * factor).astype(BF)
        dkv_out[r, kc] = dk[:128]
        dkv_out[r, vc] = dv[:128]
        dfar_out[r, kc] = dk[128:].astype(BF)
        dfar_out[r, vc] = dv[128:].astype(BF)
        return carry

    lax.fori_loop(0, 8, step, 0)


def self_back_kernel(part, part_far, res, res_grad, gains, att, q, kv, kv_far, proj_w):
    return call(
        self_back_body,
        [
            shape((256, D), F32),
            shape((1, D), F32),
            shape((512, D), BF),
            shape((256, 512), BF),
            shape((256, D), F32),
            shape((256, D), BF),
        ],
        (part, part_far, res, res_grad, gains, att, q, kv, kv_far, proj_w),
        scratch=[pltpu.VMEM((256, 512), BF)],
    )


def qkv_back_body(dq, dkv, dfar, n1, wq, wk, wv, wg_out, part_out):
    n = n1[...]
    dqv = dq[...]
    dkvv = (dkv[...] + dfar[...].astype(F32)).astype(BF)
    grads = (dqv, dkvv[:, :512], dkvv[:, 512:])
    total = None
    for i, (g, w) in enumerate(zip(grads, (wq, wk, wv))):
        wg = mm_tn(n, g).astype(BF)
        for j, (z, xh, y) in enumerate(CHIP_ORDER):
            wg_out[z, y, xh, :, 512 * i : 512 * i + 512] = wg[32 * j : 32 * j + 32]
        t = mm_nt(g, nat(w))
        total = t if total is None else total + t
    part_out[...] = total


def qkv_back_kernel(dq, dkv, dfar, n1, full):
    f = fixed
    return call(
        qkv_back_body,
        [shape((4, 4, 2, 32, 1536), BF), shape((256, D), F32)],
        (dq, dkv, dfar, n1, full, full, full),
        specs=[
            f((256, 512)),
            f((256, D)),
            f((256, D)),
            f((256, D)),
            cols_spec(0),
            cols_spec(1),
            cols_spec(2),
        ],
        out_specs=[f((4, 4, 2, 32, 1536)), f((256, D))],
        grid=(1,),
    )


def sum_body(*refs):
    total = refs[0][...].astype(F32)
    for r in refs[1:-1]:
        total = total + r[...].astype(F32)
    refs[-1][...] = total.astype(refs[-1].dtype)


def sum_kernel(*pieces):
    return call(sum_body, [shape(pieces[0].shape, BF)], pieces)[0]


LATE = C_QKV + C_TEXT + C_CQ + C_PROJ + C_CO
LATE_ROWS = LATE - C_PROJ - C_CO


def late_body(ids, text, qkv, cq, kept, came, out):
    out[:, :, :, :, :C_QKV] = qkv[...]
    at = C_QKV + C_TEXT
    out[:, :, :, :, C_QKV:at] = text[...]
    out[:, :, :, :, at : at + C_CQ] = cq[...]
    first = ids[0] == 0
    a, b = kept[...], came[...]
    out[:2, :, :, :, LATE_ROWS:] = jnp.where(first, a, b)
    out[2:, :, :, :, LATE_ROWS:] = jnp.where(first, b, a)


def late_kernel(ids, text, qkv, cq, kept, came):
    return call(
        late_body,
        [shape((4, 4, 2, 32, LATE), BF)],
        (ids, text, qkv, cq, kept, came),
        specs=[SMEM, *[WHOLE] * 5],
    )[0]


def late_sum_body(own, a, b, e, out):
    near = a[...].astype(F32) + b[...].astype(F32)
    row = lax.broadcasted_iota(jnp.int32, near.shape, 0) % 16
    col = lax.broadcasted_iota(jnp.int32, near.shape, 1)
    text = (col >= C_QKV) & (col < C_QKV + C_TEXT)
    near = jnp.where((row < 12) & text, 0.0, near)
    out[...] = (own[...].astype(F32) + e[...].astype(F32) + near).astype(BF)


def late_sum_kernel(own, a, b, e):
    return call(late_sum_body, [shape((32, LATE), BF)], (own, a, b, e))[0]


def rows_body(core, kept, came, proj_out, co_out):
    first = core[0] == 0
    i = 0
    for z in range(2):
        for xh in range(2):
            for y in range(4):
                a, b = kept[z, y, xh], came[z, y, xh]
                for bit in range(2):
                    t = jnp.where(first, a, b) if bit == 0 else jnp.where(first, b, a)
                    for out, c in ((proj_out, 0), (co_out, 512)):
                        out[16 * i : 16 * i + 16, :512] = t[:16, c : c + 512]
                        out[16 * i : 16 * i + 16, 512:] = t[16:, c : c + 512]
                    i += 1


def rows_kernel(core, kept, came):
    return call(
        rows_body,
        [shape((512, D), BF), shape((512, D), BF)],
        (core, kept, came),
        specs=[SMEM, WHOLE, WHOLE],
    )


def rows_back_body(core, proj_wg, co_wg, kept_out, sent_out):
    first = core[0] == 0
    i = 0
    for z in range(2):
        for xh in range(2):
            for y in range(4):
                t = []
                for bit in range(2):
                    r = slice(16 * i, 16 * i + 16)
                    t.append(
                        jnp.concatenate(
                            (
                                jnp.concatenate((proj_wg[r, :512], proj_wg[r, 512:]), axis=0),
                                jnp.concatenate((co_wg[r, :512], co_wg[r, 512:]), axis=0),
                            ),
                            axis=1,
                        )
                    )
                    i += 1
                kept_out[z, y, xh] = jnp.where(first, t[0], t[1])
                sent_out[z, y, xh] = jnp.where(first, t[1], t[0])


def rows_back_kernel(core, proj_wg, co_wg):
    dims = shape((2, 4, 2, 32, D), BF)
    return call(
        rows_back_body, [dims, dims], (core, proj_wg, co_wg), specs=[SMEM, WHOLE, WHOLE]
    )


def ff_unpack_body(ids, mine, came, down, up_out, down_out):
    first = ids[0] == 0
    a, b = mine[...].astype(F32), came[...].astype(F32)
    parts = (jnp.where(first, a, b), jnp.where(first, b, a))
    for i in range(32):
        for c in range(2):
            to = 128 * i + 64 * c
            up_out[:, to : to + 64] = parts[c][:, 64 * i : 64 * i + 64]
    down_out[:32] = down[:, :D].astype(F32)
    down_out[32:] = down[:, D:].astype(F32)


def ff_unpack_kernel(ids, mine, came, down):
    return call(
        ff_unpack_body,
        [shape((16, FF), F32), shape((64, D), F32)],
        (ids, mine, came, down),
        specs=[SMEM, WHOLE, WHOLE, WHOLE],
    )


def late_unpack_body(ids, mine, came, rows, qkv_out, cq_out, proj_out, co_out):
    first = ids[0] == 0
    a, b = mine[...].astype(F32), came[...].astype(F32)
    parts = (jnp.where(first, a, b), jnp.where(first, b, a))
    for c in range(2):
        to = slice(512 * c, 512 * c + 512)
        for i in range(3):
            qkv_out[i, :, to] = parts[c][:, 512 * i : 512 * i + 512]
        cq_out[:, to] = parts[c][:, LATE_ROWS - 512 : LATE_ROWS]
    for i, out in enumerate((proj_out, co_out)):
        for h in range(2):
            out[:, 512 * h : 512 * h + 512] = rows[
                16 * h : 16 * h + 16, 512 * i : 512 * i + 512
            ].astype(F32)


def late_unpack_kernel(ids, mine, came, rows):
    return call(
        late_unpack_body,
        [shape((3, 16, D), F32), shape((16, D), F32), shape((16, D), F32), shape((16, D), F32)],
        (ids, mine, came, rows),
        specs=[SMEM, WHOLE, WHOLE, WHOLE],
    )


def swap_core(value):
    return lax.ppermute(value, "core", [(0, 1), (1, 0)])


def swap_seq(value):
    return lax.ppermute(value, "xl", [(0, 1), (1, 0)])


def swap_x(value, pairs):
    return lax.ppermute(value, RING_X, [p for a, b in pairs for p in ((a, b), (b, a))])


def in_order(index, mine, other, axis):
    first = jnp.where(index == 0, mine, other)
    second = jnp.where(index == 0, other, mine)
    return jnp.stack((first, second), axis=axis)


def join(index, mine, other, axis):
    first = jnp.where(index == 0, mine, other)
    second = jnp.where(index == 0, other, mine)
    return jnp.concatenate((first, second), axis=axis)


def pick(value, index, axis):
    return jnp.where(
        index == 0, lax.index_in_dim(value, 0, axis, False), lax.index_in_dim(value, 1, axis, False)
    )


def gather_chips(pair):
    full = lax.all_gather(pair, ("z", "y"), axis=0, tiled=False)
    return full.reshape(4, 4, *pair.shape)


def ring(value, axis, size, step):
    return lax.ppermute(value, axis, [(i, (i + step) % size) for i in range(size)])


def exchange(value, axes):
    return lax.all_to_all(value, axes, 0, 0, tiled=True)


def zy_scatter(full):
    cols = full.shape[-1]
    part = lax.psum_scatter(full.reshape(D, cols), ("z", "y"), scatter_dimension=0, tiled=True)
    return part.reshape(2, 32, cols)


def halves_as_rows(value):
    k = value.shape[-1] // 2
    return jnp.concatenate((value[:, :k], value[:, k:]), axis=0)


def per_device(
    tokens_in,
    noise_emb,
    text_emb,
    prompt_len,
    mod_weight,
    qkv_weight,
    proj_weight,
    cq_weight,
    text_weight,
    co_weight,
    norm_gains,
    up_weight,
    down_weight,
    out_grad,
):
    core = lax.axis_index("core")
    xh = lax.axis_index("xh")
    xl = lax.axis_index("xl")
    rows = tokens_in.shape[1]

    misc = jnp.concatenate(
        (
            jnp.pad(text_emb[0], ((0, 0), (0, D - TEXT_W))),
            jnp.broadcast_to(prompt_len.astype(BF)[:, None], (8, D)),
        ),
        axis=0,
    )
    mine = jnp.concatenate((tokens_in[0], out_grad[0], misc), axis=0)
    both = in_order(core, mine, swap_core(mine), 0)
    tok = both[:, :rows].reshape(256, D)
    og = both[:, rows : 2 * rows].reshape(256, D)
    text = both[:, 2 * rows : 2 * rows + 8, :TEXT_W]
    lens = both[:, 2 * rows + 8, 0].astype(jnp.int32)

    def side(which):
        up = pick(up_weight.reshape(16, 32, 2, 64), which, 2).reshape(16, C_UP)
        qkv = pick(qkv_weight.reshape(16, 3, 2, 512), which, 2).reshape(16, C_QKV)
        cq = pick(cq_weight.reshape(16, 2, 512), which, 1)
        txt = pick(text_weight.reshape(12, 2, 2, 256), which, 2).reshape(12, C_TEXT)
        gains = jnp.pad(norm_gains, ((0, 2), (0, C_TEXT - 16)))
        return jnp.concatenate((qkv, cq, jnp.concatenate((txt, gains), axis=0), up), axis=1)

    shared = join(core, side(core), swap_core(side(1 - core)), 0)
    first = jnp.concatenate(
        (
            shared[:, : C_QKV + C_CQ + C_TEXT],
            halves_as_rows(proj_weight),
            halves_as_rows(co_weight),
        ),
        axis=1,
    )
    second = jnp.concatenate(
        (shared[:, C_QKV + C_CQ + C_TEXT :], down_weight[:32, C_X:], down_weight[32:, C_X:]), axis=1
    )
    near, xl_pair, across = ((0, 3), (1, 2)), ((0, 1), (2, 3)), ((0, 2), (1, 3))
    lo, hi = TEXT_COLS
    first_far = swap_x(first, ((0, 3), (1, 2)))
    text_far = swap_x(first[:, lo:hi], ((0, 2), (1, 3)))
    second, first_far = lax.optimization_barrier((second, first_far))
    first_far = jnp.concatenate((first_far[:, :lo], text_far, first_far[:, hi:]), axis=1)
    down_halves = down_weight.reshape(2, 32, D)
    first_pair = jnp.concatenate(
        (in_order(xh, first, first_far, 0), down_halves[..., :C_X]), axis=2
    )
    full_one = gather_chips(first_pair)
    full_two = gather_chips(in_order(xh, second, swap_x(second, near), 0))
    full_one, down_own = lax.optimization_barrier((full_one, full_one[..., -C_X:]))
    down_far = swap_x(down_own, near)

    text_rows = full_one[..., lo:hi].transpose(0, 2, 1, 3, 4)
    text_rows = text_rows.reshape(64, 16, C_TEXT)
    text_w = text_rows[:, :12].reshape(TEXT_W, 2, 256)
    gains = text_rows[:, 12:14, :16].transpose(1, 0, 2).reshape(2, D).astype(F32)
    core_id = core.astype(jnp.int32)[None]
    y_id = lax.axis_index("y")
    ids = jnp.stack([core, 2 * xh + xl, y_id, xl]).astype(jnp.int32)

    noise_cols = exchange(noise_emb.reshape(64, 16), FSDP)
    half = pick(mod_weight.reshape(16, 2, D), xl, 1)
    mod_parts = jnp.dot(noise_cols, half, preferred_element_type=F32)
    mod_part = jnp.sum(exchange(mod_parts, FSDP), axis=0, keepdims=True)
    mod_own = join(xl, mod_part, swap_seq(mod_part), 1)
    mod_all = in_order(core, mod_own, swap_core(mod_own), 0).reshape(2, 2, D)
    mod_scale, mod_shift = mod_all[:, 0], mod_all[:, 1]
    normed_one, queries, kv_own = qkv_kernel(tok, mod_scale, mod_shift, full_one)
    kv_far = swap_seq(kv_own)
    later, kv_own = lax.optimization_barrier((full_one, kv_own))
    halves = later[..., hi : hi + 2 * 512].reshape(2, 2, 4, 2, 32, D)
    kept = pick(halves, core, 0)
    proj_w, co_w = rows_kernel(core_id, kept, swap_core(pick(halves, 1 - core, 0)))
    attended, proj_part = attend_kernel(queries, kv_own, kv_far, proj_w)
    proj_part, down_far = lax.optimization_barrier((proj_part, down_far))
    text_own = jnp.einsum("ijt,tcn->ijcn", text, text_w, preferred_element_type=F32).astype(BF)
    text_xl = in_order(xl, text_own, swap_seq(text_own), 0)
    text_kv = join(core, pick(text_xl, core, 0), swap_core(pick(text_xl, 1 - core, 0)), 3)
    text_kv = text_kv.reshape(2, TXT, D)
    after_self, normed_two, cross_q, cross_att, co_part = cross_kernel(
        tok, proj_part, swap_core(proj_part), gains, full_one, text_kv, lens, co_w
    )
    after_cross, ff_wg, three_part, down_part = ff_kernel(
        ids, after_self, co_part, swap_core(co_part), gains, og, down_own, down_far, full_two
    )
    ff_sc = zy_scatter(ff_wg)
    down_part = down_part.reshape(2, rows, D)
    down_own = pick(down_part, core, 0) + swap_core(pick(down_part, 1 - core, 0))
    block_out = (pick(after_cross.reshape(2, rows, D), core, 0) + down_own).astype(BF)[None]

    cross_res_grad, gain_three_grad, co_wg, cq_wg, text_sum, two_part = cross_back_kernel(
        three_part, swap_core(three_part), after_cross, og, gains, cross_att, cross_q,
        normed_two, text_kv, lens, co_w, full_one,
    )
    self_res_grad, gain_two_grad, proj_wg, dq, dkv, dkv_far = self_back_kernel(
        two_part, swap_core(two_part), after_self, cross_res_grad, gains, attended, queries,
        kv_own, kv_far, proj_w,
    )
    rows_kept, rows_sent = rows_back_kernel(core_id, proj_wg, co_wg)
    dkv_came = swap_seq(dkv_far)
    rows_came = swap_core(rows_sent)
    qkv_wg, one_part = qkv_back_kernel(dq, dkv, dkv_came, normed_one, full_one)

    text_sum = (text_sum + swap_seq(text_sum.astype(BF)).astype(F32)).astype(BF)
    text_quarters = text_sum.reshape(2, TXT, 2, 2, 256)
    text_kept = pick(text_quarters, core, 3)
    text_came = swap_core(pick(text_quarters, 1 - core, 3))
    text_kv_grad = jnp.where(core == xl, text_kept, text_came)
    text_wg = jnp.einsum("ijt,ijcn->tcn", text, text_kv_grad, preferred_element_type=F32)
    text_part = jnp.einsum("ijcn,tcn->ijt", text_kv_grad, text_w, preferred_element_type=F32)

    one_part = one_part.reshape(2, rows, D)
    one_grad = pick(one_part, core, 0) + swap_core(pick(one_part, 1 - core, 0))
    own_tokens = tokens_in.astype(F32)
    _, mod_back = jax.vjp(
        modulated_norm, own_tokens, pick(mod_scale, core, 0)[None], pick(mod_shift, core, 0)[None]
    )
    input_part, scale_grad, shift_grad = mod_back(one_grad[None])
    tokens_grad = pick(self_res_grad.reshape(2, rows, D), core, 0)[None] + input_part
    mod_grad = jnp.concatenate((scale_grad, shift_grad), axis=1)
    mod_grad = (mod_grad + swap_seq(mod_grad)).astype(BF)
    mod_grads = exchange(jnp.broadcast_to(mod_grad, (64, 2 * D)), FSDP)
    mod_wgrad = jnp.einsum("if,ic->fc", noise_cols, mod_grads, preferred_element_type=F32)
    noise_parts = jnp.einsum("ic,fc->if", mod_grads, mod_weight, preferred_element_type=F32)
    noise_grad = exchange(noise_parts, FSDP).reshape(1, D)

    gains_wg = jnp.concatenate((gain_two_grad, gain_three_grad), axis=0).astype(BF)
    gains_wg = jnp.pad(
        gains_wg.reshape(2, 64, 16).transpose(1, 0, 2), ((0, 0), (0, 2), (0, C_TEXT - 16))
    )
    text_pack = jnp.concatenate((text_wg.astype(BF).reshape(64, 12, C_TEXT), gains_wg), axis=1)
    text_pack = text_pack.reshape(4, 2, 4, 32, C_TEXT).transpose(0, 2, 1, 3, 4)
    late_wg = late_kernel(ids, text_pack, qkv_wg, cq_wg, rows_kept, rows_came)
    late_wg, ff_sc = lax.optimization_barrier((late_wg, ff_sc))
    late_sc = zy_scatter(late_wg)

    own, far = pick(ff_sc, xh, 0), pick(ff_sc, 1 - xh, 0)
    ff_g = sum_kernel(own, swap_x(own, xl_pair), swap_x(far, near), swap_x(far, across))
    up_rows = ff_g[:, :C_UP].reshape(2, 16, C_UP)
    up_wgrad, down_wgrad = ff_unpack_kernel(
        ids, pick(up_rows, core, 0), swap_core(pick(up_rows, 1 - core, 0)), ff_g[:, C_UP:]
    )

    own, far = pick(late_sc, xh, 0), pick(late_sc, 1 - xh, 0)
    late_g = late_sum_kernel(own, swap_x(own, xl_pair), swap_x(far, near), swap_x(far, across))
    late_rows = late_g[:, :LATE_ROWS].reshape(2, 16, LATE_ROWS)
    kept_rows = pick(late_rows, core, 0)
    came_rows = swap_core(pick(late_rows, 1 - core, 0))
    qkv_wgrad, cq_wgrad, proj_wgrad, co_wgrad = late_unpack_kernel(
        ids, kept_rows, came_rows, late_g[:, LATE_ROWS:]
    )
    qkv_wgrad = qkv_wgrad.transpose(1, 0, 2)
    lo, hi = C_QKV, C_QKV + C_TEXT
    text_both = in_order(core, kept_rows[:, lo:hi], came_rows[:, lo:hi], 0).astype(F32)
    text_wgrad = text_both[:, :12].reshape(2, 12, 2, 256).transpose(1, 2, 0, 3).reshape(12, 2, 512)
    gains_grad = kept_rows[12:14, lo : lo + 16].astype(F32)

    text_grad = pick(text_part, core, 0) + swap_core(pick(text_part, 1 - core, 0))
    text_grad = text_grad + swap_seq(text_grad)
    return (
        block_out,
        tokens_grad,
        noise_grad,
        text_grad[None],
        mod_wgrad,
        qkv_wgrad,
        proj_wgrad,
        cq_wgrad,
        text_wgrad,
        co_wgrad,
        gains_grad,
        up_wgrad,
        down_wgrad,
    )


def solution(mesh):
    split = Mesh(mesh.devices.reshape(SIZES), AXES)
    in_specs = (
        P(FSDP, "xl", None),
        P(FSDP, None),
        P(FSDP, None, None),
        P(FSDP),
        P(FSDP, None),
        P(FSDP, None, None),
        P(FSDP, None),
        P(FSDP, None),
        P(FSDP, None, "xl"),
        P(FSDP, None),
        P(None, FSDP),
        P(FSDP, None),
        P(FSDP, None),
        P(FSDP, "xl", None),
    )
    out_specs = (
        P(FSDP, "xl", None),
        P(FSDP, "xl", None),
        P(FSDP, None),
        P(FSDP, None, None),
        P(FSDP, None),
        P(FSDP, None, None),
        P(FSDP, None),
        P(FSDP, None),
        P(FSDP, None, "xl"),
        P(FSDP, None),
        P(None, FSDP),
        P(FSDP, None),
        P(FSDP, None),
    )
    return jax.shard_map(
        per_device, mesh=split, in_specs=in_specs, out_specs=out_specs, check_vma=False
    )
```

```python
import jax
import jax.numpy as jnp
from jax import lax
from jax.experimental import pallas as pl
from jax.experimental.pallas import tpu as pltpu
from jax.sharding import Mesh
from jax.sharding import PartitionSpec as P

HEAD_DIM = 64
EPSILON = 1e-06
HIGHEST_PREC = lax.Precision.HIGHEST
NEG_LARGE = -1e30
BF = jnp.bfloat16
F32 = jnp.float32

AXES = ("z", "xh", "y", "core", "xl")
SIZES = (4, 2, 4, 2, 2)
FSDP = ("z", "xh", "y", "core")
RING_X = ("xh", "xl")

D = 1024
FF = 4096
TEXT_W = 768
TXT = 8
CHIPS = 32

C_X = 768
C_QKV, C_CQ, C_TEXT, C_PROJ, C_CO = 1536, 512, 512, 512, 512
TEXT_COLS = (C_QKV + C_CQ, C_QKV + C_CQ + C_TEXT)
C_UP, C_DOWN = 2048, 2048


def rms_norm(tensor):
    return tensor * lax.rsqrt(jnp.mean(tensor * tensor, axis=-1, keepdims=True) + EPSILON)


def modulated_norm(tensor, scale, shift):
    return rms_norm(tensor) * (1.0 + scale[:, None, :]) + shift[:, None, :]


def mm(a, b):
    return jnp.dot(a, b, preferred_element_type=F32)


def mm_nt(a, b):
    return lax.dot_general(a, b, (((1,), (1,)), ((), ())), preferred_element_type=F32)


def mm_tn(a, b):
    return lax.dot_general(a, b, (((0,), (0,)), ((), ())), preferred_element_type=F32)


CHIP_ORDER = [(z, xh, y) for z in range(4) for xh in range(2) for y in range(4)]


def nat(ref):
    return jnp.concatenate([ref[z, y, xh] for z, xh, y in CHIP_ORDER], axis=0)


def store_nat(ref, value):
    for i, (z, xh, y) in enumerate(CHIP_ORDER):
        ref[z, y, xh] = value[32 * i : 32 * i + 32].astype(ref.dtype)


def norm_of(x):
    inv = lax.rsqrt(jnp.mean(x * x, axis=-1, keepdims=True) + EPSILON)
    return x * inv, inv


def norm_grad(unit, inv, dh_w):
    return (dh_w - unit * jnp.mean(dh_w * unit, axis=-1, keepdims=True)) * inv


def call(body, outs, ins, scratch=(), specs=None, out_specs=None, grid=None, prefetch=0):
    whole = pl.BlockSpec(memory_space=pltpu.VMEM)
    return pl.pallas_call(
        body,
        out_shape=outs,
        grid_spec=pltpu.PrefetchScalarGridSpec(
            num_scalar_prefetch=prefetch,
            grid=grid or (),
            in_specs=specs or [whole] * len(ins),
            out_specs=out_specs or [whole] * len(outs),
            scratch_shapes=list(scratch),
        ),
        compiler_params=pltpu.CompilerParams(vmem_limit_bytes=60 * 1024 * 1024),
    )(*ins)


def shape(dims, dtype):
    return jax.ShapeDtypeStruct(dims, dtype)


WHOLE = pl.BlockSpec(memory_space=pltpu.VMEM)
SMEM = pl.BlockSpec(memory_space=pltpu.SMEM)


def cols_spec(block, width=512):
    return pl.BlockSpec((4, 4, 2, 32, width), lambda i: (0, 0, 0, 0, block))


def fixed(dims):
    return pl.BlockSpec(dims, lambda i: (0,) * len(dims))


def qkv_body(tok, scale, shift, wq, wk, wv, n1_out, q_out, kv_out):
    for b in range(2):
        r = slice(128 * b, 128 * b + 128)
        unit, _ = norm_of(tok[r].astype(F32))
        n1_out[r] = (unit * (1.0 + scale[b : b + 1]) + shift[b : b + 1]).astype(BF)
    n1 = n1_out[...]
    q_out[...] = mm(n1, nat(wq)).astype(BF)
    kv_out[:, :512] = mm(n1, nat(wk)).astype(BF)
    kv_out[:, 512:] = mm(n1, nat(wv)).astype(BF)


def qkv_kernel(tok, scale, shift, full):
    return call(
        qkv_body,
        [shape((256, D), BF), shape((256, 512), BF), shape((256, D), BF)],
        (tok, scale, shift, full, full, full),
        specs=[fixed((256, D)), fixed((2, D)), fixed((2, D)), cols_spec(0), cols_spec(1), cols_spec(2)],
        out_specs=[fixed((256, D)), fixed((256, 512)), fixed((256, D))],
        grid=(1,),
    )


def head_cols(h):
    return slice(64 * h, 64 * h + 64)


def self_probs(q, k):
    scores = mm_nt(q, k) * HEAD_DIM ** (-0.5)
    e = jnp.exp(scores - jnp.max(scores, axis=-1, keepdims=True))
    return e * (1.0 / jnp.sum(e, axis=-1, keepdims=True))


def attend_body(q, kv, kv_far, proj_w, att_out, part_out):
    for b in range(2):
        r = slice(128 * b, 128 * b + 128)
        for h in range(8):
            k = jnp.concatenate((kv[r, head_cols(h)], kv_far[r, head_cols(h)]), axis=0)
            v = jnp.concatenate((kv[r, head_cols(8 + h)], kv_far[r, head_cols(8 + h)]), axis=0)
            p = self_probs(q[r, head_cols(h)], k).astype(BF)
            att_out[r, head_cols(h)] = mm(p, v).astype(BF)
    part_out[...] = mm(att_out[...], proj_w[...])


def attend_kernel(q, kv, kv_far, proj_w):
    return call(
        attend_body, [shape((256, 512), BF), shape((256, D), F32)], (q, kv, kv_far, proj_w)
    )


def spread_heads(rows8):
    tall = jnp.concatenate([rows8.astype(F32)] * 16, axis=0)
    row = lax.broadcasted_iota(jnp.int32, tall.shape, 0) // 8
    col = lax.broadcasted_iota(jnp.int32, tall.shape, 1) // 64
    return jnp.where(row == col, tall, 0.0).astype(BF)


def fold_heads(tall):
    row = lax.broadcasted_iota(jnp.int32, tall.shape, 0) // 8
    col = lax.broadcasted_iota(jnp.int32, tall.shape, 1) // 64
    kept = jnp.where(row == col, tall, 0.0)
    total = kept[0:8]
    for h in range(1, 8):
        total = total + kept[8 * h : 8 * h + 8]
    return total


def by_eights(op, x):
    lane = lax.broadcasted_iota(jnp.int32, x.shape, 1)
    for step in (1, 2, 4):
        up = pltpu.roll(x, x.shape[1] - step, 1)
        down = pltpu.roll(x, step, 1)
        x = op(x, jnp.where((lane & step) == 0, up, down))
    return x


def cross_probs(q, keys, length):
    scores = mm_nt(q, keys) * HEAD_DIM ** (-0.5)
    lane = lax.broadcasted_iota(jnp.int32, scores.shape, 1)
    scores = jnp.where((lane & 7) < length, scores, NEG_LARGE)
    e = jnp.exp(scores - by_eights(jnp.maximum, scores))
    return e * (1.0 / by_eights(jnp.add, e))


def cross_body(
    tok, part, part_far, gains, cq_w, text_kv, lens, co_w, res_out, n2_out, cq_out, att_out, part_out
):
    res_out[...] = tok[...].astype(F32) + (part[...] + part_far[...])
    unit, _ = norm_of(res_out[...])
    n2_out[...] = (unit * gains[0:1]).astype(BF)
    cq_out[...] = mm(n2_out[...], nat(cq_w)).astype(BF)
    for b in range(2):
        r = slice(128 * b, 128 * b + 128)
        keys = spread_heads(text_kv[b, :, 0:512])
        vals = spread_heads(text_kv[b, :, 512:1024])
        p = cross_probs(cq_out[r], keys, lens[b]).astype(BF)
        att_out[r] = mm(p, vals).astype(BF)
    part_out[...] = mm(att_out[...], co_w[...])


def cross_kernel(tok, part, part_far, gains, full, text_kv, lens, co_w):
    f = fixed
    return call(
        cross_body,
        [
            shape((256, D), F32),
            shape((256, D), BF),
            shape((256, 512), BF),
            shape((256, 512), BF),
            shape((256, D), F32),
        ],
        (tok, part, part_far, gains, full, text_kv, lens, co_w),
        specs=[
            f((256, D)),
            f((256, D)),
            f((256, D)),
            f((2, D)),
            cols_spec(3),
            f((2, 8, D)),
            SMEM,
            f((512, D)),
        ],
        out_specs=[f((256, D)), f((256, D)), f((256, 512)), f((256, 512)), f((256, D))],
        grid=(1,),
    )


GELU_A = 0.7978845608028654
GELU_B = 0.044715


def ff_copies(g_up, g_down, grad, sem, i):
    at = pl.ds(pl.multiple_of(i * 512, 512), 512)
    return (
        pltpu.make_async_copy(g_up.at[i], grad.at[:, :, :, :, at], sem.at[0, i]),
        pltpu.make_async_copy(g_down.at[i], grad.at[i, :, :, :, C_UP:], sem.at[1, i]),
    )


def ff_body(
    ids, res, part, part_far, gains, og, up, down, down_far, rest,
    res_out, grad_out, three_out, down_out, n3, n3_t, g_up, g_down, sem,
):
    i = pl.program_id(0)

    @pl.when(i == 0)
    def _():
        res_out[...] = res[...] + (part[...] + part_far[...])
        unit, _ = norm_of(res_out[...])
        low = (unit * gains[1:2]).astype(BF)
        n3[...] = low
        n3_t[...] = low.T

    up_w = nat(up)
    low_xh = ids[1] < 2
    own, far = down[0].reshape(256, C_X), down_far[0].reshape(256, C_X)
    left = jnp.concatenate((jnp.where(low_xh, own, far), jnp.where(low_xh, far, own)), axis=0)
    k = D - C_X
    right = jnp.concatenate(
        [
            rest[0, y, xh, :, k * h : k * h + k]
            for xh in range(2)
            for y in range(4)
            for h in range(2)
        ],
        axis=0,
    )
    down_w = jnp.concatenate((left, right), axis=1)
    pre = mm(n3[...], up_w)
    t = jnp.tanh(GELU_A * (pre + GELU_B * (pre * pre * pre)))
    act = (0.5 * pre * (1.0 + t)).astype(BF)
    slope = 0.5 * (1.0 + t) + 0.5 * pre * (1.0 - t * t) * (
        GELU_A * (1.0 + 3.0 * GELU_B * (pre * pre))
    )
    pre_grad = (mm_nt(og[...], down_w) * slope).astype(BF)
    up_wg = mm(n3_t[...], pre_grad).astype(BF)
    for j, (z, xh, y) in enumerate(CHIP_ORDER):
        g_up[i, z, y, xh] = up_wg[32 * j : 32 * j + 32]
    down_wg = mm_tn(act, og[...]).astype(BF)
    j = 0
    for xh in range(2):
        for y in range(4):
            for h in range(2):
                g_down[i, y, xh, :, D * h : D * h + D] = down_wg[32 * j : 32 * j + 32]
                j += 1
    for copy in ff_copies(g_up, g_down, grad_out, sem, i):
        copy.start()
    down_part = mm(act, down_w)
    three_part = mm_nt(pre_grad, up_w)

    @pl.when(i == 0)
    def _():
        down_out[...] = down_part
        three_out[...] = three_part

    @pl.when(i > 0)
    def _():
        down_out[...] += down_part
        three_out[...] += three_part

    @pl.when(i == 3)
    def _():
        for k in range(4):
            for copy in ff_copies(g_up, g_down, grad_out, sem, k):
                copy.wait()


def ff_kernel(ids, res, part, part_far, gains, og, down, down_far, full):
    f = fixed
    return call(
        ff_body,
        [
            shape((256, D), F32),
            shape((4, 4, 2, 32, C_UP + C_DOWN), BF),
            shape((256, D), F32),
            shape((256, D), F32),
        ],
        (ids, res, part, part_far, gains, og, full, down, down_far, full),
        scratch=[
            pltpu.VMEM((256, D), BF),
            pltpu.VMEM((D, 256), BF),
            pltpu.VMEM((4, 4, 4, 2, 32, 512), BF),
            pltpu.VMEM((4, 4, 2, 32, 2048), BF),
            pltpu.SemaphoreType.DMA((2, 4)),
        ],
        specs=[
            SMEM,
            f((256, D)),
            f((256, D)),
            f((256, D)),
            f((2, D)),
            f((256, D)),
            pl.BlockSpec((4, 4, 2, 32, 512), lambda i: (0, 0, 0, 0, i)),
            pl.BlockSpec((1, 4, 2, 32, C_X), lambda i: (i, 0, 0, 0, 0)),
            pl.BlockSpec((1, 4, 2, 32, C_X), lambda i: (i, 0, 0, 0, 0)),
            pl.BlockSpec((1, 4, 2, 32, 512), lambda i: (i, 0, 0, 0, 4)),
        ],
        out_specs=[f((256, D)), pl.BlockSpec(memory_space=pl.ANY), f((256, D)), f((256, D))],
        grid=(4,),
    )

def cross_back_body(
    part, part_far, res, og, gains, att, cq, n2, text_kv, lens, co_w, cq_w,
    grad_out, gain_out, co_out, cqw_out, text_out, two_out, ag, dq,
):
    unit, inv = norm_of(res[...])
    three = part[...] + part_far[...]
    gain_out[...] = jnp.sum(three * unit, axis=0, keepdims=True)
    grad_out[...] = og[...].astype(F32) + norm_grad(unit, inv, three * gains[1:2])
    low = grad_out[...].astype(BF)
    co_out[...] = mm_tn(att[...], low).astype(BF)
    ag[...] = mm_nt(low, co_w[...]).astype(BF)
    for b in range(2):
        r = slice(128 * b, 128 * b + 128)
        keys = spread_heads(text_kv[b, :, 0:512])
        vals = spread_heads(text_kv[b, :, 512:1024])
        p = cross_probs(cq[r], keys, lens[b])
        dp = mm_nt(ag[r], vals)
        ds = (p * (dp - by_eights(jnp.add, p * dp))).astype(BF)
        dq[r] = (mm(ds, keys) * HEAD_DIM ** (-0.5)).astype(BF)
        text_out[b, :, 0:512] = fold_heads(mm_tn(ds, cq[r])) * HEAD_DIM ** (-0.5)
        text_out[b, :, 512:1024] = fold_heads(mm_tn(p.astype(BF), ag[r]))
    store_nat(cqw_out, mm_tn(n2[...], dq[...]))
    two_out[...] = mm_nt(dq[...], nat(cq_w))


def cross_back_kernel(part, part_far, res, og, gains, att, cq, n2, text_kv, lens, co_w, full):
    f = fixed
    return call(
        cross_back_body,
        [
            shape((256, D), F32),
            shape((1, D), F32),
            shape((512, D), BF),
            shape((4, 4, 2, 32, 512), BF),
            shape((2, 8, D), F32),
            shape((256, D), F32),
        ],
        (part, part_far, res, og, gains, att, cq, n2, text_kv, lens, co_w, full),
        scratch=[pltpu.VMEM((256, 512), BF), pltpu.VMEM((256, 512), BF)],
        specs=[
            f((256, D)),
            f((256, D)),
            f((256, D)),
            f((256, D)),
            f((2, D)),
            f((256, 512)),
            f((256, 512)),
            f((256, D)),
            f((2, 8, D)),
            SMEM,
            f((512, D)),
            cols_spec(3),
        ],
        out_specs=[
            f((256, D)),
            f((1, D)),
            f((512, D)),
            f((4, 4, 2, 32, 512)),
            f((2, 8, D)),
            f((256, D)),
        ],
        grid=(1,),
    )


def pair_slices(i):
    rows = pl.ds(pl.multiple_of(i // 4 * 128, 128), 128)
    cols = pl.ds(pl.multiple_of(i % 4 * 128, 128), 128)
    vals = pl.ds(pl.multiple_of(i % 4 * 128 + 512, 128), 128)
    return rows, cols, vals


def self_back_body(
    part, part_far, res, res_grad, gains, att, q, kv, kv_far, proj_w,
    grad_out, gain_out, proj_out, dq_out, dkv_out, dfar_out, ag,
):
    unit, inv = norm_of(res[...])
    two = part[...] + part_far[...]
    gain_out[...] = jnp.sum(two * unit, axis=0, keepdims=True)
    grad_out[...] = res_grad[...] + norm_grad(unit, inv, two * gains[0:1])
    low = grad_out[...].astype(BF)
    proj_out[...] = mm_tn(att[...], low).astype(BF)
    ag[...] = mm_nt(low, proj_w[...]).astype(BF)
    factor = HEAD_DIM ** (-0.5)

    def step(i, carry):
        r, kc, vc = pair_slices(i)
        q2, g2 = q[r, kc], ag[r, kc]
        k2 = jnp.concatenate((kv[r, kc], kv_far[r, kc]), axis=0)
        v2 = jnp.concatenate((kv[r, vc], kv_far[r, vc]), axis=0)
        dq, dk, dv = [], [], []
        for h in (slice(0, 64), slice(64, 128)):
            k = k2[:, h]
            qh, gh = q2[:, h], g2[:, h]
            p = self_probs(qh, k)
            dp = mm_nt(gh, v2[:, h])
            ds = (p * (dp - jnp.sum(p * dp, axis=-1, keepdims=True))).astype(BF)
            dq.append(mm(ds, k))
            dk.append(mm_tn(ds, qh))
            dv.append(mm_tn(p.astype(BF), gh))
        dk = jnp.concatenate(dk, axis=1) * factor
        dv = jnp.concatenate(dv, axis=1)
        dq_out[r, kc] = (jnp.concatenate(dq, axis=1) * factor).astype(BF)
        dkv_out[r, kc] = dk[:128]
        dkv_out[r, vc] = dv[:128]
        dfar_out[r, kc] = dk[128:].astype(BF)
        dfar_out[r, vc] = dv[128:].astype(BF)
        return carry

    lax.fori_loop(0, 8, step, 0)


def self_back_kernel(part, part_far, res, res_grad, gains, att, q, kv, kv_far, proj_w):
    return call(
        self_back_body,
        [
            shape((256, D), F32),
            shape((1, D), F32),
            shape((512, D), BF),
            shape((256, 512), BF),
            shape((256, D), F32),
            shape((256, D), BF),
        ],
        (part, part_far, res, res_grad, gains, att, q, kv, kv_far, proj_w),
        scratch=[pltpu.VMEM((256, 512), BF)],
    )


def qkv_back_body(dq, dkv, dfar, n1, wq, wk, wv, wg_out, part_out):
    n = n1[...]
    dqv = dq[...]
    dkvv = (dkv[...] + dfar[...].astype(F32)).astype(BF)
    grads = (dqv, dkvv[:, :512], dkvv[:, 512:])
    total = None
    for i, (g, w) in enumerate(zip(grads, (wq, wk, wv))):
        wg = mm_tn(n, g).astype(BF)
        for j, (z, xh, y) in enumerate(CHIP_ORDER):
            wg_out[z, y, xh, :, 512 * i : 512 * i + 512] = wg[32 * j : 32 * j + 32]
        t = mm_nt(g, nat(w))
        total = t if total is None else total + t
    part_out[...] = total


def qkv_back_kernel(dq, dkv, dfar, n1, full):
    f = fixed
    return call(
        qkv_back_body,
        [shape((4, 4, 2, 32, 1536), BF), shape((256, D), F32)],
        (dq, dkv, dfar, n1, full, full, full),
        specs=[
            f((256, 512)),
            f((256, D)),
            f((256, D)),
            f((256, D)),
            cols_spec(0),
            cols_spec(1),
            cols_spec(2),
        ],
        out_specs=[f((4, 4, 2, 32, 1536)), f((256, D))],
        grid=(1,),
    )


def sum_body(*refs):
    total = refs[0][...].astype(F32)
    for r in refs[1:-1]:
        total = total + r[...].astype(F32)
    refs[-1][...] = total.astype(refs[-1].dtype)


def sum_kernel(*pieces):
    return call(sum_body, [shape(pieces[0].shape, BF)], pieces)[0]


LATE = C_QKV + C_TEXT + C_CQ + C_PROJ + C_CO
LATE_ROWS = LATE - C_PROJ - C_CO


def late_body(ids, text, qkv, cq, kept, came, out):
    out[:, :, :, :, :C_QKV] = qkv[...]
    at = C_QKV + C_TEXT
    out[:, :, :, :, C_QKV:at] = text[...]
    out[:, :, :, :, at : at + C_CQ] = cq[...]
    first = ids[0] == 0
    a, b = kept[...], came[...]
    out[:2, :, :, :, LATE_ROWS:] = jnp.where(first, a, b)
    out[2:, :, :, :, LATE_ROWS:] = jnp.where(first, b, a)


def late_kernel(ids, text, qkv, cq, kept, came):
    return call(
        late_body,
        [shape((4, 4, 2, 32, LATE), BF)],
        (ids, text, qkv, cq, kept, came),
        specs=[SMEM, *[WHOLE] * 5],
    )[0]


def late_sum_body(own, a, b, e, out):
    near = a[...].astype(F32) + b[...].astype(F32)
    row = lax.broadcasted_iota(jnp.int32, near.shape, 0) % 16
    col = lax.broadcasted_iota(jnp.int32, near.shape, 1)
    text = (col >= C_QKV) & (col < C_QKV + C_TEXT)
    near = jnp.where((row < 12) & text, 0.0, near)
    out[...] = (own[...].astype(F32) + e[...].astype(F32) + near).astype(BF)


def late_sum_kernel(own, a, b, e):
    return call(late_sum_body, [shape((32, LATE), BF)], (own, a, b, e))[0]


def rows_body(core, kept, came, proj_out, co_out):
    first = core[0] == 0
    i = 0
    for z in range(2):
        for xh in range(2):
            for y in range(4):
                a, b = kept[z, y, xh], came[z, y, xh]
                for bit in range(2):
                    t = jnp.where(first, a, b) if bit == 0 else jnp.where(first, b, a)
                    for out, c in ((proj_out, 0), (co_out, 512)):
                        out[16 * i : 16 * i + 16, :512] = t[:16, c : c + 512]
                        out[16 * i : 16 * i + 16, 512:] = t[16:, c : c + 512]
                    i += 1


def rows_kernel(core, kept, came):
    return call(
        rows_body,
        [shape((512, D), BF), shape((512, D), BF)],
        (core, kept, came),
        specs=[SMEM, WHOLE, WHOLE],
    )


def rows_back_body(core, proj_wg, co_wg, kept_out, sent_out):
    first = core[0] == 0
    i = 0
    for z in range(2):
        for xh in range(2):
            for y in range(4):
                t = []
                for bit in range(2):
                    r = slice(16 * i, 16 * i + 16)
                    t.append(
                        jnp.concatenate(
                            (
                                jnp.concatenate((proj_wg[r, :512], proj_wg[r, 512:]), axis=0),
                                jnp.concatenate((co_wg[r, :512], co_wg[r, 512:]), axis=0),
                            ),
                            axis=1,
                        )
                    )
                    i += 1
                kept_out[z, y, xh] = jnp.where(first, t[0], t[1])
                sent_out[z, y, xh] = jnp.where(first, t[1], t[0])


def rows_back_kernel(core, proj_wg, co_wg):
    dims = shape((2, 4, 2, 32, D), BF)
    return call(
        rows_back_body, [dims, dims], (core, proj_wg, co_wg), specs=[SMEM, WHOLE, WHOLE]
    )


def ff_unpack_body(ids, mine, came, down, up_out, down_out):
    first = ids[0] == 0
    a, b = mine[...].astype(F32), came[...].astype(F32)
    parts = (jnp.where(first, a, b), jnp.where(first, b, a))
    for i in range(32):
        for c in range(2):
            to = 128 * i + 64 * c
            up_out[:, to : to + 64] = parts[c][:, 64 * i : 64 * i + 64]
    down_out[:32] = down[:, :D].astype(F32)
    down_out[32:] = down[:, D:].astype(F32)


def ff_unpack_kernel(ids, mine, came, down):
    return call(
        ff_unpack_body,
        [shape((16, FF), F32), shape((64, D), F32)],
        (ids, mine, came, down),
        specs=[SMEM, WHOLE, WHOLE, WHOLE],
    )


def late_unpack_body(ids, mine, came, rows, qkv_out, cq_out, proj_out, co_out):
    first = ids[0] == 0
    a, b = mine[...].astype(F32), came[...].astype(F32)
    parts = (jnp.where(first, a, b), jnp.where(first, b, a))
    for c in range(2):
        to = slice(512 * c, 512 * c + 512)
        for i in range(3):
            qkv_out[i, :, to] = parts[c][:, 512 * i : 512 * i + 512]
        cq_out[:, to] = parts[c][:, LATE_ROWS - 512 : LATE_ROWS]
    for i, out in enumerate((proj_out, co_out)):
        for h in range(2):
            out[:, 512 * h : 512 * h + 512] = rows[
                16 * h : 16 * h + 16, 512 * i : 512 * i + 512
            ].astype(F32)


def late_unpack_kernel(ids, mine, came, rows):
    return call(
        late_unpack_body,
        [shape((3, 16, D), F32), shape((16, D), F32), shape((16, D), F32), shape((16, D), F32)],
        (ids, mine, came, rows),
        specs=[SMEM, WHOLE, WHOLE, WHOLE],
    )


def swap_core(value):
    return lax.ppermute(value, "core", [(0, 1), (1, 0)])


def swap_seq(value):
    return lax.ppermute(value, "xl", [(0, 1), (1, 0)])


def swap_x(value, pairs):
    return lax.ppermute(value, RING_X, [p for a, b in pairs for p in ((a, b), (b, a))])


def in_order(index, mine, other, axis):
    first = jnp.where(index == 0, mine, other)
    second = jnp.where(index == 0, other, mine)
    return jnp.stack((first, second), axis=axis)


def join(index, mine, other, axis):
    first = jnp.where(index == 0, mine, other)
    second = jnp.where(index == 0, other, mine)
    return jnp.concatenate((first, second), axis=axis)


def pick(value, index, axis):
    return jnp.where(
        index == 0, lax.index_in_dim(value, 0, axis, False), lax.index_in_dim(value, 1, axis, False)
    )


def gather_chips(pair):
    full = lax.all_gather(pair, ("z", "y"), axis=0, tiled=False)
    return full.reshape(4, 4, *pair.shape)


def ring(value, axis, size, step):
    return lax.ppermute(value, axis, [(i, (i + step) % size) for i in range(size)])


def exchange(value, axes):
    return lax.all_to_all(value, axes, 0, 0, tiled=True)


def zy_scatter(full):
    cols = full.shape[-1]
    part = lax.psum_scatter(full.reshape(D, cols), ("z", "y"), scatter_dimension=0, tiled=True)
    return part.reshape(2, 32, cols)


def halves_as_rows(value):
    k = value.shape[-1] // 2
    return jnp.concatenate((value[:, :k], value[:, k:]), axis=0)


def per_device(
    tokens_in,
    noise_emb,
    text_emb,
    prompt_len,
    mod_weight,
    qkv_weight,
    proj_weight,
    cq_weight,
    text_weight,
    co_weight,
    norm_gains,
    up_weight,
    down_weight,
    out_grad,
):
    core = lax.axis_index("core")
    xh = lax.axis_index("xh")
    xl = lax.axis_index("xl")
    rows = tokens_in.shape[1]

    misc = jnp.concatenate(
        (
            jnp.pad(text_emb[0], ((0, 0), (0, D - TEXT_W))),
            jnp.broadcast_to(prompt_len.astype(BF)[:, None], (8, D)),
        ),
        axis=0,
    )
    mine = jnp.concatenate((tokens_in[0], out_grad[0], misc), axis=0)
    both = in_order(core, mine, swap_core(mine), 0)
    tok = both[:, :rows].reshape(256, D)
    og = both[:, rows : 2 * rows].reshape(256, D)
    text = both[:, 2 * rows : 2 * rows + 8, :TEXT_W]
    lens = both[:, 2 * rows + 8, 0].astype(jnp.int32)

    def side(which):
        qkv = pick(qkv_weight.reshape(16, 3, 2, 512), which, 2).reshape(16, C_QKV)
        cq = pick(cq_weight.reshape(16, 2, 512), which, 1)
        txt = pick(text_weight.reshape(12, 2, 2, 256), which, 2).reshape(12, C_TEXT)
        gains = jnp.pad(norm_gains, ((0, 2), (0, C_TEXT - 16)))
        return jnp.concatenate((qkv, cq, jnp.concatenate((txt, gains), axis=0)), axis=1)

    shared = join(core, side(core), swap_core(side(1 - core)), 0)
    first = jnp.concatenate(
        (
            shared[:, : C_QKV + C_CQ + C_TEXT],
            halves_as_rows(proj_weight),
            halves_as_rows(co_weight),
        ),
        axis=1,
    )
    near, xl_pair, across = ((0, 3), (1, 2)), ((0, 1), (2, 3)), ((0, 2), (1, 3))
    lo, hi = TEXT_COLS
    first_far = swap_x(first, ((0, 3), (1, 2)))
    text_far = swap_x(first[:, lo:hi], ((0, 2), (1, 3)))
    first_far, up_late = lax.optimization_barrier((first_far, up_weight))

    def up_side(which):
        return pick(up_late.reshape(16, 32, 2, 64), which, 2).reshape(16, C_UP)

    second = jnp.concatenate(
        (
            join(core, up_side(core), swap_core(up_side(1 - core)), 0),
            down_weight[:32, C_X:],
            down_weight[32:, C_X:],
        ),
        axis=1,
    )
    first_far = jnp.concatenate((first_far[:, :lo], text_far, first_far[:, hi:]), axis=1)
    down_halves = down_weight.reshape(2, 32, D)
    first_pair = jnp.concatenate(
        (in_order(xh, first, first_far, 0), down_halves[..., :C_X]), axis=2
    )
    full_one = gather_chips(first_pair)
    full_two = gather_chips(in_order(xh, second, swap_x(second, near), 0))
    full_one, down_own = lax.optimization_barrier((full_one, full_one[..., -C_X:]))
    down_far = swap_x(down_own, near)

    text_rows = full_one[..., lo:hi].transpose(0, 2, 1, 3, 4)
    text_rows = text_rows.reshape(64, 16, C_TEXT)
    text_w = text_rows[:, :12].reshape(TEXT_W, 2, 256)
    gains = text_rows[:, 12:14, :16].transpose(1, 0, 2).reshape(2, D).astype(F32)
    core_id = core.astype(jnp.int32)[None]
    y_id = lax.axis_index("y")
    ids = jnp.stack([core, 2 * xh + xl, y_id, xl]).astype(jnp.int32)

    noise_cols = exchange(noise_emb.reshape(64, 16), FSDP)
    half = pick(mod_weight.reshape(16, 2, D), xl, 1)
    mod_parts = jnp.dot(noise_cols, half, preferred_element_type=F32)
    mod_part = jnp.sum(exchange(mod_parts, FSDP), axis=0, keepdims=True)
    mod_own = join(xl, mod_part, swap_seq(mod_part), 1)
    mod_all = in_order(core, mod_own, swap_core(mod_own), 0).reshape(2, 2, D)
    mod_scale, mod_shift = mod_all[:, 0], mod_all[:, 1]
    normed_one, queries, kv_own = qkv_kernel(tok, mod_scale, mod_shift, full_one)
    kv_far = swap_seq(kv_own)
    later, kv_own = lax.optimization_barrier((full_one, kv_own))
    halves = later[..., hi : hi + 2 * 512].reshape(2, 2, 4, 2, 32, D)
    kept = pick(halves, core, 0)
    proj_w, co_w = rows_kernel(core_id, kept, swap_core(pick(halves, 1 - core, 0)))
    attended, proj_part = attend_kernel(queries, kv_own, kv_far, proj_w)
    proj_part, down_far = lax.optimization_barrier((proj_part, down_far))
    text_own = jnp.einsum("ijt,tcn->ijcn", text, text_w, preferred_element_type=F32).astype(BF)
    text_xl = in_order(xl, text_own, swap_seq(text_own), 0)
    text_kv = join(core, pick(text_xl, core, 0), swap_core(pick(text_xl, 1 - core, 0)), 3)
    text_kv = text_kv.reshape(2, TXT, D)
    after_self, normed_two, cross_q, cross_att, co_part = cross_kernel(
        tok, proj_part, swap_core(proj_part), gains, full_one, text_kv, lens, co_w
    )
    after_cross, ff_wg, three_part, down_part = ff_kernel(
        ids, after_self, co_part, swap_core(co_part), gains, og, down_own, down_far, full_two
    )
    ff_sc = zy_scatter(ff_wg)
    down_part = down_part.reshape(2, rows, D)
    down_own = pick(down_part, core, 0) + swap_core(pick(down_part, 1 - core, 0))
    block_out = (pick(after_cross.reshape(2, rows, D), core, 0) + down_own).astype(BF)[None]

    cross_res_grad, gain_three_grad, co_wg, cq_wg, text_sum, two_part = cross_back_kernel(
        three_part, swap_core(three_part), after_cross, og, gains, cross_att, cross_q,
        normed_two, text_kv, lens, co_w, full_one,
    )
    self_res_grad, gain_two_grad, proj_wg, dq, dkv, dkv_far = self_back_kernel(
        two_part, swap_core(two_part), after_self, cross_res_grad, gains, attended, queries,
        kv_own, kv_far, proj_w,
    )
    rows_kept, rows_sent = rows_back_kernel(core_id, proj_wg, co_wg)
    dkv_came = swap_seq(dkv_far)
    rows_came = swap_core(rows_sent)
    qkv_wg, one_part = qkv_back_kernel(dq, dkv, dkv_came, normed_one, full_one)

    text_sum = (text_sum + swap_seq(text_sum.astype(BF)).astype(F32)).astype(BF)
    text_quarters = text_sum.reshape(2, TXT, 2, 2, 256)
    text_kept = pick(text_quarters, core, 3)
    text_came = swap_core(pick(text_quarters, 1 - core, 3))
    text_kv_grad = jnp.where(core == xl, text_kept, text_came)
    text_wg = jnp.einsum("ijt,ijcn->tcn", text, text_kv_grad, preferred_element_type=F32)
    text_part = jnp.einsum("ijcn,tcn->ijt", text_kv_grad, text_w, preferred_element_type=F32)

    one_part = one_part.reshape(2, rows, D)
    one_grad = pick(one_part, core, 0) + swap_core(pick(one_part, 1 - core, 0))
    own_tokens = tokens_in.astype(F32)
    _, mod_back = jax.vjp(
        modulated_norm, own_tokens, pick(mod_scale, core, 0)[None], pick(mod_shift, core, 0)[None]
    )
    input_part, scale_grad, shift_grad = mod_back(one_grad[None])
    tokens_grad = pick(self_res_grad.reshape(2, rows, D), core, 0)[None] + input_part
    mod_grad = jnp.concatenate((scale_grad, shift_grad), axis=1)
    mod_grad = (mod_grad + swap_seq(mod_grad)).astype(BF)
    mod_grads = exchange(jnp.broadcast_to(mod_grad, (64, 2 * D)), FSDP)
    mod_wgrad = jnp.einsum("if,ic->fc", noise_cols, mod_grads, preferred_element_type=F32)
    noise_parts = jnp.einsum("ic,fc->if", mod_grads, mod_weight, preferred_element_type=F32)
    noise_grad = exchange(noise_parts, FSDP).reshape(1, D)

    gains_wg = jnp.concatenate((gain_two_grad, gain_three_grad), axis=0).astype(BF)
    gains_wg = jnp.pad(
        gains_wg.reshape(2, 64, 16).transpose(1, 0, 2), ((0, 0), (0, 2), (0, C_TEXT - 16))
    )
    text_pack = jnp.concatenate((text_wg.astype(BF).reshape(64, 12, C_TEXT), gains_wg), axis=1)
    text_pack = text_pack.reshape(4, 2, 4, 32, C_TEXT).transpose(0, 2, 1, 3, 4)
    late_wg = late_kernel(ids, text_pack, qkv_wg, cq_wg, rows_kept, rows_came)
    late_wg, ff_sc = lax.optimization_barrier((late_wg, ff_sc))
    late_sc = zy_scatter(late_wg)

    own, far = pick(ff_sc, xh, 0), pick(ff_sc, 1 - xh, 0)
    ff_g = sum_kernel(own, swap_x(own, xl_pair), swap_x(far, near), swap_x(far, across))
    up_rows = ff_g[:, :C_UP].reshape(2, 16, C_UP)
    up_wgrad, down_wgrad = ff_unpack_kernel(
        ids, pick(up_rows, core, 0), swap_core(pick(up_rows, 1 - core, 0)), ff_g[:, C_UP:]
    )

    own, far = pick(late_sc, xh, 0), pick(late_sc, 1 - xh, 0)
    late_g = late_sum_kernel(own, swap_x(own, xl_pair), swap_x(far, near), swap_x(far, across))
    late_rows = late_g[:, :LATE_ROWS].reshape(2, 16, LATE_ROWS)
    kept_rows = pick(late_rows, core, 0)
    came_rows = swap_core(pick(late_rows, 1 - core, 0))
    qkv_wgrad, cq_wgrad, proj_wgrad, co_wgrad = late_unpack_kernel(
        ids, kept_rows, came_rows, late_g[:, LATE_ROWS:]
    )
    qkv_wgrad = qkv_wgrad.transpose(1, 0, 2)
    lo, hi = C_QKV, C_QKV + C_TEXT
    text_both = in_order(core, kept_rows[:, lo:hi], came_rows[:, lo:hi], 0).astype(F32)
    text_wgrad = text_both[:, :12].reshape(2, 12, 2, 256).transpose(1, 2, 0, 3).reshape(12, 2, 512)
    gains_grad = kept_rows[12:14, lo : lo + 16].astype(F32)

    text_grad = pick(text_part, core, 0) + swap_core(pick(text_part, 1 - core, 0))
    text_grad = text_grad + swap_seq(text_grad)
    return (
        block_out,
        tokens_grad,
        noise_grad,
        text_grad[None],
        mod_wgrad,
        qkv_wgrad,
        proj_wgrad,
        cq_wgrad,
        text_wgrad,
        co_wgrad,
        gains_grad,
        up_wgrad,
        down_wgrad,
    )


def solution(mesh):
    split = Mesh(mesh.devices.reshape(SIZES), AXES)
    in_specs = (
        P(FSDP, "xl", None),
        P(FSDP, None),
        P(FSDP, None, None),
        P(FSDP),
        P(FSDP, None),
        P(FSDP, None, None),
        P(FSDP, None),
        P(FSDP, None),
        P(FSDP, None, "xl"),
        P(FSDP, None),
        P(None, FSDP),
        P(FSDP, None),
        P(FSDP, None),
        P(FSDP, "xl", None),
    )
    out_specs = (
        P(FSDP, "xl", None),
        P(FSDP, "xl", None),
        P(FSDP, None),
        P(FSDP, None, None),
        P(FSDP, None),
        P(FSDP, None, None),
        P(FSDP, None),
        P(FSDP, None),
        P(FSDP, None, "xl"),
        P(FSDP, None),
        P(None, FSDP),
        P(FSDP, None),
        P(FSDP, None),
    )
    return jax.shard_map(
        per_device, mesh=split, in_specs=in_specs, out_specs=out_specs, check_vma=False
    )
```
